32 devices in a mesh: group: 2 (over y), tile: 4 (over z), dp: 2 (over x), chan: 2 (over core).
Axes of the slice: x: 2, y: 2, z: 4, core: 2. Of those that a mesh axis runs over, the one named last changes fastest.
Arguments:
- inputs: bfloat16 [4, 4, 32, 32, 128], P(('group', 'dp'), 'tile'), parts along dimension 0, may hold values from -6 to 6
- kernel: float32 [49, 128], replicated, may hold values from -0.875 to 0.875
- norm_gain: float32 [128], replicated, may hold values from 0.1 to 1.9
- w_in: bfloat16 [128, 512], P(None, 'chan'), may hold values from -0.5 to 0.5
- w_out: bfloat16 [512, 128], P('chan'), may hold values from -0.25 to 0.25
- layer_scale: float32 [128], replicated, may hold values from 0.25 to 2
- cotangent: bfloat16 [4, 4, 32, 32, 128], P(('group', 'dp'), 'tile'), parts along dimension 0, may hold values from -6 to 6
- adjacency: int32 [4, 8, 2], replicated, may hold values from 0 to 3, as said below
Outputs:
- inputs_grad: bfloat16 [4, 4, 32, 32, 128], P(('group', 'dp'), 'tile'), parts along dimension 0
- kernel_grad: float32 [98, 128], P('group'), parts along dimension 0
- gain_grad: float32 [256], P('group'), parts along dimension 0
- w_in_grad: float32 [256, 512], P(('group', 'dp'), 'chan'), parts along dimension 0
- w_out_grad: float32 [1024, 128], P(('group', 'chan'), 'dp'), parts along dimension 0
- scale_grad: float32 [256], P('group'), parts along dimension 0
The draws below stay inside these ranges and needn't reach their ends.
There are 2 independent parts, one for each index of `group`. The reference program is written for one: setup_inputs(seed, part) draws one part's arguments, and reference() takes and returns one part's arrays. A program takes and returns all parts, laid end to end along the dimension named above; an argument that names none is the same for every part. Nothing has to cross between parts.
Inputs may be any that keep to these rules, and one draw needn't show every extreme that they name: adjacency[t, k, 0] is the tile beside tile t in direction k of t's own frame and adjacency[t, k, 1] the quarter turns relating the two frames, as in the reference program. The tiles form a closed band of two rows of 2 tiles, a stand-in for a sphere's tiling with rotated neighbours, with consistent neighbours; every tile is some tile's neighbour.
All inputs are finite; a program needn't handle non-finite values.
Results may differ from the reference program's by a relative error of at most 0.0063.
Values may be sent and summed in bfloat16 or wider, within the bound.
A program may use at most 64 MiB of HBM per device.

```python
import math
import jax
import jax.numpy as jnp
from jax import lax

C = 128
HID = 512
KS = 7
TS = 32
TILES = 4
BATCH = 2


def draw_adjacency(key, part):
    columns = TILES // 2
    placing = jax.random.permutation(jax.random.fold_in(key, 11), TILES).astype(jnp.int32)
    quarter_turns = jax.random.randint(jax.random.fold_in(key, 23), (TILES,), 0, 4, dtype=jnp.int32)
    tile_ids = jnp.arange(TILES, dtype=jnp.int32)
    at_cell = jnp.zeros((TILES,), jnp.int32).at[placing].set(tile_ids)
    grid_row = placing // columns
    grid_col = placing % columns
    step_rows = jnp.array([-1, 0, 1, 0, -1, 1, 1, -1], jnp.int32)
    step_cols = jnp.array([0, 1, 0, -1, 1, 1, -1, -1], jnp.int32)
    slot_ids = jnp.arange(8, dtype=jnp.int32)
    edge_dirs = (slot_ids[None, :] + quarter_turns[:, None]) % 4
    corner_dirs = 4 + (slot_ids[None, :] - 4 + quarter_turns[:, None]) % 4
    direction = jnp.where(slot_ids[None, :] < 4, edge_dirs, corner_dirs)
    neighbour_row = (grid_row[:, None] + step_rows[direction]) % 2
    neighbour_col = (grid_col[:, None] + step_cols[direction]) % columns
    neighbour = at_cell[neighbour_row * columns + neighbour_col]
    relative = (quarter_turns[:, None] - quarter_turns[neighbour]) % 4
    return jnp.stack([neighbour, relative], axis=-1).astype(jnp.int32)


def strengthened(drawn, key, source, target, blocks, factor):
    owner, partner = [(jnp.arange(drawn.shape[dim]) // (drawn.shape[dim] // blocks)).reshape([-1 if axis == dim else 1 for axis in range(drawn.ndim)]) for dim in (source, target)]
    chosen = jax.random.permutation(key, blocks)[partner]
    strong = (owner == chosen) | (owner == (partner + blocks // 2) % blocks)
    return jnp.where(strong, factor * drawn, drawn)


def block_levels(key, extent, shards, smallest, largest):
    gain = 1.0
    for dim, shards_of in shards:
        heights = jax.random.uniform(jax.random.fold_in(jax.random.fold_in(key, 6), dim), (shards_of,), jnp.float32, smallest / len(shards), largest / len(shards))
        gain = gain * jnp.repeat(jnp.exp(heights), extent[dim] // shards_of).reshape((-1,) + (1,) * (len(extent) - 1 - dim))
    return gain


def scatter_about(stream_key, shape, scale, bound, cuts=(), kind=jnp.bfloat16):
    result = jax.random.normal(stream_key, shape, jnp.float32) * scale
    if len(cuts) > 0:
        result = block_levels(stream_key, shape, cuts, -0.22, 0.18) * result
    return jnp.clip(result, min=-bound, max=bound).astype(kind)


def bell_draw_with(rng, shape, spread, reach, cuts, heavy, kind=jnp.bfloat16):
    entries = spread * jax.random.normal(rng, shape, jnp.float32)
    if cuts:
        entries = entries * block_levels(rng, shape, cuts, -0.22, 0.18)
    return jnp.clip(strengthened(entries, jax.random.fold_in(rng, 3), *heavy), -reach, reach).astype(kind)


def setup_inputs(seed: int = 0, part: int = 0) -> dict:
    key_list = jax.random.split(jax.random.key(seed), 9)
    own_keys = jax.random.split(jax.random.fold_in(key_list[8], part), 9)
    return {
        "inputs": scatter_about(own_keys[0], (BATCH, TILES, TS, TS, C), 1.0, 6.0, ((0, 2), (1, 4))),
        "kernel": scatter_about(key_list[1], (KS * KS, C), (KS * KS) ** -0.5, 0.875, (), jnp.float32),
        "norm_gain": jnp.clip(1.0 + 0.18 * jax.random.normal(key_list[2], (C,), jnp.float32), 0.1, 1.9),
        "w_in": scatter_about(key_list[3], (C, HID), C ** -0.5, 0.5, ((1, 2),)),
        "w_out": scatter_about(key_list[4], (HID, C), HID ** -0.5, 0.25, ((0, 2),)),
        "layer_scale": jnp.clip(jnp.exp(jax.random.uniform(key_list[5], (C,), jnp.float32, math.log(0.25), math.log(2.0))), 0.25, 2.0),
        "cotangent": bell_draw_with(own_keys[6], (BATCH, TILES, TS, TS, C), 1.0, 6.0, ((0, 2), (1, 4)), (0, 4, 2, 2.0)),
        "adjacency": draw_adjacency(jax.random.fold_in(key_list[8], 71), part),
    }


eps = 1e-06
root_two_pi = 0.7978845608028654
cubic_coef = 0.044715

def gelu_pair(values):
    inner = root_two_pi * (values + cubic_coef * values * values * values)
    tanh_part = jnp.tanh(inner)
    active = 0.5 * values * (1.0 + tanh_part)
    gelu_slope = 0.5 * (1.0 + tanh_part) + 0.5 * values * (1.0 - tanh_part * tanh_part) * root_two_pi * (1.0 + 3.0 * cubic_coef * values * values)
    return (active, gelu_slope)

def norm_forward(conv_flat, norm_gain):
    row_mean = lax.optimization_barrier(jnp.mean(conv_flat, axis=1, keepdims=True))
    centred = conv_flat - row_mean
    inv_std = lax.rsqrt(lax.optimization_barrier(jnp.mean(centred * centred, axis=1, keepdims=True)) + eps)
    normed = centred * inv_std
    return (normed, inv_std, (normed * norm_gain).astype(jnp.bfloat16))

def norm_backward(normed_grad, normed, inv_std, norm_gain):
    scaled = normed_grad * norm_gain
    first_mean = lax.optimization_barrier(jnp.mean(scaled, axis=1, keepdims=True))
    second_mean = lax.optimization_barrier(jnp.mean(scaled * normed, axis=1, keepdims=True))
    return (inv_std * (scaled - first_mean - normed * second_mean)).astype(jnp.bfloat16)

def pointwise(conv_flat, upstream_flat, norm_gain, w_in, w_out, layer_scale):
    normed, inv_std, normed_b = norm_forward(conv_flat, norm_gain)
    hidden = jnp.dot(normed_b, w_in, preferred_element_type=jnp.float32)
    active, gelu_slope = gelu_pair(hidden)
    active_b = active.astype(jnp.bfloat16)
    branch = jnp.dot(active_b, w_out, preferred_element_type=jnp.float32)
    scale_part = lax.optimization_barrier(jnp.sum(upstream_flat * branch, axis=0))
    scaled_b = (upstream_flat * layer_scale).astype(jnp.bfloat16)
    w_out_part = jnp.dot(active_b.T, scaled_b, preferred_element_type=jnp.float32)
    hidden_grad = (jnp.dot(scaled_b, w_out.T, preferred_element_type=jnp.float32) * gelu_slope).astype(jnp.bfloat16)
    w_in_part = jnp.dot(normed_b.T, hidden_grad, preferred_element_type=jnp.float32)
    normed_grad = jnp.dot(hidden_grad, w_in.T, preferred_element_type=jnp.float32)
    gain_part = lax.optimization_barrier(jnp.sum(normed_grad * normed, axis=0))
    conv_grad = norm_backward(normed_grad, normed, inv_std, norm_gain)
    return (conv_grad, w_in_part, w_out_part, gain_part, scale_part)

def depthwise(padded, kernel, first_row, row_count):
    rim_width = KS // 2
    rows = lax.dynamic_slice_in_dim(padded, first_row, row_count + 2 * rim_width, 1)
    tile_side = padded.shape[2] - 2 * rim_width
    summed = jnp.zeros((rows.shape[0], row_count, tile_side, rows.shape[3]), jnp.float32)
    for shift_row in range(KS):
        for shift_col in range(KS):
            summed = summed + rows[:, shift_row:shift_row + row_count, shift_col:shift_col + tile_side].astype(jnp.float32) * kernel[shift_row * KS + shift_col]
    return summed

def kernel_terms(rows, conv_grad):
    row_count, tile_side = (conv_grad.shape[1], conv_grad.shape[2])
    grad_f = conv_grad.astype(jnp.float32)
    terms = []
    for shift_row in range(KS):
        for shift_col in range(KS):
            window = rows[:, shift_row:shift_row + row_count, shift_col:shift_col + tile_side].astype(jnp.float32)
            terms.append(lax.optimization_barrier(jnp.sum(window * grad_f, axis=(0, 1, 2))))
    return jnp.stack(terms, axis=0)

def turned(image, quarter):
    options = [lambda values, count=count: jnp.rot90(values, count, axes=(1, 2)) for count in range(4)]
    return lax.switch(quarter, options, image)

def rim_regions(rim_width):
    near = slice(0, rim_width)
    far = slice(-rim_width, None)
    inner = slice(rim_width, -rim_width)
    whole = slice(None)
    return ((near, inner, far, whole), (inner, far, whole, near), (far, inner, near, whole), (inner, near, whole, far), (near, far, far, near), (far, far, near, near), (far, near, near, far), (near, near, far, far))

def padded_tile(inputs, adjacency, tile_id):
    rim_width = KS // 2
    pieces = []
    for slot_index in range(8):
        source = adjacency[tile_id, slot_index, 0]
        image = lax.dynamic_index_in_dim(inputs, source, 1, keepdims=False)
        pieces.append(turned(image, adjacency[tile_id, slot_index, 1]))
    north, east, south, west, north_east, south_east, south_west, north_west = pieces
    centre = lax.dynamic_index_in_dim(inputs, tile_id, 1, keepdims=False)
    top_rows = jnp.concatenate([north_west[:, -rim_width:, -rim_width:], north[:, -rim_width:, :], north_east[:, -rim_width:, :rim_width]], axis=2)
    middle_rows = jnp.concatenate([west[:, :, -rim_width:], centre, east[:, :, :rim_width]], axis=2)
    bottom_rows = jnp.concatenate([south_west[:, :rim_width, -rim_width:], south[:, :rim_width, :], south_east[:, :rim_width, :rim_width]], axis=2)
    return jnp.concatenate([top_rows, middle_rows, bottom_rows], axis=1)

def reference(inputs, kernel, norm_gain, w_in, w_out, layer_scale, cotangent, adjacency):
    rim_width = KS // 2
    channels = inputs.shape[4]

    def one_tile(tile_id):
        padded = padded_tile(inputs, adjacency, tile_id)
        upstream = lax.dynamic_index_in_dim(cotangent, tile_id, 1, keepdims=False)
        samples = upstream.shape[0]
        conv = depthwise(padded, kernel, 0, TS)
        conv_grad, w_in_part, w_out_part, gain_part, scale_part = pointwise(conv.reshape(-1, channels), upstream.reshape(-1, channels).astype(jnp.float32), norm_gain, w_in, w_out, layer_scale)
        conv_grad = conv_grad.reshape(samples, TS, TS, channels)
        kernel_part = kernel_terms(padded, conv_grad)
        pad_grad = jnp.zeros(padded.shape, jnp.float32)
        grad_f = conv_grad.astype(jnp.float32)
        for shift_row in range(KS):
            for shift_col in range(KS):
                pad_grad = pad_grad.at[:, shift_row:shift_row + TS, shift_col:shift_col + TS].add(kernel[shift_row * KS + shift_col] * grad_f)
        return (pad_grad, kernel_part, gain_part, w_in_part, w_out_part, scale_part)
    pad_grads, kernel_parts, gain_parts, w_in_parts, w_out_parts, scale_parts = lax.map(one_tile, jnp.arange(TILES, dtype=jnp.int32))
    regions = rim_regions(rim_width)
    summed = cotangent.astype(jnp.float32) + jnp.moveaxis(pad_grads[:, :, rim_width:-rim_width, rim_width:-rim_width], 0, 1)

    def route(tile_id, summed):
        slot_grads = lax.dynamic_index_in_dim(pad_grads, tile_id, 0, keepdims=False)
        for slot_index in range(8):
            pad_rows, pad_cols, image_rows, image_cols = regions[slot_index]
            placed = jnp.zeros((BATCH, TS, TS, channels), jnp.float32).at[:, image_rows, image_cols].set(slot_grads[:, pad_rows, pad_cols])
            back = turned(placed, (4 - adjacency[tile_id, slot_index, 1]) % 4)
            target = adjacency[tile_id, slot_index, 0]
            current = lax.dynamic_index_in_dim(summed, target, 1, keepdims=False)
            summed = lax.dynamic_update_index_in_dim(summed, current + back, target, 1)
        return summed
    summed = lax.fori_loop(0, TILES, route, summed)
    factor = 1.0 / math.sqrt(BATCH * TILES * TS * TS)
    return (summed.astype(jnp.bfloat16), lax.optimization_barrier(jnp.sum(kernel_parts, axis=0)) * factor, lax.optimization_barrier(jnp.sum(gain_parts, axis=0)) * factor, lax.optimization_barrier(jnp.sum(w_in_parts, axis=0)) * factor, lax.optimization_barrier(jnp.sum(w_out_parts, axis=0)) * factor, lax.optimization_barrier(jnp.sum(scale_parts, axis=0)) * factor)
```

```python
import functools
import math

import jax
import jax.numpy as jnp
from jax import lax
from jax.experimental import pallas as pl
from jax.experimental.pallas import tpu as pltpu
from jax.sharding import PartitionSpec as P

KS = 7
H = KS // 2
COL = 8
ROWS_AT_ONCE = 4
SMALL_ROWS = 64

eps = 1e-06
root_two_pi = 0.7978845608028654
cubic_coef = 0.044715
facing_turns = (2, 3, 0, 1, 2, 0, 0, 2)
corner_at_end = (True, False, True, False)
MESH = pl.DeviceIdType.MESH
F32 = jnp.float32
BF16 = jnp.bfloat16


def gelu_pair(values):
    square = values * values
    tanh_part = jnp.tanh(values * (root_two_pi + (root_two_pi * cubic_coef) * square))
    half_up = 0.5 + 0.5 * tanh_part
    active = values * half_up
    gelu_slope = half_up + active * (1.0 - tanh_part) * (
        root_two_pi + (3.0 * root_two_pi * cubic_coef) * square
    )
    return active, gelu_slope


def mm(left, right, left_dim, right_dim):
    return lax.dot_general(
        left, right, (((left_dim,), (right_dim,)), ((), ())), preferred_element_type=F32
    )


def body(
    tiles, dps, factor,
    adj_hbm, x_hbm, ct_hbm, kern_hbm, gain_hbm, w_in_ref, w_out_ref, scale_hbm,
    out_ref, small_out, w_out_all,
    adj, kern, gain_ref, scale_ref, pad, strips, faces, win, wout, conv_ref, part, cg, cpad, gpad, rimf, rims, incoming,
    chan_recv, dp_send, dp_recv, piece_send, piece_recv, piece_all, kacc, small_part, small_recv,
    small_dp, small_tile, small_done, base, x_ref, ct_ref, local_sem,
    face_send, face_recv, pair_send, pair_recv, rim_send, rim_recv,
    dp_send_sem, dp_recv_sem, rs_send, rs_recv, tg_send, tg_recv, sd_send, sd_recv, st_send, st_recv,
):
    ts = x_ref.shape[0]
    half = ts // 2
    strip = H * ts
    me_t = lax.axis_index("tile")
    me_d = lax.axis_index("dp")
    me_c = lax.axis_index("chan")
    sib = 1 - me_c

    barrier = pltpu.get_barrier_semaphore()
    for o in range(1, tiles):
        pl.semaphore_signal(barrier, inc=1, device_id={"tile": lax.rem(me_t + o, tiles)}, device_id_type=MESH)
    for o in range(1, dps):
        pl.semaphore_signal(barrier, inc=1, device_id={"dp": lax.rem(me_d + o, dps)}, device_id_type=MESH)
    pl.semaphore_signal(barrier, inc=1, device_id={"chan": sib}, device_id_type=MESH)

    x_copy = pltpu.make_async_copy(x_hbm, x_ref, local_sem.at[0])
    x_copy.start()
    win_local = pltpu.make_async_copy(w_in_ref, win.at[me_c], local_sem.at[1])
    win_local.start()
    wout_local = pltpu.make_async_copy(w_out_ref, wout.at[me_c], local_sem.at[2])
    wout_local.start()
    ct_copy = pltpu.make_async_copy(ct_hbm, ct_ref, local_sem.at[3])
    ct_copy.start()
    adj_copy = pltpu.make_async_copy(adj_hbm, adj, local_sem.at[4])
    adj_copy.start()
    kern_copy = pltpu.make_async_copy(kern_hbm, kern, local_sem.at[5])
    kern_copy.start()
    gain_copy = pltpu.make_async_copy(gain_hbm, gain_ref, local_sem.at[6])
    gain_copy.start()
    scale_copy = pltpu.make_async_copy(scale_hbm, scale_ref, local_sem.at[7])
    scale_copy.start()

    def to_peers(axis, size, me, source, target, send_sems, recv_sems):
        copies = []
        for o in range(1, size):
            peer = lax.rem(me + o, size)
            copy = pltpu.make_async_remote_copy(
                src_ref=source(peer), dst_ref=target, send_sem=send_sems.at[o - 1],
                recv_sem=recv_sems.at[o - 1], device_id={axis: peer}, device_id_type=MESH,
            )
            copy.start()
            copies.append(copy)
        return copies

    def to_sibling(source, target, index):
        copy = pltpu.make_async_remote_copy(
            src_ref=source, dst_ref=target, send_sem=pair_send.at[index],
            recv_sem=pair_recv.at[index], device_id={"chan": sib}, device_id_type=MESH,
        )
        copy.start()
        return copy

    def rows_loop(count, step):
        def wrapped(index, carry):
            step(index)
            return carry
        lax.fori_loop(0, count, wrapped, 0)

    x_copy.wait()

    def fill(i):
        pad[H + i, COL:COL + ts, :] = x_ref[i].astype(F32)
    rows_loop(ts, fill)
    for d in range(H):
        strips[0, d * ts:(d + 1) * ts, :] = x_ref[d].astype(F32)

    def face_row(p):
        for d in range(H):
            strips[1, pl.ds(d * ts + p, 1), :] = pad[H + p, COL + ts - 1 - d:COL + ts - d, :]
            strips[2, pl.ds(d * ts + p, 1), :] = pad[H + ts - 1 - d, pl.ds(COL + ts - 1 - p, 1), :]
            strips[3, pl.ds(d * ts + p, 1), :] = pad[H + ts - 1 - p, COL + d:COL + d + 1, :]
    rows_loop(ts, face_row)
    for f in range(4):
        faces[me_t, f] = strips[f].astype(BF16)

    pl.semaphore_wait(barrier, tiles - 1 + dps - 1 + 1)
    mine = pl.ds(2 * me_c, 2)
    face_copies = to_peers("tile", tiles, me_t, lambda peer: faces.at[me_t, mine], faces.at[me_t, mine], face_send, face_recv)
    win_copy = to_sibling(w_in_ref, win.at[me_c], 0)
    wout_copy = to_sibling(w_out_ref, wout.at[me_c], 1)

    def zero_rows(i):
        cpad[i] = jnp.zeros(cpad.shape[1:], F32)
    rows_loop(cpad.shape[0], zero_rows)
    kacc[...] = jnp.zeros_like(kacc)

    face_passes = []
    for o in range(1, tiles):
        face_copies[o - 1].wait_recv()
        source = lax.rem(me_t - o + tiles, tiles)
        face_passes.append(to_sibling(faces.at[source, mine], faces.at[source, mine], 5 + o))
    for copy in face_passes:
        copy.wait_recv()

    adj_copy.wait()
    kern_copy.wait()
    for k in range(8):
        source = adj[me_t, 0, k]
        face = (adj[me_t, 1, k] + facing_turns[k]) % 4
        strips[k] = faces[source, face].astype(F32)
    for d in range(H):
        pad[H + ts + d, COL:COL + ts, :] = strips[2, d * ts:(d + 1) * ts, :]

    def rim_row(p):
        for d in range(H):
            pad[d, pl.ds(COL + p, 1), :] = strips[0, pl.ds((H - 1 - d) * ts + ts - 1 - p, 1), :]
            pad[H + p, COL + ts + d:COL + ts + d + 1, :] = strips[1, pl.ds(d * ts + ts - 1 - p, 1), :]
            pad[H + p, COL - H + d:COL - H + d + 1, :] = strips[3, pl.ds((H - 1 - d) * ts + p, 1), :]
    rows_loop(ts, rim_row)
    for i in range(H):
        for j in range(H):
            at = (H - 1 - i) * ts + ts - H + (H - 1 - j)
            pad[i, COL + ts + j:COL + ts + j + 1, :] = strips[4, at:at + 1, :]
            at = i * ts + j
            pad[H + ts + i, COL + ts + j:COL + ts + j + 1, :] = strips[5, at:at + 1, :]
            at = i * ts + ts - H + j
            pad[H + ts + i, COL - H + j:COL - H + j + 1, :] = strips[6, at:at + 1, :]
            at = (H - 1 - i) * ts + (H - 1 - j)
            pad[i, COL - H + j:COL - H + j + 1, :] = strips[7, at:at + 1, :]

    first = me_c * half

    def conv_rows(block):
        i = block * ROWS_AT_ONCE
        acc = [jnp.zeros((ts, pad.shape[2]), F32) for _ in range(ROWS_AT_ONCE)]
        for a in range(ROWS_AT_ONCE + KS - 1):
            for b in range(KS):
                window = pad[first + i + a, COL - H + b:COL - H + b + ts, :]
                for r in range(ROWS_AT_ONCE):
                    if 0 <= a - r < KS:
                        at = (a - r) * KS + b
                        acc[r] = acc[r] + window * kern[at:at + 1, :]
        for r in range(ROWS_AT_ONCE):
            conv_ref[i + r] = acc[r]
    rows_loop(half // ROWS_AT_ONCE, conv_rows)

    win_copy.wait_recv()
    wout_copy.wait_recv()
    win_local.wait()
    wout_local.wait()
    ct_copy.wait()
    gain_copy.wait()
    scale_copy.wait()

    gain = gain_ref[...]
    layer_scale = scale_ref[...]
    block_rows = 8
    pixels = block_rows * ts
    channels = pad.shape[2]
    gain_total = jnp.zeros((1, channels), F32)
    scale_total = jnp.zeros((1, channels), F32)
    for block in range(half // block_rows):
        at = block * block_rows
        conv = conv_ref[at:at + block_rows].reshape(pixels, channels)
        mean = jnp.mean(conv, axis=1, keepdims=True)
        centred = conv - mean
        inv_std = lax.rsqrt(jnp.mean(centred * centred, axis=1, keepdims=True) + eps)
        normed = centred * inv_std
        normed_b = (normed * gain).astype(BF16)
        upstream = ct_ref[pl.ds(first + at, block_rows)].reshape(pixels, channels).astype(F32)
        scaled_b = (upstream * layer_scale).astype(BF16)
        branch = jnp.zeros((pixels, channels), F32)
        normed_grad = jnp.zeros((pixels, channels), F32)
        for c in range(2):
            active, slope = gelu_pair(mm(normed_b, win[c], 1, 0))
            active_b = active.astype(BF16)
            branch = branch + mm(active_b, wout[c], 1, 0)
            hidden_grad = (mm(scaled_b, wout[c], 1, 1) * slope).astype(BF16)
            normed_grad = normed_grad + mm(hidden_grad, win[c], 1, 1)
            in_grad = mm(normed_b, hidden_grad, 0, 0)
            out_grad = mm(scaled_b, active_b, 0, 0)
            if block == 0:
                part[c, 0] = in_grad
                part[c, 1] = out_grad
            else:
                part[c, 0] += in_grad
                part[c, 1] += out_grad
        scale_total = scale_total + jnp.sum(upstream * branch, axis=0, keepdims=True)
        gain_total = gain_total + jnp.sum(normed_grad * normed, axis=0, keepdims=True)
        scaled = normed_grad * gain
        first_mean = jnp.mean(scaled, axis=1, keepdims=True)
        second_mean = jnp.mean(scaled * normed, axis=1, keepdims=True)
        grad_b = (inv_std * (scaled - first_mean - normed * second_mean)).astype(BF16)
        cg[pl.ds(first + at, block_rows)] = grad_b.reshape(block_rows, ts, channels)

    cg_copy = to_sibling(cg.at[pl.ds(first, half)], cg.at[pl.ds(first, half)], 2)
    part_copy = to_sibling(part.at[sib], chan_recv, 3)

    for a in range(KS):
        def kernel_row(i, acc):
            grad = cg[first + i].astype(F32)
            new = []
            for b in range(KS):
                window = pad[first + i + a, COL - H + b:COL - H + b + ts, :]
                new.append(acc[b] + jnp.sum((window * grad).reshape(ts // 8, 8, channels), axis=0))
            return tuple(new)
        sums = lax.fori_loop(0, half, kernel_row, tuple(jnp.zeros((8, channels), F32) for _ in range(KS)))
        for b in range(KS):
            kacc[a * KS + b] = sums[b]
    for c in range(2):
        small_part[c] = jnp.sum(kacc[c * SMALL_ROWS // 2:(c + 1) * SMALL_ROWS // 2], axis=1)
    at = KS * KS - SMALL_ROWS // 2
    small_part[1, at:at + 1, :] = gain_total
    small_part[1, at + 1:at + 2, :] = scale_total
    small_copy = to_sibling(small_part.at[sib], small_recv, 4)

    cg_copy.wait_recv()

    def widen(i):
        cpad[KS - 1 + i, COL:COL + ts, :] = cg[i].astype(F32)
    rows_loop(ts, widen)
    wide = gpad.shape[1]

    def spread_rows(block):
        i = block * ROWS_AT_ONCE
        acc = [jnp.zeros((wide, channels), F32) for _ in range(ROWS_AT_ONCE)]
        for a in range(ROWS_AT_ONCE + KS - 1):
            for b in range(KS):
                window = cpad[i + a, COL - (KS - 1) + b:COL - (KS - 1) + b + wide, :]
                for r in range(ROWS_AT_ONCE):
                    if 0 <= a - r < KS:
                        at = (KS - 1 - (a - r)) * KS + KS - 1 - b
                        acc[r] = acc[r] + window * kern[at:at + 1, :]
        for r in range(ROWS_AT_ONCE):
            gpad[i + r] = acc[r]
    spread_blocks = gpad.shape[0] // ROWS_AT_ONCE
    rows_loop(spread_blocks // 2, spread_rows)

    part_rows = channels // dps
    part_copy.wait_recv()
    for w in range(2):
        for d in range(dps):
            rows = slice(d * part_rows, (d + 1) * part_rows)
            dp_send[d, w] = part[me_c, w, rows, :] + chan_recv[w, rows, :]
    dp_recv[me_d] = dp_send[me_d]
    dp_copies = to_peers("dp", dps, me_d, lambda peer: dp_send.at[peer], dp_recv.at[me_d], dp_send_sem, dp_recv_sem)
    small_copy.wait_recv()
    small_dp[me_d] = small_part[me_c] + small_recv[...]
    sd_copies = to_peers("dp", dps, me_d, lambda peer: small_dp.at[me_d], small_dp.at[me_d], sd_send, sd_recv)

    def later_rows(block):
        spread_rows(block + spread_blocks // 2)
    rows_loop(spread_blocks - spread_blocks // 2, later_rows)

    def edge_row(p):
        for d in range(H):
            at = d * ts + p
            rimf[0, pl.ds(at, 1), :] = gpad[H - 1 - d, pl.ds(H + ts - 1 - p, 1), :]
            rimf[0, pl.ds(strip + at, 1), :] = gpad[H + ts - 1 - p, H + ts + d:H + ts + d + 1, :]
            rimf[1, pl.ds(strip + at, 1), :] = gpad[H + p, H - 1 - d:H - d, :]
    rows_loop(ts, edge_row)
    for c in range(2):
        rimf[c, 2 * strip:, :] = jnp.zeros((32, channels), F32)
    for d in range(H):
        rimf[1, d * ts:(d + 1) * ts, :] = gpad[H + ts + d, H:H + ts, :]
    for i in range(H):
        for j in range(H):
            spots = (
                (H - 1 - i, H + ts + H - 1 - j), (H + ts + i, H + ts + j),
                (H + ts + i, j), (H - 1 - i, H - 1 - j),
            )
            for k in range(4):
                at = 2 * strip + 16 * (k % 2) + H * i + j
                row, col = spots[k]
                rimf[k // 2, at:at + 1, :] = gpad[row, col:col + 1, :]
    rims[me_t] = rimf[...].astype(BF16)
    rim_copies = to_peers("tile", tiles, me_t, lambda peer: rims.at[me_t, me_c], rims.at[me_t, me_c], rim_send, rim_recv)

    piece_rows = 2 * part_rows // tiles
    for copy in dp_copies:
        copy.wait_recv()
    total = dp_recv[0]
    for d in range(1, dps):
        total = total + dp_recv[d]
    total = total.reshape(2 * part_rows, total.shape[2]).astype(BF16)
    for t in range(tiles):
        piece_send[t] = total[t * piece_rows:(t + 1) * piece_rows]
    piece_recv[me_t] = piece_send[me_t]
    rs_copies = to_peers("tile", tiles, me_t, lambda peer: piece_send.at[peer], piece_recv.at[me_t], rs_send, rs_recv)
    for copy in sd_copies:
        copy.wait_recv()
    total = small_dp[0]
    for d in range(1, dps):
        total = total + small_dp[d]
    small_tile[me_t] = total
    st_copies = to_peers("tile", tiles, me_t, lambda peer: small_tile.at[me_t], small_tile.at[me_t], st_send, st_recv)

    def base_row(i):
        base[i] = ct_ref[i].astype(F32) + gpad[H + i, H:H + ts, :]
    rows_loop(ts, base_row)

    for copy in rs_copies:
        copy.wait_recv()
    total = piece_recv[0].astype(F32)
    for t in range(1, tiles):
        total = total + piece_recv[t].astype(F32)
    piece_all[me_t] = (total * factor).astype(BF16)
    tg_copies = to_peers("tile", tiles, me_t, lambda peer: piece_all.at[me_t], piece_all.at[me_t], tg_send, tg_recv)
    for copy in st_copies:
        copy.wait_recv()
    total = small_tile[0]
    for t in range(1, tiles):
        total = total + small_tile[t]
    small_done[me_c] = total * factor
    done_copy = to_sibling(small_done.at[me_c], small_done.at[me_c], 5)

    rim_passes = []
    for o in range(1, tiles):
        rim_copies[o - 1].wait_recv()
        source = lax.rem(me_t - o + tiles, tiles)
        rim_passes.append(to_sibling(rims.at[source, me_c], rims.at[source, me_c], 5 + tiles - 1 + o))
    for copy in rim_passes:
        copy.wait_recv()
    for f in range(4):
        def gather(p, carry):
            edge, at_start, at_end = carry
            for k in range(8):
                face = (adj[p, 1, k] + facing_turns[k]) % 4
                chosen = jnp.where((adj[p, 0, k] == me_t) & (face == f), 1.0, 0.0).astype(F32)
                if k < 4:
                    edge = edge + chosen * rims[p, k // 2, strip * (k % 2):strip * (k % 2 + 1), :].astype(F32)
                else:
                    at = 2 * strip + 16 * (k % 2)
                    piece = chosen * rims[p, (k - 4) // 2, at:at + 16, :].astype(F32)
                    if corner_at_end[k - 4]:
                        at_end = at_end + piece
                    else:
                        at_start = at_start + piece
            return edge, at_start, at_end
        zero = jnp.zeros((16, channels), F32)
        edge, at_start, at_end = lax.fori_loop(0, tiles, gather, (jnp.zeros((strip, channels), F32), zero, zero))
        incoming[f] = edge
        for d in range(H):
            incoming[f, d * ts:d * ts + H, :] += at_start[d * H:(d + 1) * H]
            incoming[f, (d + 1) * ts - H:(d + 1) * ts, :] += at_end[d * H:(d + 1) * H]
    for d in range(H):
        base[d] += incoming[0, d * ts:(d + 1) * ts, :]

    def add_row(p):
        for d in range(H):
            base[p, ts - H + d:ts - H + d + 1, :] += incoming[1, pl.ds((H - 1 - d) * ts + p, 1), :]
            base[ts - H + d, pl.ds(p, 1), :] += incoming[2, pl.ds((H - 1 - d) * ts + ts - 1 - p, 1), :]
            base[p, d:d + 1, :] += incoming[3, pl.ds(d * ts + ts - 1 - p, 1), :]
    rows_loop(ts, add_row)

    def out_row(i):
        out_ref[i] = base[i].astype(BF16)
    rows_loop(ts, out_row)

    for copy in tg_copies:
        copy.wait_recv()
    for t in range(tiles):
        w_out_all[t * piece_rows:(t + 1) * piece_rows, :] = piece_all[t].astype(F32)
    done_copy.wait_recv()
    small_out[...] = small_done[...]

    for copy in face_copies + face_passes + rim_copies + rim_passes + rs_copies + dp_copies + sd_copies + tg_copies + st_copies + [
        win_copy, wout_copy, cg_copy, part_copy, small_copy, done_copy
    ]:
        copy.wait_send()


def write_out(out, small, grads, out_hbm, kernel_hbm, gain_hbm, w_in_hbm, w_out_hbm, scale_hbm, sems):
    taps = KS * KS
    rows = w_in_hbm.shape[0]
    pairs = (
        (out, out_hbm),
        (grads.at[:rows], w_in_hbm),
        (grads.at[rows:], w_out_hbm),
        (small.at[:taps], kernel_hbm),
        (small.at[taps:taps + 1], gain_hbm),
        (small.at[taps + 1:taps + 2], scale_hbm),
    )
    copies = [pltpu.make_async_copy(source, target, sems.at[i]) for i, (source, target) in enumerate(pairs)]
    for copy in copies:
        copy.start()
    for copy in copies:
        copy.wait()


def in_hbm(array):
    return pltpu.with_memory_space_constraint(array, pltpu.MemorySpace.HBM)


def on_device(inputs, kernel, norm_gain, w_in, w_out, layer_scale, cotangent, adjacency):
    ts, ch = inputs.shape[2], inputs.shape[4]
    hid = w_in.shape[1]
    tiles, dps = lax.axis_size("tile"), lax.axis_size("dp")
    factor = 1.0 / math.sqrt(dps * tiles * ts * ts)
    strip = H * ts
    rim_rows = 2 * strip + 32
    piece = 2 * (ch // dps) // tiles
    half_small = SMALL_ROWS // 2
    part_rows = ch // dps
    vmem = pl.BlockSpec(memory_space=pltpu.VMEM)
    hbm = pl.BlockSpec(memory_space=pltpu.MemorySpace.HBM)
    dma = pltpu.SemaphoreType.DMA
    peers_t, peers_d = max(tiles - 1, 1), max(dps - 1, 1)
    out, small, grads = pl.pallas_call(
        functools.partial(body, tiles, dps, factor),
        out_shape=(
            jax.ShapeDtypeStruct((ts, ts, ch), BF16),
            jax.ShapeDtypeStruct((2, SMALL_ROWS // 2, ch), F32),
            jax.ShapeDtypeStruct((2 * part_rows, hid), F32),
        ),
        in_specs=[hbm] * 8,
        out_specs=(vmem,) * 3,
        scratch_shapes=[
            pltpu.SMEM((tiles, 2, 8), jnp.int32),
            pltpu.VMEM((KS * KS, ch), F32),
            pltpu.VMEM((1, ch), F32),
            pltpu.VMEM((1, ch), F32),
            pltpu.VMEM((ts + 2 * H, ts + 2 * COL, ch), F32),
            pltpu.VMEM((8, strip, ch), F32),
            pltpu.VMEM((tiles, 4, strip, ch), BF16),
            pltpu.VMEM((2, ch, hid), BF16),
            pltpu.VMEM((2, hid, ch), BF16),
            pltpu.VMEM((ts // 2, ts, ch), F32),
            pltpu.VMEM((2, 2, ch, hid), F32),
            pltpu.VMEM((ts, ts, ch), BF16),
            pltpu.VMEM((ts + 2 * (KS - 1) + 2, ts + 2 * COL, ch), F32),
            pltpu.VMEM((ts + 2 * H + 2, ts + 8, ch), F32),
            pltpu.VMEM((2, rim_rows, ch), F32),
            pltpu.VMEM((tiles, 2, rim_rows, ch), BF16),
            pltpu.VMEM((4, strip, ch), F32),
            pltpu.VMEM((2, ch, hid), F32),
            pltpu.VMEM((dps, 2, part_rows, hid), F32),
            pltpu.VMEM((dps, 2, part_rows, hid), F32),
            pltpu.VMEM((tiles, piece, hid), BF16),
            pltpu.VMEM((tiles, piece, hid), BF16),
            pltpu.VMEM((tiles, piece, hid), BF16),
            pltpu.VMEM((SMALL_ROWS, 8, ch), F32),
            pltpu.VMEM((2, half_small, ch), F32),
            pltpu.VMEM((half_small, ch), F32),
            pltpu.VMEM((dps, half_small, ch), F32),
            pltpu.VMEM((tiles, half_small, ch), F32),
            pltpu.VMEM((2, half_small, ch), F32),
            pltpu.VMEM((ts, ts, ch), F32),
            pltpu.VMEM((ts, ts, ch), BF16),
            pltpu.VMEM((ts, ts, ch), BF16),
            dma((8,)),
            dma((peers_t,)), dma((peers_t,)), dma((4 + 2 * tiles,)), dma((4 + 2 * tiles,)), dma((peers_t,)), dma((peers_t,)),
            dma((peers_d,)), dma((peers_d,)), dma((peers_t,)), dma((peers_t,)), dma((peers_t,)), dma((peers_t,)),
            dma((peers_d,)), dma((peers_d,)), dma((peers_t,)), dma((peers_t,)),
        ],
        compiler_params=pltpu.CompilerParams(
            collective_id=0, has_side_effects=True, vmem_limit_bytes=48 * 1024 * 1024
        ),
    )(
        in_hbm(jnp.transpose(adjacency, (0, 2, 1))), in_hbm(inputs[0, 0]), in_hbm(cotangent[0, 0]), in_hbm(kernel),
        in_hbm(norm_gain[None]), in_hbm(w_in), in_hbm(w_out), in_hbm(layer_scale[None]),
    )
    results = pl.pallas_call(
        write_out,
        out_shape=(
            jax.ShapeDtypeStruct((ts, ts, ch), BF16),
            jax.ShapeDtypeStruct((KS * KS, ch), F32),
            jax.ShapeDtypeStruct((1, ch), F32),
            jax.ShapeDtypeStruct((part_rows, hid), F32),
            jax.ShapeDtypeStruct((part_rows, hid), F32),
            jax.ShapeDtypeStruct((1, ch), F32),
        ),
        in_specs=[pl.BlockSpec(memory_space=pl.ANY)] * 3,
        out_specs=(hbm,) * 6,
        scratch_shapes=[dma((6,))],
        compiler_params=pltpu.CompilerParams(vmem_limit_bytes=1024 * 1024),
    )(out, small.reshape(SMALL_ROWS, ch), grads)
    return (
        results[0][None, None],
        results[1],
        results[2].reshape(ch),
        results[3],
        results[4].T,
        results[5].reshape(ch),
    )


def solution(mesh):
    placed = (
        P(("group", "dp"), "tile", None, None, None),
        P(),
        P(),
        P(None, "chan"),
        P("chan", None),
        P(),
        P(("group", "dp"), "tile", None, None, None),
        P(),
    )
    return jax.shard_map(
        on_device,
        mesh=mesh,
        in_specs=placed,
        out_specs=(
            P(("group", "dp"), "tile", None, None, None),
            P("group", None),
            P("group"),
            P(("group", "dp"), "chan"),
            P(("group", "chan"), "dp"),
            P("group"),
        ),
        check_vma=False,
    )
```

```python
import functools
import math

import jax
import jax.numpy as jnp
from jax import lax
from jax.experimental import pallas as pl
from jax.experimental.pallas import tpu as pltpu
from jax.sharding import PartitionSpec as P

KS = 7
H = KS // 2
COL = 8
ROWS_AT_ONCE = 4
SMALL_ROWS = 64
SIDE_ROWS = 64
SLOT_ROWS = 2 * SIDE_ROWS
CORNER_ROWS = 16

eps = 1e-06
root_two_pi = 0.7978845608028654
cubic_coef = 0.044715
MESH = pl.DeviceIdType.MESH
F32 = jnp.float32
BF16 = jnp.bfloat16


def gelu_pair(values):
    square = values * values
    tanh_part = jnp.tanh(values * (root_two_pi + (root_two_pi * cubic_coef) * square))
    half_up = 0.5 + 0.5 * tanh_part
    active = values * half_up
    gelu_slope = half_up + active * (1.0 - tanh_part) * (
        root_two_pi + (3.0 * root_two_pi * cubic_coef) * square
    )
    return active, gelu_slope


def mm(left, right, left_dim, right_dim):
    return lax.dot_general(
        left, right, (((left_dim,), (right_dim,)), ((), ())), preferred_element_type=F32
    )


def slot_source(adj, owner, reader, core, slot, ts):
    half = ts // 2
    span = half + H
    strip = H * ts
    lower = core == 1
    edge_k, first_k, second_k = 2 * core, 4 + core, 7 - core
    near_turn = 2 - 2 * core

    def edge(face, flipped, depth, along):
        return face * strip + depth * ts + jnp.where(flipped, ts - 1 - along, along)

    def corner(face, depth, along):
        return face * strip + depth * ts + jnp.where(face < 2, along, ts - 1 - along)

    face = (adj[reader, 1, edge_k] + near_turn) % 4
    row_edge = edge(face, (core == 0) == (face < 2), slot // ts, slot % ts)
    is_row = adj[reader, 0, edge_k] == owner

    within = slot % SIDE_ROWS
    depth = jnp.where(within >= span, 1, 0) + jnp.where(within >= 2 * span, 1, 0)
    along = within - depth * span + core * (half - H)
    east = (adj[reader, 1, 1] + 3) % 4
    west = (adj[reader, 1, 3] + 1) % 4
    on_east = slot < SIDE_ROWS
    side = jnp.where(on_east, edge(east, east < 2, depth, along), edge(west, west >= 2, depth, along))
    east_here, west_here = adj[reader, 0, 1] == owner, adj[reader, 0, 3] == owner
    side_ok = (within < H * span) & ((on_east & east_here) | ((slot >= SIDE_ROWS) & west_here))

    spot = slot % CORNER_ROWS
    i = jnp.where(spot >= H, 1, 0) + jnp.where(spot >= 2 * H, 1, 0)
    j = spot - H * i
    into = jnp.where(lower, i, H - 1 - i)
    face_a = (adj[reader, 1, first_k] + near_turn) % 4
    face_b = (adj[reader, 1, second_k] + near_turn) % 4
    on_a = slot < CORNER_ROWS
    piece = jnp.where(
        on_a,
        corner(face_a, into, jnp.where(lower, j, ts - 1 - j)),
        corner(face_b, into, jnp.where(lower, ts - H + j, H - 1 - j)),
    )
    a_here, b_here = adj[reader, 0, first_k] == owner, adj[reader, 0, second_k] == owner
    piece_ok = (spot < H * H) & ((on_a & a_here) | ((slot >= CORNER_ROWS) & (slot < 2 * CORNER_ROWS) & b_here))

    found = jnp.where(side_ok, side, jnp.where(piece_ok & ~(east_here | west_here), piece, -1))
    return jnp.where(is_row, jnp.where(slot < strip, row_edge, -1), found)


def body(
    tiles, dps, factor,
    adj_hbm, x_hbm, ct_hbm, kern_hbm, gain_hbm, w_in_ref, w_out_ref, scale_hbm,
    out_ref, small_out, w_out_all,
    adj, kern, gain_ref, scale_ref, x_ref, ct_ref, pad, faces, sel, sel_t, face_slots, halo, side_tmp, corner_tmp,
    win, wout, conv_ref, part, chan_recv, cg, cpad, vert, stage, rim_slots, rims,
    dp_send, dp_recv, piece_send, piece_recv, piece_all, kacc, small_mine, small_sib, small_dp, small_tile, base,
    local_sem, face_send, face_recv, pair_send, pair_recv, rim_send, rim_recv,
    dp_send_sem, dp_recv_sem, rs_send, rs_recv, tg_send, tg_recv, sd_send, sd_recv, st_send, st_recv,
):
    ts = x_ref.shape[0]
    channels = x_ref.shape[2]
    wide = ts + 2 * COL
    half = ts // 2
    span = half + H
    strip = H * ts
    me_t = lax.axis_index("tile")
    me_d = lax.axis_index("dp")
    me_c = lax.axis_index("chan")
    sib = 1 - me_c
    first = me_c * half
    side_first = me_c * (half - H)

    barrier = pltpu.get_barrier_semaphore()
    for o in range(1, tiles):
        pl.semaphore_signal(barrier, inc=1, device_id={"tile": lax.rem(me_t + o, tiles)}, device_id_type=MESH)
    for o in range(1, dps):
        pl.semaphore_signal(barrier, inc=1, device_id={"dp": lax.rem(me_d + o, dps)}, device_id_type=MESH)
    pl.semaphore_signal(barrier, inc=1, device_id={"chan": sib}, device_id_type=MESH)

    local = []
    for source, target in (
        (adj_hbm, adj), (x_hbm, x_ref), (kern_hbm, kern), (w_in_ref, win.at[me_c]), (w_out_ref, wout.at[me_c]),
        (ct_hbm, ct_ref), (gain_hbm, gain_ref), (scale_hbm, scale_ref),
    ):
        copy = pltpu.make_async_copy(source, target, local_sem.at[len(local)])
        copy.start()
        local.append(copy)

    def to_peers(axis, size, me, source, target, send_sems, recv_sems):
        copies = []
        for o in range(1, size):
            peer = lax.rem(me + o, size)
            copy = pltpu.make_async_remote_copy(
                src_ref=source(o, peer), dst_ref=target, send_sem=send_sems.at[o - 1],
                recv_sem=recv_sems.at[o - 1], device_id={axis: peer}, device_id_type=MESH,
            )
            copy.start()
            copies.append(copy)
        return copies

    def to_sibling(source, target, index):
        copy = pltpu.make_async_remote_copy(
            src_ref=source, dst_ref=target, send_sem=pair_send.at[index],
            recv_sem=pair_recv.at[index], device_id={"chan": sib}, device_id_type=MESH,
        )
        copy.start()
        return copy

    def rows_loop(count, step):
        def wrapped(index, carry):
            step(index)
            return carry
        lax.fori_loop(0, count, wrapped, 0)

    def zero_pad(i):
        pad[pl.ds(pl.multiple_of(i * wide, 8), wide), :] = jnp.zeros((wide, channels), F32)
    rows_loop(ts + 2 * H, zero_pad)

    local[0].wait()
    slot_down = lax.broadcasted_iota(jnp.int32, (SLOT_ROWS, 1), 0)
    face_across = lax.broadcasted_iota(jnp.int32, (SLOT_ROWS, 4 * strip), 1)
    for o in range(1, tiles):
        peer = lax.rem(me_t + o, tiles)
        chosen = slot_source(adj, me_t, peer, me_c, slot_down, ts)
        sel[o - 1] = jnp.where(face_across == chosen, 1.0, 0.0).astype(BF16)

    local[1].wait()

    def fill(i):
        pad[pl.ds(pl.multiple_of((H + i) * wide + COL, 8), ts), :] = x_ref[i].astype(F32)
    rows_loop(ts, fill)
    for d in range(H):
        faces[d * ts:(d + 1) * ts, :] = x_ref[d]
        faces[2 * strip + d * ts:2 * strip + (d + 1) * ts, :] = x_ref[ts - 1 - d]
        for f, col in ((1, COL + ts - 1 - d), (3, COL + d)):
            column = pad[pl.ds(H * wide + col, ts, stride=wide), :]
            faces[f * strip + d * ts:f * strip + (d + 1) * ts, :] = column.astype(BF16)
    for o in range(1, tiles):
        face_slots[o - 1] = mm(sel[o - 1], faces[...], 1, 0).astype(BF16)

    pl.semaphore_wait(barrier, tiles - 1 + dps - 1 + 1)
    face_copies = to_peers("tile", tiles, me_t, lambda o, peer: face_slots.at[o - 1], halo.at[me_t], face_send, face_recv)
    win_copy = to_sibling(w_in_ref, win.at[me_c], 0)
    wout_copy = to_sibling(w_out_ref, wout.at[me_c], 1)

    halo[me_t] = jnp.zeros((SLOT_ROWS, channels), BF16)
    local[2].wait()

    def conv_rows(block):
        i = block * ROWS_AT_ONCE
        acc = [jnp.zeros((ts, channels), F32) for _ in range(ROWS_AT_ONCE)]
        for a in range(ROWS_AT_ONCE + KS - 1):
            for b in range(KS):
                window = pad[pl.ds((first + i + a) * wide + COL - H + b, ts), :]
                for r in range(ROWS_AT_ONCE):
                    if 0 <= a - r < KS:
                        at = (a - r) * KS + b
                        acc[r] = acc[r] + window * kern[at:at + 1, :]
        for r in range(ROWS_AT_ONCE):
            conv_ref[pl.ds(pl.multiple_of((i + r) * ts, 8), ts), :] = acc[r]
    rows_loop(half // ROWS_AT_ONCE, conv_rows)

    def zero_rows(i):
        cpad[pl.ds(pl.multiple_of(i * wide, 8), wide), :] = jnp.zeros((wide, channels), F32)
    rows_loop(cpad.shape[0] // wide, zero_rows)
    kacc[...] = jnp.zeros_like(kacc)
    slot_across = lax.broadcasted_iota(jnp.int32, (1, SLOT_ROWS), 1)
    face_down = lax.broadcasted_iota(jnp.int32, (4 * strip, SLOT_ROWS), 0)
    for core in range(2):
        for o in range(1, tiles):
            peer = lax.rem(me_t + o, tiles)
            chosen = slot_source(adj, me_t, peer, core, slot_across, ts)
            sel_t[core, o - 1] = jnp.where(face_down == chosen, 1.0, 0.0).astype(BF16)

    for copy in face_copies:
        copy.wait_recv()
    side_tmp[0] = halo[adj[me_t, 0, 1], :SIDE_ROWS].astype(F32)
    side_tmp[1] = halo[adj[me_t, 0, 3], SIDE_ROWS:].astype(F32)
    corner_tmp[0] = halo[adj[me_t, 0, 4 + me_c], :CORNER_ROWS].astype(F32)
    corner_tmp[1] = halo[adj[me_t, 0, 7 - me_c], CORNER_ROWS:2 * CORNER_ROWS].astype(F32)
    row_strip = halo[adj[me_t, 0, 2 * me_c], :strip].astype(F32)
    side_row = (H + side_first) * wide
    for d in range(H):
        pad[pl.ds(side_row + COL + ts + d, span, stride=wide), :] = side_tmp[0, d * span:(d + 1) * span, :]
        pad[pl.ds(side_row + COL - 1 - d, span, stride=wide), :] = side_tmp[1, d * span:(d + 1) * span, :]

    west_fix = [jnp.zeros((half, channels), F32) for _ in range(H)]
    east_fix = [jnp.zeros((half, channels), F32) for _ in range(H)]
    for a in range(KS):
        for e in range(H):
            west = pad[pl.ds((first + a) * wide + COL - H + e, half, stride=wide), :]
            east = pad[pl.ds((first + a) * wide + COL + ts + e, half, stride=wide), :]
            for m in range(H):
                if m <= e:
                    at = a * KS + e - m
                    west_fix[m] = west_fix[m] + west * kern[at:at + 1, :]
                if e + m < H:
                    at = a * KS + H + 1 + e + m
                    east_fix[m] = east_fix[m] + east * kern[at:at + 1, :]
    for m in range(H):
        conv_ref[pl.ds(m, half, stride=ts), :] += west_fix[m]
        conv_ref[pl.ds(ts - 1 - m, half, stride=ts), :] += east_fix[m]

    for d in range(H):
        row = H - 1 - d + me_c * (ts + 1 + 2 * d)
        pad[pl.ds(pl.multiple_of(row * wide + COL, 8), ts), :] = row_strip[d * ts:(d + 1) * ts]
    for i in range(H):
        row = i + me_c * (ts + H)
        pad[pl.ds(row * wide + COL + ts, H), :] = corner_tmp[0, H * i:H * (i + 1), :]
        pad[pl.ds(row * wide + COL - H, H), :] = corner_tmp[1, H * i:H * (i + 1), :]
    row_fix = [jnp.zeros((ts, channels), F32) for _ in range(H)]
    for h in range(H):
        for b in range(KS):
            window = pad[pl.ds((h + me_c * (ts + 2 * H - 1 - 2 * h)) * wide + COL - H + b, ts), :]
            for i in range(h + 1):
                a = h - i + me_c * (KS - 1 - 2 * (h - i))
                row_fix[i] = row_fix[i] + window * kern[pl.ds(a * KS + b, 1), :]
    for i in range(H):
        conv_ref[pl.ds(pl.multiple_of((i + me_c * (half - 1 - 2 * i)) * ts, 8), ts), :] += row_fix[i]

    win_copy.wait_recv()
    wout_copy.wait_recv()
    for copy in local[3:]:
        copy.wait()

    gain = gain_ref[...]
    layer_scale = scale_ref[...]
    block_rows = 8
    pixels = block_rows * ts
    gain_total = jnp.zeros((1, channels), F32)
    scale_total = jnp.zeros((1, channels), F32)
    blocks = []
    for block in range(half // block_rows):
        at = block * block_rows
        conv = conv_ref[at * ts:(at + block_rows) * ts, :]
        mean = jnp.mean(conv, axis=1, keepdims=True)
        centred = conv - mean
        inv_std = lax.rsqrt(jnp.mean(centred * centred, axis=1, keepdims=True) + eps)
        normed = centred * inv_std
        normed_b = (normed * gain).astype(BF16)
        upstream = ct_ref[pl.ds(first + at, block_rows)].reshape(pixels, channels).astype(F32)
        scaled_b = (upstream * layer_scale).astype(BF16)
        blocks.append([inv_std, normed, normed_b, upstream, scaled_b, 0.0, 0.0])
    part_copy = None
    for c in (sib, me_c):
        for block, state in enumerate(blocks):
            inv_std, normed, normed_b, upstream, scaled_b, branch, normed_grad = state
            active, slope = gelu_pair(mm(normed_b, win[c], 1, 0))
            active_b = active.astype(BF16)
            state[5] = branch + mm(active_b, wout[c], 1, 0)
            hidden_grad = (mm(scaled_b, wout[c], 1, 1) * slope).astype(BF16)
            state[6] = normed_grad + mm(hidden_grad, win[c], 1, 1)
            in_grad = mm(normed_b, hidden_grad, 0, 0)
            out_grad = mm(scaled_b, active_b, 0, 0)
            if block == 0:
                part[c, 0] = in_grad
                part[c, 1] = out_grad
            else:
                part[c, 0] += in_grad
                part[c, 1] += out_grad
        if part_copy is None:
            part_copy = to_sibling(part.at[sib], chan_recv, 3)
    for block, (inv_std, normed, normed_b, upstream, scaled_b, branch, normed_grad) in enumerate(blocks):
        at = block * block_rows
        scaled = normed_grad * gain
        first_mean = jnp.mean(scaled, axis=1, keepdims=True)
        second_mean = jnp.mean(scaled * normed, axis=1, keepdims=True)
        grad_b = (inv_std * (scaled - first_mean - normed * second_mean)).astype(BF16)
        cg[pl.ds(first + at, block_rows)] = grad_b.reshape(block_rows, ts, channels)
        scale_total = scale_total + jnp.sum(upstream * branch, axis=0, keepdims=True)
        gain_total = gain_total + jnp.sum(normed_grad * normed, axis=0, keepdims=True)
    cg_copy = to_sibling(cg.at[pl.ds(first, half)], cg.at[pl.ds(first, half)], 2)

    part_rows = channels // dps
    part_copy.wait_recv()
    for w in range(2):
        for d in range(dps):
            rows = slice(d * part_rows, (d + 1) * part_rows)
            dp_send[d, w * part_rows:(w + 1) * part_rows] = (part[me_c, w, rows, :] + chan_recv[w, rows, :]).astype(BF16)
    dp_recv[me_d] = dp_send[me_d]
    dp_copies = to_peers("dp", dps, me_d, lambda o, peer: dp_send.at[peer], dp_recv.at[me_d], dp_send_sem, dp_recv_sem)

    def widen(row):
        cpad[pl.ds(pl.multiple_of((KS - 1 + row) * wide + COL, 8), ts), :] = cg[row].astype(F32)
    rows_loop(half, lambda i: widen(first + i))

    across = ts + 8
    for h in range(H):
        acc = jnp.zeros((across, channels), F32)
        for i in range(h + 1):
            row = KS - 1 + i + me_c * (ts - 1 - 2 * i)
            a = h - i + me_c * (KS - 1 - 2 * (h - i))
            for b in range(KS):
                acc = acc + cpad[pl.ds(row * wide + COL - b, across), :] * kern[pl.ds(a * KS + b, 1), :]
        vert[h * across:(h + 1) * across, :] = acc
    west_rim = [jnp.zeros((24, channels), F32) for _ in range(H)]
    east_rim = [jnp.zeros((24, channels), F32) for _ in range(H)]
    for a in range(KS):
        row = (KS - 1 + H + side_first - a) * wide
        for j in range(H):
            west = cpad[pl.ds(row + COL + j, 24, stride=wide), :]
            east = cpad[pl.ds(row + COL + ts - 1 - j, 24, stride=wide), :]
            for d in range(H):
                if j <= H - 1 - d:
                    at = a * KS + H - 1 - d - j
                    west_rim[d] = west_rim[d] + west * kern[at:at + 1, :]
                    at = a * KS + H + 1 + d + j
                    east_rim[d] = east_rim[d] + east * kern[at:at + 1, :]
    for s in range(2):
        side_tmp[s] = jnp.zeros((SIDE_ROWS, channels), F32)
        corner_tmp[s] = jnp.zeros((CORNER_ROWS, channels), F32)
    for d in range(H):
        side_tmp[0, d * span:d * span + 24, :] = east_rim[d]
        side_tmp[1, d * span:d * span + 24, :] = west_rim[d]
    for i in range(H):
        row = (i + me_c * (H - 1 - 2 * i)) * across
        corner_tmp[0, H * i:H * (i + 1), :] = vert[pl.ds(row + H + ts, H), :]
        corner_tmp[1, H * i:H * (i + 1), :] = vert[pl.ds(row, H), :]
    for h in range(H):
        d = H - 1 - h
        stage[0, d * ts:(d + 1) * ts, :] = vert[h * across + H:h * across + H + ts, :].astype(BF16)
    stage[0, strip:, :] = jnp.zeros((SLOT_ROWS - strip, channels), BF16)
    stage[2, 2 * CORNER_ROWS:, :] = jnp.zeros((SLOT_ROWS - 2 * CORNER_ROWS, channels), BF16)
    for s in range(2):
        stage[1, s * SIDE_ROWS:(s + 1) * SIDE_ROWS, :] = side_tmp[s].astype(BF16)
        stage[2, s * CORNER_ROWS:(s + 1) * CORNER_ROWS, :] = corner_tmp[s].astype(BF16)
    for o in range(1, tiles):
        peer = lax.rem(me_t + o, tiles)
        beside = (adj[me_t, 0, 1] == peer) | (adj[me_t, 0, 3] == peer)
        kind = jnp.where(adj[me_t, 0, 2 * me_c] == peer, 0, jnp.where(beside, 1, 2))
        rim_slots[o - 1] = stage[kind]
    rim_copies = to_peers("tile", tiles, me_t, lambda o, peer: rim_slots.at[o - 1], rims.at[me_c, me_t], rim_send, rim_recv)

    for a in range(KS):
        def kernel_row(i, acc):
            grad = cpad[pl.ds(pl.multiple_of((KS - 1 + first + i) * wide + COL, 8), ts), :]
            new = []
            for b in range(KS):
                window = pad[pl.ds((first + i + a) * wide + COL - H + b, ts), :]
                new.append(acc[b] + jnp.sum((window * grad).reshape(ts // 8, 8, channels), axis=0))
            return tuple(new)
        sums = lax.fori_loop(0, half, kernel_row, tuple(jnp.zeros((8, channels), F32) for _ in range(KS)))
        for b in range(KS):
            kacc[a * KS + b] = sums[b]
    taps = KS * KS
    kacc[taps, 0:1, :] = gain_total
    kacc[taps + 1, 0:1, :] = scale_total
    small_mine[...] = jnp.sum(kacc[...], axis=1).astype(BF16)
    small_copy = to_sibling(small_mine, small_sib, 4)

    piece_rows = 2 * part_rows // tiles
    for copy in dp_copies:
        copy.wait_recv()
    total = dp_recv[0].astype(F32)
    for d in range(1, dps):
        total = total + dp_recv[d].astype(F32)
    total = total.astype(BF16)
    for t in range(tiles):
        piece_send[t] = total[t * piece_rows:(t + 1) * piece_rows]
    piece_recv[me_t] = piece_send[me_t]
    rs_copies = to_peers("tile", tiles, me_t, lambda o, peer: piece_send.at[peer], piece_recv.at[me_t], rs_send, rs_recv)

    small_copy.wait_recv()
    small_dp[me_d] = (small_mine[...].astype(F32) + small_sib[...].astype(F32)).astype(BF16)
    sd_copies = to_peers("dp", dps, me_d, lambda o, peer: small_dp.at[me_d], small_dp.at[me_d], sd_send, sd_recv)

    cg_copy.wait_recv()
    rows_loop(half, lambda i: widen(sib * half + i))

    def spread_rows(block):
        i = block * ROWS_AT_ONCE
        acc = [ct_ref[i + r].astype(F32) for r in range(ROWS_AT_ONCE)]
        for up in range(ROWS_AT_ONCE + KS - 1):
            for b in range(KS):
                window = cpad[pl.ds((i + H + up) * wide + COL + H - b, ts), :]
                for r in range(ROWS_AT_ONCE):
                    a = KS - 1 + r - up
                    if 0 <= a < KS:
                        acc[r] = acc[r] + window * kern[a * KS + b:a * KS + b + 1, :]
        for r in range(ROWS_AT_ONCE):
            base[pl.ds(pl.multiple_of((i + r) * ts, 8), ts), :] = acc[r]
    spread_blocks = ts // ROWS_AT_ONCE
    rows_loop(spread_blocks // 2, spread_rows)

    for copy in sd_copies:
        copy.wait_recv()
    total = small_dp[0].astype(F32)
    for d in range(1, dps):
        total = total + small_dp[d].astype(F32)
    small_tile[me_t] = total.astype(BF16)
    st_copies = to_peers("tile", tiles, me_t, lambda o, peer: small_tile.at[me_t], small_tile.at[me_t], st_send, st_recv)

    rows_loop(spread_blocks - spread_blocks // 2, lambda block: spread_rows(block + spread_blocks // 2))

    rim_passes = []
    for o in range(1, tiles):
        rim_copies[o - 1].wait_recv()
        source = lax.rem(me_t - o + tiles, tiles)
        rim_passes.append(to_sibling(rims.at[me_c, source], rims.at[me_c, source], 4 + o))

    for copy in rs_copies:
        copy.wait_recv()
    total = piece_recv[0].astype(F32)
    for t in range(1, tiles):
        total = total + piece_recv[t].astype(F32)
    piece_all[me_t] = (total * factor).astype(BF16)
    tg_copies = to_peers("tile", tiles, me_t, lambda o, peer: piece_all.at[me_t], piece_all.at[me_t], tg_send, tg_recv)

    for copy in rim_passes:
        copy.wait_recv()
    incoming = jnp.zeros((4 * strip, channels), F32)
    for core in range(2):
        for o in range(1, tiles):
            peer = lax.rem(me_t + o, tiles)
            incoming = incoming + mm(sel_t[core, o - 1], rims[core, peer], 1, 0)
    for d in range(H):
        part_of = [incoming[f * strip + d * ts:f * strip + (d + 1) * ts] for f in range(4)]
        base[d * ts:(d + 1) * ts, :] += part_of[0]
        base[(ts - 1 - d) * ts:(ts - d) * ts, :] += part_of[2]
        base[pl.ds(ts - 1 - d, ts, stride=ts), :] += part_of[1]
        base[pl.ds(d, ts, stride=ts), :] += part_of[3]

    def out_row(i):
        out_ref[i] = base[pl.ds(pl.multiple_of(i * ts, 8), ts), :].astype(BF16)
    rows_loop(ts, out_row)

    for copy in st_copies:
        copy.wait_recv()
    total = small_tile[0].astype(F32)
    for t in range(1, tiles):
        total = total + small_tile[t].astype(F32)
    small_out[...] = total * factor
    for copy in tg_copies:
        copy.wait_recv()
    for t in range(tiles):
        w_out_all[t * piece_rows:(t + 1) * piece_rows, :] = piece_all[t].astype(F32)

    for copy in face_copies + rim_copies + rim_passes + rs_copies + dp_copies + sd_copies + tg_copies + st_copies + [
        win_copy, wout_copy, cg_copy, part_copy, small_copy
    ]:
        copy.wait_send()


def write_out(out, small, grads, out_hbm, kernel_hbm, gain_hbm, w_in_hbm, w_out_hbm, scale_hbm, sems):
    taps = KS * KS
    rows = w_in_hbm.shape[0]
    pairs = (
        (out, out_hbm),
        (grads.at[:rows], w_in_hbm),
        (grads.at[rows:], w_out_hbm),
        (small.at[:taps], kernel_hbm),
        (small.at[taps:taps + 1], gain_hbm),
        (small.at[taps + 1:taps + 2], scale_hbm),
    )
    copies = [pltpu.make_async_copy(source, target, sems.at[i]) for i, (source, target) in enumerate(pairs)]
    for copy in copies:
        copy.start()
    for copy in copies:
        copy.wait()


def in_hbm(array):
    return pltpu.with_memory_space_constraint(array, pltpu.MemorySpace.HBM)


def on_device(inputs, kernel, norm_gain, w_in, w_out, layer_scale, cotangent, adjacency):
    ts, ch = inputs.shape[2], inputs.shape[4]
    hid = w_in.shape[1]
    tiles, dps = lax.axis_size("tile"), lax.axis_size("dp")
    factor = 1.0 / math.sqrt(dps * tiles * ts * ts)
    strip = H * ts
    wide = ts + 2 * COL
    part_rows = ch // dps
    piece = 2 * part_rows // tiles
    vmem = pl.BlockSpec(memory_space=pltpu.VMEM)
    hbm = pl.BlockSpec(memory_space=pltpu.MemorySpace.HBM)
    dma = pltpu.SemaphoreType.DMA
    peers_t, peers_d = max(tiles - 1, 1), max(dps - 1, 1)
    pairs = 5 + peers_t
    out, small, grads = pl.pallas_call(
        functools.partial(body, tiles, dps, factor),
        out_shape=(
            jax.ShapeDtypeStruct((ts, ts, ch), BF16),
            jax.ShapeDtypeStruct((SMALL_ROWS, ch), F32),
            jax.ShapeDtypeStruct((2 * part_rows, hid), F32),
        ),
        in_specs=[hbm] * 8,
        out_specs=(vmem,) * 3,
        scratch_shapes=[
            pltpu.SMEM((tiles, 2, 8), jnp.int32),
            pltpu.VMEM((KS * KS, ch), F32),
            pltpu.VMEM((1, ch), F32),
            pltpu.VMEM((1, ch), F32),
            pltpu.VMEM((ts, ts, ch), BF16),
            pltpu.VMEM((ts, ts, ch), BF16),
            pltpu.VMEM(((ts + 2 * H) * wide, ch), F32),
            pltpu.VMEM((4 * strip, ch), BF16),
            pltpu.VMEM((peers_t, SLOT_ROWS, 4 * strip), BF16),
            pltpu.VMEM((2, peers_t, 4 * strip, SLOT_ROWS), BF16),
            pltpu.VMEM((peers_t, SLOT_ROWS, ch), BF16),
            pltpu.VMEM((tiles, SLOT_ROWS, ch), BF16),
            pltpu.VMEM((2, SIDE_ROWS, ch), F32),
            pltpu.VMEM((2, CORNER_ROWS, ch), F32),
            pltpu.VMEM((2, ch, hid), BF16),
            pltpu.VMEM((2, hid, ch), BF16),
            pltpu.VMEM((ts // 2 * ts, ch), F32),
            pltpu.VMEM((2, 2, ch, hid), F32),
            pltpu.VMEM((2, ch, hid), F32),
            pltpu.VMEM((ts, ts, ch), BF16),
            pltpu.VMEM(((ts + 2 * KS) * wide, ch), F32),
            pltpu.VMEM((H * (ts + 8), ch), F32),
            pltpu.VMEM((3, SLOT_ROWS, ch), BF16),
            pltpu.VMEM((peers_t, SLOT_ROWS, ch), BF16),
            pltpu.VMEM((2, tiles, SLOT_ROWS, ch), BF16),
            pltpu.VMEM((dps, 2 * part_rows, hid), BF16),
            pltpu.VMEM((dps, 2 * part_rows, hid), BF16),
            pltpu.VMEM((tiles, piece, hid), BF16),
            pltpu.VMEM((tiles, piece, hid), BF16),
            pltpu.VMEM((tiles, piece, hid), BF16),
            pltpu.VMEM((SMALL_ROWS, 8, ch), F32),
            pltpu.VMEM((SMALL_ROWS, ch), BF16),
            pltpu.VMEM((SMALL_ROWS, ch), BF16),
            pltpu.VMEM((dps, SMALL_ROWS, ch), BF16),
            pltpu.VMEM((tiles, SMALL_ROWS, ch), BF16),
            pltpu.VMEM((ts * ts, ch), F32),
            dma((8,)),
            dma((peers_t,)), dma((peers_t,)), dma((pairs,)), dma((pairs,)), dma((peers_t,)), dma((peers_t,)),
            dma((peers_d,)), dma((peers_d,)), dma((peers_t,)), dma((peers_t,)), dma((peers_t,)), dma((peers_t,)),
            dma((peers_d,)), dma((peers_d,)), dma((peers_t,)), dma((peers_t,)),
        ],
        compiler_params=pltpu.CompilerParams(
            collective_id=0, has_side_effects=True, vmem_limit_bytes=48 * 1024 * 1024
        ),
    )(
        in_hbm(jnp.transpose(adjacency, (0, 2, 1))), in_hbm(inputs[0, 0]), in_hbm(cotangent[0, 0]), in_hbm(kernel),
        in_hbm(norm_gain[None]), in_hbm(w_in), in_hbm(w_out), in_hbm(layer_scale[None]),
    )
    results = pl.pallas_call(
        write_out,
        out_shape=(
            jax.ShapeDtypeStruct((ts, ts, ch), BF16),
            jax.ShapeDtypeStruct((KS * KS, ch), F32),
            jax.ShapeDtypeStruct((1, ch), F32),
            jax.ShapeDtypeStruct((part_rows, hid), F32),
            jax.ShapeDtypeStruct((part_rows, hid), F32),
            jax.ShapeDtypeStruct((1, ch), F32),
        ),
        in_specs=[pl.BlockSpec(memory_space=pl.ANY)] * 3,
        out_specs=(hbm,) * 6,
        scratch_shapes=[dma((6,))],
        compiler_params=pltpu.CompilerParams(vmem_limit_bytes=1024 * 1024),
    )(out, small, grads)
    return (
        results[0][None, None],
        results[1],
        results[2].reshape(ch),
        results[3],
        results[4].T,
        results[5].reshape(ch),
    )


def solution(mesh):
    placed = (
        P(("group", "dp"), "tile", None, None, None),
        P(),
        P(),
        P(None, "chan"),
        P("chan", None),
        P(),
        P(("group", "dp"), "tile", None, None, None),
        P(),
    )
    return jax.shard_map(
        on_device,
        mesh=mesh,
        in_specs=placed,
        out_specs=(
            P(("group", "dp"), "tile", None, None, None),
            P("group", None),
            P("group"),
            P(("group", "dp"), "chan"),
            P(("group", "chan"), "dp"),
            P("group"),
        ),
        check_vma=False,
    )
```

```python
import functools
import math

import jax
import jax.numpy as jnp
from jax import lax
from jax.experimental import pallas as pl
from jax.experimental.pallas import tpu as pltpu
from jax.sharding import PartitionSpec as P

KS = 7
H = KS // 2
COL = 8
ROWS_AT_ONCE = 4
SMALL_ROWS = 64
SIDE_ROWS = 64
SLOT_ROWS = 2 * SIDE_ROWS
CORNER_ROWS = 16

eps = 1e-06
root_two_pi = 0.7978845608028654
cubic_coef = 0.044715
MESH = pl.DeviceIdType.MESH
F32 = jnp.float32
BF16 = jnp.bfloat16


def gelu_pair(values):
    square = values * values
    tanh_part = jnp.tanh(values * (root_two_pi + (root_two_pi * cubic_coef) * square))
    half_up = 0.5 + 0.5 * tanh_part
    active = values * half_up
    gelu_slope = half_up + active * (1.0 - tanh_part) * (
        root_two_pi + (3.0 * root_two_pi * cubic_coef) * square
    )
    return active, gelu_slope


def mm(left, right, left_dim, right_dim):
    return lax.dot_general(
        left, right, (((left_dim,), (right_dim,)), ((), ())), preferred_element_type=F32
    )


def slot_source(adj, owner, reader, core, slot, ts, span, side_rows):
    strip = H * ts
    lower = core == 1
    edge_k, first_k, second_k = 2 * core, 4 + core, 7 - core
    near_turn = 2 - 2 * core

    def edge(face, flipped, depth, along):
        return face * strip + depth * ts + jnp.where(flipped, ts - 1 - along, along)

    def corner(face, depth, along):
        return face * strip + depth * ts + jnp.where(face < 2, along, ts - 1 - along)

    face = (adj[reader, 1, edge_k] + near_turn) % 4
    row_edge = edge(face, (core == 0) == (face < 2), slot // ts, slot % ts)
    is_row = adj[reader, 0, edge_k] == owner

    within = slot % side_rows
    depth = jnp.where(within >= span, 1, 0) + jnp.where(within >= 2 * span, 1, 0)
    along = within - depth * span + core * (ts - span)
    east = (adj[reader, 1, 1] + 3) % 4
    west = (adj[reader, 1, 3] + 1) % 4
    on_east = slot < side_rows
    side = jnp.where(on_east, edge(east, east < 2, depth, along), edge(west, west >= 2, depth, along))
    east_here, west_here = adj[reader, 0, 1] == owner, adj[reader, 0, 3] == owner
    side_ok = (within < H * span) & ((on_east & east_here) | ((slot >= side_rows) & west_here))

    spot = slot % CORNER_ROWS
    i = jnp.where(spot >= H, 1, 0) + jnp.where(spot >= 2 * H, 1, 0)
    j = spot - H * i
    into = jnp.where(lower, i, H - 1 - i)
    face_a = (adj[reader, 1, first_k] + near_turn) % 4
    face_b = (adj[reader, 1, second_k] + near_turn) % 4
    on_a = slot < CORNER_ROWS
    piece = jnp.where(
        on_a,
        corner(face_a, into, jnp.where(lower, j, ts - 1 - j)),
        corner(face_b, into, jnp.where(lower, ts - H + j, H - 1 - j)),
    )
    a_here, b_here = adj[reader, 0, first_k] == owner, adj[reader, 0, second_k] == owner
    piece_ok = (spot < H * H) & ((on_a & a_here) | ((slot >= CORNER_ROWS) & (slot < 2 * CORNER_ROWS) & b_here))

    found = jnp.where(side_ok, side, jnp.where(piece_ok & ~(east_here | west_here), piece, -1))
    return jnp.where(is_row, jnp.where(slot < strip, row_edge, -1), found)


def body(
    tiles, dps, factor,
    adj_hbm, x_hbm, ct_hbm, kern_hbm, gain_hbm, w_in_ref, w_out_ref, scale_hbm,
    out_ref, small_out, w_out_all,
    adj, kern, gain_ref, scale_ref, x_ref, ct_ref, pad, faces, sel, sel_t, face_slots, halo, side_tmp, corner_tmp,
    win, wout, conv_ref, part, chan_send, chan_recv, cg, cpad, vert, stage, rim_slots, rims,
    piece_send, piece_recv, piece_all, kacc, small_mine, small_sib, small_dp, small_tile, base,
    local_sem, face_send, face_recv, pair_send, pair_recv, rim_send, rim_recv,
    rs_send, rs_recv, tg_send, tg_recv, sd_send, sd_recv, st_send, st_recv,
):
    ts = x_ref.shape[0]
    channels = x_ref.shape[2]
    wide = ts + 2 * COL
    half = ts // 2
    span = half + H
    strip = H * ts
    me_t = lax.axis_index("tile")
    me_d = lax.axis_index("dp")
    me_c = lax.axis_index("chan")
    sib = 1 - me_c
    first = me_c * half
    side_first = me_c * (half - H)

    barrier = pltpu.get_barrier_semaphore()
    for o in range(1, tiles):
        pl.semaphore_signal(barrier, inc=1, device_id={"tile": lax.rem(me_t + o, tiles)}, device_id_type=MESH)
    for o in range(1, dps):
        pl.semaphore_signal(barrier, inc=1, device_id={"dp": lax.rem(me_d + o, dps)}, device_id_type=MESH)
    pl.semaphore_signal(barrier, inc=1, device_id={"chan": sib}, device_id_type=MESH)

    local = []
    for source, target in (
        (adj_hbm, adj), (x_hbm, x_ref), (kern_hbm, kern), (w_in_ref, win.at[me_c]), (w_out_ref, wout.at[me_c]),
        (ct_hbm, ct_ref), (gain_hbm, gain_ref), (scale_hbm, scale_ref),
    ):
        copy = pltpu.make_async_copy(source, target, local_sem.at[len(local)])
        copy.start()
        local.append(copy)

    dp_peers = [lax.rem(me_d + o, dps) for o in range(1, dps)]
    if tiles == 4:
        tile_peers = [lax.rem(me_t + 2, 4), 3 - me_t, me_t + 1 - 2 * lax.rem(me_t, 2)]
        tile_sources = tile_peers
    else:
        tile_peers = [lax.rem(me_t + o, tiles) for o in range(1, tiles)]
        tile_sources = [lax.rem(me_t - o + tiles, tiles) for o in range(1, tiles)]

    all_peers = [(t, d) for t in tile_peers for d in dp_peers + [me_d]] + [(me_t, d) for d in dp_peers]

    def to_peers(axis, peers, source, target, send_sems, recv_sems):
        copies = []
        for o, peer in enumerate(peers):
            copy = pltpu.make_async_remote_copy(
                src_ref=source(o, peer), dst_ref=target, send_sem=send_sems.at[o],
                recv_sem=recv_sems.at[o], device_id=axis(peer), device_id_type=MESH,
            )
            copy.start()
            copies.append(copy)
        return copies

    def to_sibling(source, target, index):
        copy = pltpu.make_async_remote_copy(
            src_ref=source, dst_ref=target, send_sem=pair_send.at[index],
            recv_sem=pair_recv.at[index], device_id={"chan": sib}, device_id_type=MESH,
        )
        copy.start()
        return copy

    def rows_loop(count, step, unroll=1):
        def wrapped(index, carry):
            step(index)
            return carry
        lax.fori_loop(0, count, wrapped, 0, unroll=unroll)

    def on_tile(peer):
        return {"tile": peer}

    def on_dp(peer):
        return {"dp": peer}

    def on_both(peer):
        return {"tile": peer[0], "dp": peer[1]}

    def zero_pad(i):
        pad[pl.ds(pl.multiple_of(i * wide, 8), wide), :] = jnp.zeros((wide, channels), F32)
    rows_loop(ts + 2 * H, zero_pad)

    local[0].wait()
    slot_down = lax.broadcasted_iota(jnp.int32, (SLOT_ROWS, 1), 0)
    face_across = lax.broadcasted_iota(jnp.int32, (SLOT_ROWS, 4 * strip), 1)
    for o, peer in enumerate(tile_peers):
        chosen = slot_source(adj, me_t, peer, me_c, slot_down, ts, span, SIDE_ROWS)
        sel[o] = jnp.where(face_across == chosen, 1.0, 0.0).astype(BF16)

    local[1].wait()

    def fill(i):
        pad[pl.ds(pl.multiple_of((H + i) * wide + COL, 8), ts), :] = x_ref[i].astype(F32)
    rows_loop(ts, fill, 8)
    for d in range(H):
        faces[d * ts:(d + 1) * ts, :] = x_ref[d]
        faces[2 * strip + d * ts:2 * strip + (d + 1) * ts, :] = x_ref[ts - 1 - d]
        for f, col in ((1, COL + ts - 1 - d), (3, COL + d)):
            column = pad[pl.ds(H * wide + col, ts, stride=wide), :]
            faces[f * strip + d * ts:f * strip + (d + 1) * ts, :] = column.astype(BF16)
    for o in range(tiles - 1):
        face_slots[o] = mm(sel[o], faces[...], 1, 0).astype(BF16)

    pl.semaphore_wait(barrier, tiles - 1 + dps - 1 + 1)
    face_copies = to_peers(on_tile, tile_peers, lambda o, peer: face_slots.at[o], halo.at[me_t], face_send, face_recv)
    win_copy = to_sibling(w_in_ref, win.at[me_c], 0)
    wout_copy = to_sibling(w_out_ref, wout.at[me_c], 1)

    halo[me_t] = jnp.zeros((SLOT_ROWS, channels), BF16)
    local[2].wait()

    def conv_rows(block):
        i = block * ROWS_AT_ONCE
        acc = [jnp.zeros((ts, channels), F32) for _ in range(ROWS_AT_ONCE)]
        for a in range(ROWS_AT_ONCE + KS - 1):
            for b in range(KS):
                window = pad[pl.ds((first + i + a) * wide + COL - H + b, ts), :]
                for r in range(ROWS_AT_ONCE):
                    if 0 <= a - r < KS:
                        at = (a - r) * KS + b
                        acc[r] = acc[r] + window * kern[at:at + 1, :]
        for r in range(ROWS_AT_ONCE):
            conv_ref[pl.ds(pl.multiple_of((i + r) * ts, 8), ts), :] = acc[r]
    rows_loop(half // ROWS_AT_ONCE, conv_rows)

    def zero_rows(i):
        cpad[pl.ds(pl.multiple_of(i * wide, 8), wide), :] = jnp.zeros((wide, channels), F32)
    rows_loop(cpad.shape[0] // wide, zero_rows)
    kacc[...] = jnp.zeros_like(kacc)
    slot_across = lax.broadcasted_iota(jnp.int32, (1, strip), 1)
    face_down = lax.broadcasted_iota(jnp.int32, (4 * strip, strip), 0)
    for core in range(2):
        for o, peer in enumerate(tile_sources):
            chosen = slot_source(adj, me_t, peer, core, slot_across, ts, half, strip // 2)
            sel_t[core, o] = jnp.where(face_down == chosen, 1.0, 0.0).astype(BF16)

    for copy in face_copies:
        copy.wait_recv()
    side_tmp[0] = halo[adj[me_t, 0, 1], :SIDE_ROWS].astype(F32)
    side_tmp[1] = halo[adj[me_t, 0, 3], SIDE_ROWS:].astype(F32)
    corner_tmp[0] = halo[adj[me_t, 0, 4 + me_c], :CORNER_ROWS].astype(F32)
    corner_tmp[1] = halo[adj[me_t, 0, 7 - me_c], CORNER_ROWS:2 * CORNER_ROWS].astype(F32)
    row_strip = halo[adj[me_t, 0, 2 * me_c], :strip].astype(F32)
    side_row = (H + side_first) * wide
    for d in range(H):
        pad[pl.ds(side_row + COL + ts + d, span, stride=wide), :] = side_tmp[0, d * span:(d + 1) * span, :]
        pad[pl.ds(side_row + COL - 1 - d, span, stride=wide), :] = side_tmp[1, d * span:(d + 1) * span, :]

    west_fix = [jnp.zeros((half, channels), F32) for _ in range(H)]
    east_fix = [jnp.zeros((half, channels), F32) for _ in range(H)]
    for a in range(KS):
        for e in range(H):
            west = pad[pl.ds((first + a) * wide + COL - H + e, half, stride=wide), :]
            east = pad[pl.ds((first + a) * wide + COL + ts + e, half, stride=wide), :]
            for m in range(H):
                if m <= e:
                    at = a * KS + e - m
                    west_fix[m] = west_fix[m] + west * kern[at:at + 1, :]
                if e + m < H:
                    at = a * KS + H + 1 + e + m
                    east_fix[m] = east_fix[m] + east * kern[at:at + 1, :]
    for m in range(H):
        conv_ref[pl.ds(m, half, stride=ts), :] += west_fix[m]
        conv_ref[pl.ds(ts - 1 - m, half, stride=ts), :] += east_fix[m]

    for d in range(H):
        row = H - 1 - d + me_c * (ts + 1 + 2 * d)
        pad[pl.ds(pl.multiple_of(row * wide + COL, 8), ts), :] = row_strip[d * ts:(d + 1) * ts]
    for i in range(H):
        row = i + me_c * (ts + H)
        pad[pl.ds(row * wide + COL + ts, H), :] = corner_tmp[0, H * i:H * (i + 1), :]
        pad[pl.ds(row * wide + COL - H, H), :] = corner_tmp[1, H * i:H * (i + 1), :]
    row_fix = [jnp.zeros((ts, channels), F32) for _ in range(H)]
    for h in range(H):
        for b in range(KS):
            window = pad[pl.ds((h + me_c * (ts + 2 * H - 1 - 2 * h)) * wide + COL - H + b, ts), :]
            for i in range(h + 1):
                a = h - i + me_c * (KS - 1 - 2 * (h - i))
                row_fix[i] = row_fix[i] + window * kern[pl.ds(a * KS + b, 1), :]
    for i in range(H):
        conv_ref[pl.ds(pl.multiple_of((i + me_c * (half - 1 - 2 * i)) * ts, 8), ts), :] += row_fix[i]

    win_copy.wait_recv()
    wout_copy.wait_recv()
    for copy in local[3:]:
        copy.wait()

    gain = gain_ref[...]
    layer_scale = scale_ref[...]
    block_rows = 8
    pixels = block_rows * ts
    gain_total = jnp.zeros((1, channels), F32)
    scale_total = jnp.zeros((1, channels), F32)
    blocks = []
    for block in range(half // block_rows):
        at = block * block_rows
        conv = conv_ref[at * ts:(at + block_rows) * ts, :]
        mean = jnp.mean(conv, axis=1, keepdims=True)
        centred = conv - mean
        inv_std = lax.rsqrt(jnp.mean(centred * centred, axis=1, keepdims=True) + eps)
        normed = centred * inv_std
        normed_b = (normed * gain).astype(BF16)
        upstream = ct_ref[pl.ds(first + at, block_rows)].reshape(pixels, channels).astype(F32)
        scaled_b = (upstream * layer_scale).astype(BF16)
        blocks.append([inv_std, normed, normed_b, upstream, scaled_b, 0.0, 0.0])
    part_rows = channels // dps
    part_copy = None
    for c in (sib, me_c):
        grads = [0.0, 0.0]
        for state in blocks:
            inv_std, normed, normed_b, upstream, scaled_b, branch, normed_grad = state
            active, slope = gelu_pair(mm(normed_b, win[c], 1, 0))
            active_b = active.astype(BF16)
            state[5] = branch + mm(active_b, wout[c], 1, 0)
            hidden_grad = (mm(scaled_b, wout[c], 1, 1) * slope).astype(BF16)
            state[6] = normed_grad + mm(hidden_grad, win[c], 1, 1)
            grads[0] = grads[0] + mm(normed_b, hidden_grad, 0, 0)
            grads[1] = grads[1] + mm(scaled_b, active_b, 0, 0)
        for w in range(2):
            if part_copy is None:
                chan_send[w] = grads[w].astype(BF16)
            else:
                part[w] = grads[w]
        if part_copy is None:
            part_copy = to_sibling(chan_send, chan_recv, 2)
    for block, (inv_std, normed, normed_b, upstream, scaled_b, branch, normed_grad) in enumerate(blocks):
        at = block * block_rows
        scaled = normed_grad * gain
        first_mean = jnp.mean(scaled, axis=1, keepdims=True)
        second_mean = jnp.mean(scaled * normed, axis=1, keepdims=True)
        grad_b = (inv_std * (scaled - first_mean - normed * second_mean)).astype(BF16)
        cg[pl.ds(first + at, block_rows)] = grad_b.reshape(block_rows, ts, channels)
        scale_total = scale_total + jnp.sum(upstream * branch, axis=0, keepdims=True)
        gain_total = gain_total + jnp.sum(normed_grad * normed, axis=0, keepdims=True)
    cg_copy = to_sibling(cg.at[pl.ds(first, half)], cg.at[pl.ds(first, half)], 3)

    def widen(row):
        cpad[pl.ds(pl.multiple_of((KS - 1 + row) * wide + COL, 8), ts), :] = cg[row].astype(F32)
    rows_loop(half, lambda i: widen(first + i), 4)

    def kernel_taps(start, stop):
        for a in range(start, stop):
            def kernel_row(i, acc):
                grad = cpad[pl.ds(pl.multiple_of((KS - 1 + first + i) * wide + COL, 8), ts), :]
                new = []
                for b in range(KS):
                    window = pad[pl.ds((first + i + a) * wide + COL - H + b, ts), :]
                    new.append(acc[b] + jnp.sum((window * grad).reshape(ts // 8, 8, channels), axis=0))
                return tuple(new)
            sums = lax.fori_loop(0, half, kernel_row, tuple(jnp.zeros((8, channels), F32) for _ in range(KS)), unroll=4)
            for b in range(KS):
                kacc[a * KS + b] = sums[b]

    kernel_taps(0, 3)
    part_copy.wait_recv()
    at_once = part_rows // tiles
    for w in range(2):
        whole = (part[w] + chan_recv[w].astype(F32)).astype(BF16)
        for d in range(dps):
            for t in range(tiles):
                at = d * part_rows + t * at_once
                piece_send[t, d, w * at_once:(w + 1) * at_once] = whole[at:at + at_once]
    piece_recv[me_t, me_d] = piece_send[me_t, me_d]
    rs_copies = to_peers(
        on_both, all_peers, lambda o, peer: piece_send.at[peer[0], peer[1]], piece_recv.at[me_t, me_d], rs_send, rs_recv
    )
    kernel_taps(3, KS)
    taps = KS * KS
    kacc[taps, 0:1, :] = gain_total
    kacc[taps + 1, 0:1, :] = scale_total
    small_mine[...] = jnp.sum(kacc[...], axis=1)
    small_copy = to_sibling(small_mine, small_sib, 4)

    cg_copy.wait_recv()
    rows_loop(half, lambda i: widen(sib * half + i), 4)

    across = ts + 8
    for h in range(H):
        acc = jnp.zeros((across, channels), F32)
        for i in range(h + 1):
            row = KS - 1 + i + me_c * (ts - 1 - 2 * i)
            a = h - i + me_c * (KS - 1 - 2 * (h - i))
            for b in range(KS):
                acc = acc + cpad[pl.ds(row * wide + COL - b, across), :] * kern[pl.ds(a * KS + b, 1), :]
        vert[h * across:(h + 1) * across, :] = acc
    west_rim = [jnp.zeros((half, channels), F32) for _ in range(H)]
    east_rim = [jnp.zeros((half, channels), F32) for _ in range(H)]
    for a in range(KS):
        row = (KS - 1 + H + first - a) * wide
        for j in range(H):
            west = cpad[pl.ds(row + COL + j, half, stride=wide), :]
            east = cpad[pl.ds(row + COL + ts - 1 - j, half, stride=wide), :]
            for d in range(H):
                if j <= H - 1 - d:
                    at = a * KS + H - 1 - d - j
                    west_rim[d] = west_rim[d] + west * kern[at:at + 1, :]
                    at = a * KS + H + 1 + d + j
                    east_rim[d] = east_rim[d] + east * kern[at:at + 1, :]
    for s in range(2):
        corner_tmp[s] = jnp.zeros((CORNER_ROWS, channels), F32)
    for d in range(H):
        stage[1, d * half:(d + 1) * half, :] = east_rim[d].astype(BF16)
        stage[1, (H + d) * half:(H + d + 1) * half, :] = west_rim[d].astype(BF16)
    for i in range(H):
        row = (i + me_c * (H - 1 - 2 * i)) * across
        corner_tmp[0, H * i:H * (i + 1), :] = vert[pl.ds(row + H + ts, H), :]
        corner_tmp[1, H * i:H * (i + 1), :] = vert[pl.ds(row, H), :]
    for h in range(H):
        d = H - 1 - h
        stage[0, d * ts:(d + 1) * ts, :] = vert[h * across + H:h * across + H + ts, :].astype(BF16)
    stage[2, 2 * CORNER_ROWS:, :] = jnp.zeros((strip - 2 * CORNER_ROWS, channels), BF16)
    for s in range(2):
        stage[2, s * CORNER_ROWS:(s + 1) * CORNER_ROWS, :] = corner_tmp[s].astype(BF16)
    for o, peer in enumerate(tile_peers):
        beside = (adj[me_t, 0, 1] == peer) | (adj[me_t, 0, 3] == peer)
        kind = jnp.where(adj[me_t, 0, 2 * me_c] == peer, 0, jnp.where(beside, 1, 2))
        rim_slots[o] = stage[kind]
    rim_copies = to_peers(on_tile, tile_peers, lambda o, peer: rim_slots.at[o], rims.at[me_c, me_t], rim_send, rim_recv)

    small_copy.wait_recv()
    small_dp[me_d] = (small_mine[...] + small_sib[...]).astype(BF16)
    sd_copies = to_peers(on_dp, dp_peers, lambda o, peer: small_dp.at[me_d], small_dp.at[me_d], sd_send, sd_recv)

    def spread_rows(block):
        i = block * ROWS_AT_ONCE
        acc = [ct_ref[i + r].astype(F32) for r in range(ROWS_AT_ONCE)]
        for up in range(ROWS_AT_ONCE + KS - 1):
            for b in range(KS):
                window = cpad[pl.ds((i + H + up) * wide + COL + H - b, ts), :]
                for r in range(ROWS_AT_ONCE):
                    a = KS - 1 + r - up
                    if 0 <= a < KS:
                        acc[r] = acc[r] + window * kern[a * KS + b:a * KS + b + 1, :]
        for r in range(ROWS_AT_ONCE):
            base[pl.ds(pl.multiple_of((i + r) * ts, 8), ts), :] = acc[r]
    spread_blocks = ts // ROWS_AT_ONCE

    def spread_part(start, stop):
        rows_loop((stop - start) * spread_blocks // 8, lambda block: spread_rows(block + start * spread_blocks // 8))

    spread_part(0, 6)
    for copy in sd_copies:
        copy.wait_recv()
    total = small_dp[0].astype(F32)
    for d in range(1, dps):
        total = total + small_dp[d].astype(F32)
    small_tile[me_t] = total.astype(BF16)
    st_copies = to_peers(on_tile, tile_peers, lambda o, peer: small_tile.at[me_t], small_tile.at[me_t], st_send, st_recv)
    spread_part(6, 8)

    for copy in rs_copies:
        copy.wait_recv()
    total = jnp.zeros((2 * at_once, win.shape[2]), F32)
    for t in range(tiles):
        for d in range(dps):
            total = total + piece_recv[t, d].astype(F32)
    piece_all[me_t] = (total * factor).astype(BF16)
    tg_copies = to_peers(on_tile, tile_peers, lambda o, peer: piece_all.at[me_t], piece_all.at[me_t], tg_send, tg_recv)

    rim_passes = []
    for o, source in enumerate(tile_sources):
        rim_copies[o].wait_recv()
        rim_passes.append(to_sibling(rims.at[me_c, source], rims.at[me_c, source], 5 + o))

    def taken_back(core):
        found = jnp.zeros((4 * strip, channels), F32)
        for o, peer in enumerate(tile_sources):
            found = found + mm(sel_t[core, o], rims[core, peer], 1, 0)
        return found

    from_mine = taken_back(me_c)
    for copy in rim_passes:
        copy.wait_recv()
    incoming = from_mine + taken_back(sib)
    for d in range(H):
        part_of = [incoming[f * strip + d * ts:f * strip + (d + 1) * ts] for f in range(4)]
        base[d * ts:(d + 1) * ts, :] += part_of[0]
        base[(ts - 1 - d) * ts:(ts - d) * ts, :] += part_of[2]
        base[pl.ds(ts - 1 - d, ts, stride=ts), :] += part_of[1]
        base[pl.ds(d, ts, stride=ts), :] += part_of[3]

    def out_row(i):
        out_ref[i] = base[pl.ds(pl.multiple_of(i * ts, 8), ts), :].astype(BF16)
    rows_loop(ts, out_row, 4)

    for copy in st_copies:
        copy.wait_recv()
    total = small_tile[0].astype(F32)
    for t in range(1, tiles):
        total = total + small_tile[t].astype(F32)
    small_out[...] = total * factor
    for copy in tg_copies:
        copy.wait_recv()
    for w in range(2):
        for t in range(tiles):
            at = w * part_rows + t * at_once
            w_out_all[at:at + at_once, :] = piece_all[t, w * at_once:(w + 1) * at_once].astype(F32)

    for copy in face_copies + rim_copies + rim_passes + rs_copies + sd_copies + tg_copies + st_copies + [
        win_copy, wout_copy, cg_copy, part_copy, small_copy
    ]:
        copy.wait_send()


def write_out(out, small, grads, out_hbm, kernel_hbm, gain_hbm, w_in_hbm, w_out_hbm, scale_hbm, sems):
    taps = KS * KS
    rows = w_in_hbm.shape[0]
    pairs = (
        (out, out_hbm),
        (grads.at[:rows], w_in_hbm),
        (grads.at[rows:], w_out_hbm),
        (small.at[:taps], kernel_hbm),
        (small.at[taps:taps + 1], gain_hbm),
        (small.at[taps + 1:taps + 2], scale_hbm),
    )
    copies = [pltpu.make_async_copy(source, target, sems.at[i]) for i, (source, target) in enumerate(pairs)]
    for copy in copies:
        copy.start()
    for copy in copies:
        copy.wait()


def in_hbm(array):
    return pltpu.with_memory_space_constraint(array, pltpu.MemorySpace.HBM)


def on_device(inputs, kernel, norm_gain, w_in, w_out, layer_scale, cotangent, adjacency):
    ts, ch = inputs.shape[2], inputs.shape[4]
    hid = w_in.shape[1]
    tiles, dps = lax.axis_size("tile"), lax.axis_size("dp")
    factor = 1.0 / math.sqrt(dps * tiles * ts * ts)
    strip = H * ts
    wide = ts + 2 * COL
    part_rows = ch // dps
    vmem = pl.BlockSpec(memory_space=pltpu.VMEM)
    hbm = pl.BlockSpec(memory_space=pltpu.MemorySpace.HBM)
    dma = pltpu.SemaphoreType.DMA
    peers_t, peers_d = max(tiles - 1, 1), max(dps - 1, 1)
    pairs = 5 + peers_t
    out, small, grads = pl.pallas_call(
        functools.partial(body, tiles, dps, factor),
        out_shape=(
            jax.ShapeDtypeStruct((ts, ts, ch), BF16),
            jax.ShapeDtypeStruct((SMALL_ROWS, ch), F32),
            jax.ShapeDtypeStruct((2 * part_rows, hid), F32),
        ),
        in_specs=[hbm] * 8,
        out_specs=(vmem,) * 3,
        scratch_shapes=[
            pltpu.SMEM((tiles, 2, 8), jnp.int32),
            pltpu.VMEM((KS * KS, ch), F32),
            pltpu.VMEM((1, ch), F32),
            pltpu.VMEM((1, ch), F32),
            pltpu.VMEM((ts, ts, ch), BF16),
            pltpu.VMEM((ts, ts, ch), BF16),
            pltpu.VMEM(((ts + 2 * H) * wide, ch), F32),
            pltpu.VMEM((4 * strip, ch), BF16),
            pltpu.VMEM((peers_t, SLOT_ROWS, 4 * strip), BF16),
            pltpu.VMEM((2, peers_t, 4 * strip, strip), BF16),
            pltpu.VMEM((peers_t, SLOT_ROWS, ch), BF16),
            pltpu.VMEM((tiles, SLOT_ROWS, ch), BF16),
            pltpu.VMEM((2, SIDE_ROWS, ch), F32),
            pltpu.VMEM((2, CORNER_ROWS, ch), F32),
            pltpu.VMEM((2, ch, hid), BF16),
            pltpu.VMEM((2, hid, ch), BF16),
            pltpu.VMEM((ts // 2 * ts, ch), F32),
            pltpu.VMEM((2, ch, hid), F32),
            pltpu.VMEM((2, ch, hid), BF16),
            pltpu.VMEM((2, ch, hid), BF16),
            pltpu.VMEM((ts, ts, ch), BF16),
            pltpu.VMEM(((ts + 2 * KS) * wide, ch), F32),
            pltpu.VMEM((H * (ts + 8), ch), F32),
            pltpu.VMEM((3, strip, ch), BF16),
            pltpu.VMEM((peers_t, strip, ch), BF16),
            pltpu.VMEM((2, tiles, strip, ch), BF16),
            pltpu.VMEM((tiles, dps, 2 * part_rows // tiles, hid), BF16),
            pltpu.VMEM((tiles, dps, 2 * part_rows // tiles, hid), BF16),
            pltpu.VMEM((tiles, 2 * part_rows // tiles, hid), BF16),
            pltpu.VMEM((SMALL_ROWS, 8, ch), F32),
            pltpu.VMEM((SMALL_ROWS, ch), F32),
            pltpu.VMEM((SMALL_ROWS, ch), F32),
            pltpu.VMEM((dps, SMALL_ROWS, ch), BF16),
            pltpu.VMEM((tiles, SMALL_ROWS, ch), BF16),
            pltpu.VMEM((ts * ts, ch), F32),
            dma((8,)),
            dma((peers_t,)), dma((peers_t,)), dma((pairs,)), dma((pairs,)), dma((peers_t,)), dma((peers_t,)),
            dma((tiles * dps,)), dma((tiles * dps,)), dma((peers_t,)), dma((peers_t,)),
            dma((peers_d,)), dma((peers_d,)), dma((peers_t,)), dma((peers_t,)),
        ],
        compiler_params=pltpu.CompilerParams(
            collective_id=0, has_side_effects=True, vmem_limit_bytes=48 * 1024 * 1024
        ),
    )(
        in_hbm(jnp.transpose(adjacency, (0, 2, 1))), in_hbm(inputs[0, 0]), in_hbm(cotangent[0, 0]), in_hbm(kernel),
        in_hbm(norm_gain[None]), in_hbm(w_in), in_hbm(w_out), in_hbm(layer_scale[None]),
    )
    results = pl.pallas_call(
        write_out,
        out_shape=(
            jax.ShapeDtypeStruct((ts, ts, ch), BF16),
            jax.ShapeDtypeStruct((KS * KS, ch), F32),
            jax.ShapeDtypeStruct((1, ch), F32),
            jax.ShapeDtypeStruct((part_rows, hid), F32),
            jax.ShapeDtypeStruct((part_rows, hid), F32),
            jax.ShapeDtypeStruct((1, ch), F32),
        ),
        in_specs=[pl.BlockSpec(memory_space=pl.ANY)] * 3,
        out_specs=(hbm,) * 6,
        scratch_shapes=[dma((6,))],
        compiler_params=pltpu.CompilerParams(vmem_limit_bytes=1024 * 1024),
    )(out, small, grads)
    return (
        results[0][None, None],
        results[1],
        results[2].reshape(ch),
        results[3],
        results[4].T,
        results[5].reshape(ch),
    )


def solution(mesh):
    placed = (
        P(("group", "dp"), "tile", None, None, None),
        P(),
        P(),
        P(None, "chan"),
        P("chan", None),
        P(),
        P(("group", "dp"), "tile", None, None, None),
        P(),
    )
    return jax.shard_map(
        on_device,
        mesh=mesh,
        in_specs=placed,
        out_specs=(
            P(("group", "dp"), "tile", None, None, None),
            P("group", None),
            P("group"),
            P(("group", "dp"), "chan"),
            P(("group", "chan"), "dp"),
            P("group"),
        ),
        check_vma=False,
    )
```

```python
import functools
import math

import jax
import jax.numpy as jnp
from jax import lax
from jax.experimental import pallas as pl
from jax.experimental.pallas import tpu as pltpu
from jax.sharding import PartitionSpec as P

KS = 7
H = KS // 2
COL = 8
ROWS_AT_ONCE = 4
SMALL_ROWS = 64
SIDE_ROWS = 64
SLOT_ROWS = 2 * SIDE_ROWS
CORNER_ROWS = 16

eps = 1e-06
root_two_pi = 0.7978845608028654
cubic_coef = 0.044715
MESH = pl.DeviceIdType.MESH
F32 = jnp.float32
BF16 = jnp.bfloat16


def gelu_pair(values):
    square = values * values
    tanh_part = jnp.tanh(values * (root_two_pi + (root_two_pi * cubic_coef) * square))
    half_up = 0.5 + 0.5 * tanh_part
    active = values * half_up
    gelu_slope = half_up + active * (1.0 - tanh_part) * (
        root_two_pi + (3.0 * root_two_pi * cubic_coef) * square
    )
    return active, gelu_slope


def mm(left, right, left_dim, right_dim):
    return lax.dot_general(
        left, right, (((left_dim,), (right_dim,)), ((), ())), preferred_element_type=F32
    )


def slot_source(adj, owner, reader, core, slot, ts, span, side_rows):
    strip = H * ts
    lower = core == 1
    edge_k, first_k, second_k = 2 * core, 4 + core, 7 - core
    near_turn = 2 - 2 * core

    def edge(face, flipped, depth, along):
        return face * strip + depth * ts + jnp.where(flipped, ts - 1 - along, along)

    def corner(face, depth, along):
        return face * strip + depth * ts + jnp.where(face < 2, along, ts - 1 - along)

    face = (adj[reader, 1, edge_k] + near_turn) % 4
    row_edge = edge(face, (core == 0) == (face < 2), slot // ts, slot % ts)
    is_row = adj[reader, 0, edge_k] == owner

    within = slot % side_rows
    depth = jnp.where(within >= span, 1, 0) + jnp.where(within >= 2 * span, 1, 0)
    along = within - depth * span + core * (ts - span)
    east = (adj[reader, 1, 1] + 3) % 4
    west = (adj[reader, 1, 3] + 1) % 4
    on_east = slot < side_rows
    side = jnp.where(on_east, edge(east, east < 2, depth, along), edge(west, west >= 2, depth, along))
    east_here, west_here = adj[reader, 0, 1] == owner, adj[reader, 0, 3] == owner
    side_ok = (within < H * span) & ((on_east & east_here) | ((slot >= side_rows) & west_here))

    spot = slot % CORNER_ROWS
    i = jnp.where(spot >= H, 1, 0) + jnp.where(spot >= 2 * H, 1, 0)
    j = spot - H * i
    into = jnp.where(lower, i, H - 1 - i)
    face_a = (adj[reader, 1, first_k] + near_turn) % 4
    face_b = (adj[reader, 1, second_k] + near_turn) % 4
    on_a = slot < CORNER_ROWS
    piece = jnp.where(
        on_a,
        corner(face_a, into, jnp.where(lower, j, ts - 1 - j)),
        corner(face_b, into, jnp.where(lower, ts - H + j, H - 1 - j)),
    )
    a_here, b_here = adj[reader, 0, first_k] == owner, adj[reader, 0, second_k] == owner
    piece_ok = (spot < H * H) & ((on_a & a_here) | ((slot >= CORNER_ROWS) & (slot < 2 * CORNER_ROWS) & b_here))

    found = jnp.where(side_ok, side, jnp.where(piece_ok & ~(east_here | west_here), piece, -1))
    return jnp.where(is_row, jnp.where(slot < strip, row_edge, -1), found)


def body(
    tiles, dps, factor,
    adj_hbm, x_hbm, ct_hbm, kern_hbm, gain_hbm, w_in_ref, w_out_ref, scale_hbm,
    out_ref, small_out, w_out_all,
    adj, kern, gain_ref, scale_ref, x_ref, ct_ref, pad, faces, sel, sel_t, face_slots, halo, side_tmp, corner_tmp,
    win, wout, conv_ref, part, chan_send, chan_recv, cg, cpad, vert, stage, rim_slots, rims,
    piece_send, piece_recv, piece_all, kacc, small_mine, small_sib, small_dp, small_tile, small_done, base,
    local_sem, face_send, face_recv, pair_send, pair_recv, rim_send, rim_recv,
    rs_send, rs_recv, tg_send, tg_recv, sd_send, sd_recv, st_send, st_recv,
):
    ts = x_ref.shape[0]
    channels = x_ref.shape[2]
    wide = ts + 2 * COL
    half = ts // 2
    span = half + H
    strip = H * ts
    me_t = lax.axis_index("tile")
    me_d = lax.axis_index("dp")
    me_c = lax.axis_index("chan")
    sib = 1 - me_c
    first = me_c * half
    side_first = me_c * (half - H)

    barrier = pltpu.get_barrier_semaphore()
    for o in range(1, tiles):
        pl.semaphore_signal(barrier, inc=1, device_id={"tile": lax.rem(me_t + o, tiles)}, device_id_type=MESH)
    for o in range(1, dps):
        pl.semaphore_signal(barrier, inc=1, device_id={"dp": lax.rem(me_d + o, dps)}, device_id_type=MESH)
    pl.semaphore_signal(barrier, inc=1, device_id={"chan": sib}, device_id_type=MESH)

    local = []
    for source, target in (
        (adj_hbm, adj), (x_hbm, x_ref), (kern_hbm, kern), (w_in_ref, win.at[me_c]), (w_out_ref, wout.at[me_c]),
        (ct_hbm, ct_ref), (gain_hbm, gain_ref), (scale_hbm, scale_ref),
    ):
        copy = pltpu.make_async_copy(source, target, local_sem.at[len(local)])
        copy.start()
        local.append(copy)

    dp_peers = [lax.rem(me_d + o, dps) for o in range(1, dps)]
    if tiles == 4:
        tile_peers = [lax.rem(me_t + 2, 4), 3 - me_t, me_t + 1 - 2 * lax.rem(me_t, 2)]
        tile_sources = tile_peers
    else:
        tile_peers = [lax.rem(me_t + o, tiles) for o in range(1, tiles)]
        tile_sources = [lax.rem(me_t - o + tiles, tiles) for o in range(1, tiles)]

    all_peers = [(t, d) for t in tile_peers for d in dp_peers + [me_d]] + [(me_t, d) for d in dp_peers]

    def to_peers(axis, peers, source, target, send_sems, recv_sems):
        copies = []
        for o, peer in enumerate(peers):
            copy = pltpu.make_async_remote_copy(
                src_ref=source(o, peer), dst_ref=target, send_sem=send_sems.at[o],
                recv_sem=recv_sems.at[o], device_id=axis(peer), device_id_type=MESH,
            )
            copy.start()
            copies.append(copy)
        return copies

    def to_sibling(source, target, index):
        copy = pltpu.make_async_remote_copy(
            src_ref=source, dst_ref=target, send_sem=pair_send.at[index],
            recv_sem=pair_recv.at[index], device_id={"chan": sib}, device_id_type=MESH,
        )
        copy.start()
        return copy

    def rows_loop(count, step, unroll=1):
        def wrapped(index, carry):
            step(index)
            return carry
        lax.fori_loop(0, count, wrapped, 0, unroll=unroll)

    def on_tile(peer):
        return {"tile": peer}

    def on_dp(peer):
        return {"dp": peer}

    def on_both(peer):
        return {"tile": peer[0], "dp": peer[1]}

    def zero_pad(i):
        pad[pl.ds(pl.multiple_of(i * wide, 8), wide), :] = jnp.zeros((wide, channels), F32)
    rows_loop(ts + 2 * H, zero_pad)

    local[0].wait()
    slot_down = lax.broadcasted_iota(jnp.int32, (SLOT_ROWS, 1), 0)
    face_across = lax.broadcasted_iota(jnp.int32, (SLOT_ROWS, 4 * strip), 1)
    for o, peer in enumerate(tile_peers):
        chosen = slot_source(adj, me_t, peer, me_c, slot_down, ts, span, SIDE_ROWS)
        sel[o * SLOT_ROWS:(o + 1) * SLOT_ROWS] = jnp.where(face_across == chosen, 1.0, 0.0).astype(BF16)

    local[1].wait()

    def fill(i):
        pad[pl.ds(pl.multiple_of((H + i) * wide + COL, 8), ts), :] = x_ref[i].astype(F32)
    rows_loop(ts, fill, 8)
    for d in range(H):
        faces[d * ts:(d + 1) * ts, :] = x_ref[d]
        faces[2 * strip + d * ts:2 * strip + (d + 1) * ts, :] = x_ref[ts - 1 - d]
        for f, col in ((1, COL + ts - 1 - d), (3, COL + d)):
            column = pad[pl.ds(H * wide + col, ts, stride=wide), :]
            faces[f * strip + d * ts:f * strip + (d + 1) * ts, :] = column.astype(BF16)
    face_slots[...] = mm(sel[...], faces[...], 1, 0).astype(BF16)

    pl.semaphore_wait(barrier, tiles - 1 + dps - 1 + 1)
    face_copies = to_peers(on_tile, tile_peers, lambda o, peer: face_slots.at[pl.ds(o * SLOT_ROWS, SLOT_ROWS)], halo.at[me_t], face_send, face_recv)
    win_copy = to_sibling(w_in_ref, win.at[me_c], 0)
    wout_copy = to_sibling(w_out_ref, wout.at[me_c], 1)

    halo[me_t] = jnp.zeros((SLOT_ROWS, channels), BF16)
    local[2].wait()

    def conv_rows(block):
        i = block * ROWS_AT_ONCE
        acc = [jnp.zeros((ts, channels), F32) for _ in range(ROWS_AT_ONCE)]
        for a in range(ROWS_AT_ONCE + KS - 1):
            for b in range(KS):
                window = pad[pl.ds((first + i + a) * wide + COL - H + b, ts), :]
                for r in range(ROWS_AT_ONCE):
                    if 0 <= a - r < KS:
                        at = (a - r) * KS + b
                        acc[r] = acc[r] + window * kern[at:at + 1, :]
        for r in range(ROWS_AT_ONCE):
            conv_ref[pl.ds(pl.multiple_of((i + r) * ts, 8), ts), :] = acc[r]
    rows_loop(half // ROWS_AT_ONCE, conv_rows)

    def zero_rows(i):
        cpad[pl.ds(pl.multiple_of(i * wide, 8), wide), :] = jnp.zeros((wide, channels), F32)
    rows_loop(cpad.shape[0] // wide, zero_rows)
    kacc[...] = jnp.zeros_like(kacc)
    lane = lax.broadcasted_iota(jnp.int32, (1, (tiles - 1) * strip), 1)
    face_down = lax.broadcasted_iota(jnp.int32, (4 * strip, (tiles - 1) * strip), 0)
    for core in range(2):
        chosen = jnp.full(lane.shape, -1, jnp.int32)
        for o, peer in enumerate(tile_sources):
            at = lane - o * strip
            here = slot_source(adj, me_t, peer, core, jnp.clip(at, 0, strip - 1), ts, half, strip // 2)
            chosen = jnp.where((at >= 0) & (at < strip), here, chosen)
        sel_t[core] = jnp.where(face_down == chosen, 1.0, 0.0).astype(BF16)

    for copy in face_copies:
        copy.wait_recv()
    side_tmp[0] = halo[adj[me_t, 0, 1], :SIDE_ROWS].astype(F32)
    side_tmp[1] = halo[adj[me_t, 0, 3], SIDE_ROWS:].astype(F32)
    corner_tmp[0] = halo[adj[me_t, 0, 4 + me_c], :CORNER_ROWS].astype(F32)
    corner_tmp[1] = halo[adj[me_t, 0, 7 - me_c], CORNER_ROWS:2 * CORNER_ROWS].astype(F32)
    row_strip = halo[adj[me_t, 0, 2 * me_c], :strip].astype(F32)
    side_row = (H + side_first) * wide
    for d in range(H):
        pad[pl.ds(side_row + COL + ts + d, span, stride=wide), :] = side_tmp[0, d * span:(d + 1) * span, :]
        pad[pl.ds(side_row + COL - 1 - d, span, stride=wide), :] = side_tmp[1, d * span:(d + 1) * span, :]

    west_fix = [jnp.zeros((half, channels), F32) for _ in range(H)]
    east_fix = [jnp.zeros((half, channels), F32) for _ in range(H)]
    for a in range(KS):
        for e in range(H):
            west = pad[pl.ds((first + a) * wide + COL - H + e, half, stride=wide), :]
            east = pad[pl.ds((first + a) * wide + COL + ts + e, half, stride=wide), :]
            for m in range(H):
                if m <= e:
                    at = a * KS + e - m
                    west_fix[m] = west_fix[m] + west * kern[at:at + 1, :]
                if e + m < H:
                    at = a * KS + H + 1 + e + m
                    east_fix[m] = east_fix[m] + east * kern[at:at + 1, :]
    for m in range(H):
        conv_ref[pl.ds(m, half, stride=ts), :] += west_fix[m]
        conv_ref[pl.ds(ts - 1 - m, half, stride=ts), :] += east_fix[m]

    for d in range(H):
        row = H - 1 - d + me_c * (ts + 1 + 2 * d)
        pad[pl.ds(pl.multiple_of(row * wide + COL, 8), ts), :] = row_strip[d * ts:(d + 1) * ts]
    for i in range(H):
        row = i + me_c * (ts + H)
        pad[pl.ds(row * wide + COL + ts, H), :] = corner_tmp[0, H * i:H * (i + 1), :]
        pad[pl.ds(row * wide + COL - H, H), :] = corner_tmp[1, H * i:H * (i + 1), :]
    row_fix = [jnp.zeros((ts, channels), F32) for _ in range(H)]
    for h in range(H):
        for b in range(KS):
            window = pad[pl.ds((h + me_c * (ts + 2 * H - 1 - 2 * h)) * wide + COL - H + b, ts), :]
            for i in range(h + 1):
                a = h - i + me_c * (KS - 1 - 2 * (h - i))
                row_fix[i] = row_fix[i] + window * kern[pl.ds(a * KS + b, 1), :]
    for i in range(H):
        conv_ref[pl.ds(pl.multiple_of((i + me_c * (half - 1 - 2 * i)) * ts, 8), ts), :] += row_fix[i]

    win_copy.wait_recv()
    wout_copy.wait_recv()
    for copy in local[3:]:
        copy.wait()

    gain = gain_ref[...]
    layer_scale = scale_ref[...]
    block_rows = 16
    pixels = block_rows * ts
    gain_total = jnp.zeros((1, channels), F32)
    scale_total = jnp.zeros((1, channels), F32)
    blocks = []
    for block in range(half // block_rows):
        at = block * block_rows
        conv = conv_ref[at * ts:(at + block_rows) * ts, :]
        mean = jnp.mean(conv, axis=1, keepdims=True)
        centred = conv - mean
        inv_std = lax.rsqrt(jnp.mean(centred * centred, axis=1, keepdims=True) + eps)
        normed = centred * inv_std
        normed_b = (normed * gain).astype(BF16)
        upstream = ct_ref[pl.ds(first + at, block_rows)].reshape(pixels, channels).astype(F32)
        scaled_b = (upstream * layer_scale).astype(BF16)
        blocks.append([inv_std, normed, normed_b, upstream, scaled_b, 0.0, 0.0])
    part_rows = channels // dps
    part_copy = None
    for c in (sib, me_c):
        grads = [0.0, 0.0]
        for state in blocks:
            inv_std, normed, normed_b, upstream, scaled_b, branch, normed_grad = state
            active, slope = gelu_pair(mm(normed_b, win[c], 1, 0))
            active_b = active.astype(BF16)
            state[5] = branch + mm(active_b, wout[c], 1, 0)
            hidden_grad = (mm(scaled_b, wout[c], 1, 1) * slope).astype(BF16)
            state[6] = normed_grad + mm(hidden_grad, win[c], 1, 1)
            grads[0] = grads[0] + mm(normed_b, hidden_grad, 0, 0)
            grads[1] = grads[1] + mm(scaled_b, active_b, 0, 0)
        for w in range(2):
            if part_copy is None:
                chan_send[w] = grads[w].astype(BF16)
            else:
                part[w] = grads[w]
        if part_copy is None:
            part_copy = to_sibling(chan_send, chan_recv, 2)
    for block, (inv_std, normed, normed_b, upstream, scaled_b, branch, normed_grad) in enumerate(blocks):
        at = block * block_rows
        scaled = normed_grad * gain
        first_mean = jnp.mean(scaled, axis=1, keepdims=True)
        second_mean = jnp.mean(scaled * normed, axis=1, keepdims=True)
        grad_b = (inv_std * (scaled - first_mean - normed * second_mean)).astype(BF16)
        cg[pl.ds(first + at, block_rows)] = grad_b.reshape(block_rows, ts, channels)
        scale_total = scale_total + jnp.sum(upstream * branch, axis=0, keepdims=True)
        gain_total = gain_total + jnp.sum(normed_grad * normed, axis=0, keepdims=True)
    cg_copy = to_sibling(cg.at[pl.ds(first, half)], cg.at[pl.ds(first, half)], 3)

    def widen(row):
        cpad[pl.ds(pl.multiple_of((KS - 1 + row) * wide + COL, 8), ts), :] = cg[row].astype(F32)
    rows_loop(half, lambda i: widen(first + i), 4)

    def kernel_taps(start, stop):
        for a in range(start, stop):
            def kernel_row(i, acc):
                grad = cpad[pl.ds(pl.multiple_of((KS - 1 + first + i) * wide + COL, 8), ts), :]
                new = []
                for b in range(KS):
                    window = pad[pl.ds((first + i + a) * wide + COL - H + b, ts), :]
                    new.append(acc[b] + jnp.sum((window * grad).reshape(ts // 8, 8, channels), axis=0))
                return tuple(new)
            sums = lax.fori_loop(0, half, kernel_row, tuple(jnp.zeros((8, channels), F32) for _ in range(KS)), unroll=4)
            for b in range(KS):
                kacc[a * KS + b] = sums[b]

    kernel_taps(0, KS)
    taps = KS * KS
    kacc[taps, 0:1, :] = gain_total
    kacc[taps + 1, 0:1, :] = scale_total
    half_small = SMALL_ROWS // 2
    for c in range(2):
        small_mine[c] = jnp.sum(kacc[c * half_small:(c + 1) * half_small], axis=1)
    small_copy = to_sibling(small_mine.at[sib], small_sib, 4)

    part_copy.wait_recv()
    at_once = part_rows // tiles
    for w in range(2):
        whole = (part[w] + chan_recv[w].astype(F32)).astype(BF16)
        for d in range(dps):
            for t in range(tiles):
                at = d * part_rows + t * at_once
                piece_send[t, d, w * at_once:(w + 1) * at_once] = whole[at:at + at_once]
    piece_recv[me_t, me_d] = piece_send[me_t, me_d]
    rs_copies = to_peers(
        on_both, all_peers, lambda o, peer: piece_send.at[peer[0], peer[1]], piece_recv.at[me_t, me_d], rs_send, rs_recv
    )

    cg_copy.wait_recv()
    rows_loop(half, lambda i: widen(sib * half + i), 4)

    small_copy.wait_recv()
    small_dp[me_d] = (small_mine[me_c] + small_sib[...]).astype(BF16)
    sd_copies = to_peers(on_dp, dp_peers, lambda o, peer: small_dp.at[me_d], small_dp.at[me_d], sd_send, sd_recv)

    across = ts + 8
    for h in range(H):
        acc = jnp.zeros((across, channels), F32)
        for i in range(h + 1):
            row = KS - 1 + i + me_c * (ts - 1 - 2 * i)
            a = h - i + me_c * (KS - 1 - 2 * (h - i))
            for b in range(KS):
                acc = acc + cpad[pl.ds(row * wide + COL - b, across), :] * kern[pl.ds(a * KS + b, 1), :]
        vert[h * across:(h + 1) * across, :] = acc
    west_rim = [jnp.zeros((half, channels), F32) for _ in range(H)]
    east_rim = [jnp.zeros((half, channels), F32) for _ in range(H)]
    for a in range(KS):
        row = (KS - 1 + H + first - a) * wide
        for j in range(H):
            west = cpad[pl.ds(row + COL + j, half, stride=wide), :]
            east = cpad[pl.ds(row + COL + ts - 1 - j, half, stride=wide), :]
            for d in range(H):
                if j <= H - 1 - d:
                    at = a * KS + H - 1 - d - j
                    west_rim[d] = west_rim[d] + west * kern[at:at + 1, :]
                    at = a * KS + H + 1 + d + j
                    east_rim[d] = east_rim[d] + east * kern[at:at + 1, :]
    for s in range(2):
        corner_tmp[s] = jnp.zeros((CORNER_ROWS, channels), F32)
    for d in range(H):
        stage[1, d * half:(d + 1) * half, :] = east_rim[d].astype(BF16)
        stage[1, (H + d) * half:(H + d + 1) * half, :] = west_rim[d].astype(BF16)
    for i in range(H):
        row = (i + me_c * (H - 1 - 2 * i)) * across
        corner_tmp[0, H * i:H * (i + 1), :] = vert[pl.ds(row + H + ts, H), :]
        corner_tmp[1, H * i:H * (i + 1), :] = vert[pl.ds(row, H), :]
    for h in range(H):
        d = H - 1 - h
        stage[0, d * ts:(d + 1) * ts, :] = vert[h * across + H:h * across + H + ts, :].astype(BF16)
    stage[2, 2 * CORNER_ROWS:, :] = jnp.zeros((strip - 2 * CORNER_ROWS, channels), BF16)
    for s in range(2):
        stage[2, s * CORNER_ROWS:(s + 1) * CORNER_ROWS, :] = corner_tmp[s].astype(BF16)
    for o, peer in enumerate(tile_peers):
        beside = (adj[me_t, 0, 1] == peer) | (adj[me_t, 0, 3] == peer)
        kind = jnp.where(adj[me_t, 0, 2 * me_c] == peer, 0, jnp.where(beside, 1, 2))
        rim_slots[o * strip:(o + 1) * strip] = stage[kind]
    rim_copies = []
    for o, peer in enumerate(tile_peers):
        slots = pl.ds(o * strip, strip)
        copy = pltpu.make_async_remote_copy(
            src_ref=rim_slots.at[slots], dst_ref=rims.at[me_c, slots], send_sem=rim_send.at[o],
            recv_sem=rim_recv.at[o], device_id={"tile": peer}, device_id_type=MESH,
        )
        copy.start()
        rim_copies.append(copy)

    def spread_rows(block):
        i = block * ROWS_AT_ONCE
        acc = [ct_ref[i + r].astype(F32) for r in range(ROWS_AT_ONCE)]
        for up in range(ROWS_AT_ONCE + KS - 1):
            for b in range(KS):
                window = cpad[pl.ds((i + H + up) * wide + COL + H - b, ts), :]
                for r in range(ROWS_AT_ONCE):
                    a = KS - 1 + r - up
                    if 0 <= a < KS:
                        acc[r] = acc[r] + window * kern[a * KS + b:a * KS + b + 1, :]
        for r in range(ROWS_AT_ONCE):
            base[pl.ds(pl.multiple_of((i + r) * ts, 8), ts), :] = acc[r]
    spread_blocks = ts // ROWS_AT_ONCE

    def spread_part(start, stop):
        rows_loop((stop - start) * spread_blocks // 8, lambda block: spread_rows(block + start * spread_blocks // 8))

    spread_part(0, 6)
    for copy in sd_copies:
        copy.wait_recv()
    total = small_dp[0].astype(F32)
    for d in range(1, dps):
        total = total + small_dp[d].astype(F32)
    small_tile[me_t] = total.astype(BF16)
    st_copies = to_peers(on_tile, tile_peers, lambda o, peer: small_tile.at[me_t], small_tile.at[me_t], st_send, st_recv)
    spread_part(6, 8)

    for copy in rs_copies:
        copy.wait_recv()
    total = jnp.zeros((2 * at_once, win.shape[2]), F32)
    for t in range(tiles):
        for d in range(dps):
            total = total + piece_recv[t, d].astype(F32)
    piece_all[me_t] = (total * factor).astype(BF16)
    tg_copies, tg_waits = [], []
    for o in range(tiles - 1):
        peer = o + jnp.where(o >= me_t, 1, 0)
        for source, target, copies in ((me_t, peer, tg_copies), (peer, peer, tg_waits)):
            copies.append(pltpu.make_async_remote_copy(
                src_ref=piece_all.at[source], dst_ref=piece_all.at[source], send_sem=tg_send.at[o],
                recv_sem=tg_recv.at[source], device_id={"tile": target}, device_id_type=MESH,
            ))
        tg_copies[o].start()

    rim_passes = []
    for o, copy in enumerate(rim_copies):
        slots = pl.ds(o * strip, strip)
        copy.wait_recv()
        rim_passes.append(to_sibling(rims.at[me_c, slots], rims.at[me_c, slots], 5 + o))
    from_mine = mm(sel_t[me_c], rims[me_c], 1, 0)

    for copy in st_copies:
        copy.wait_recv()
    total = small_tile[0].astype(F32)
    for t in range(1, tiles):
        total = total + small_tile[t].astype(F32)
    small_done[me_c] = total * factor
    done_copy = to_sibling(small_done.at[me_c], small_done.at[me_c], 4 + tiles)

    for copy in rim_passes:
        copy.wait_recv()
    incoming = from_mine + mm(sel_t[sib], rims[sib], 1, 0)
    for d in range(H):
        part_of = [incoming[f * strip + d * ts:f * strip + (d + 1) * ts] for f in range(4)]
        base[d * ts:(d + 1) * ts, :] += part_of[0]
        base[(ts - 1 - d) * ts:(ts - d) * ts, :] += part_of[2]
        base[pl.ds(ts - 1 - d, ts, stride=ts), :] += part_of[1]
        base[pl.ds(d, ts, stride=ts), :] += part_of[3]

    def out_row(i):
        out_ref[i] = base[pl.ds(pl.multiple_of(i * ts, 8), ts), :].astype(BF16)
    rows_loop(ts, out_row, 4)

    done_copy.wait_recv()
    small_out[...] = small_done[...]
    for copy in tg_waits:
        copy.wait_recv()
    for w in range(2):
        for t in range(tiles):
            at = w * part_rows + t * at_once
            w_out_all[at:at + at_once, :] = piece_all[t, w * at_once:(w + 1) * at_once].astype(F32)

    for copy in face_copies + rim_copies + rim_passes + rs_copies + sd_copies + tg_copies + st_copies + [
        win_copy, wout_copy, cg_copy, part_copy, small_copy, done_copy
    ]:
        copy.wait_send()


def write_out(out, small, grads, out_hbm, kernel_hbm, gain_hbm, w_in_hbm, w_out_hbm, scale_hbm, sems):
    taps = KS * KS
    rows = w_in_hbm.shape[0]
    pairs = (
        (out, out_hbm),
        (grads.at[:rows], w_in_hbm),
        (grads.at[rows:], w_out_hbm),
        (small.at[:taps], kernel_hbm),
        (small.at[taps:taps + 1], gain_hbm),
        (small.at[taps + 1:taps + 2], scale_hbm),
    )
    copies = [pltpu.make_async_copy(source, target, sems.at[i]) for i, (source, target) in enumerate(pairs)]
    for copy in copies:
        copy.start()
    for copy in copies:
        copy.wait()


def in_hbm(array):
    return pltpu.with_memory_space_constraint(array, pltpu.MemorySpace.HBM)


def on_device(inputs, kernel, norm_gain, w_in, w_out, layer_scale, cotangent, adjacency):
    ts, ch = inputs.shape[2], inputs.shape[4]
    hid = w_in.shape[1]
    tiles, dps = lax.axis_size("tile"), lax.axis_size("dp")
    factor = 1.0 / math.sqrt(dps * tiles * ts * ts)
    strip = H * ts
    wide = ts + 2 * COL
    part_rows = ch // dps
    vmem = pl.BlockSpec(memory_space=pltpu.VMEM)
    hbm = pl.BlockSpec(memory_space=pltpu.MemorySpace.HBM)
    dma = pltpu.SemaphoreType.DMA
    peers_t, peers_d = max(tiles - 1, 1), max(dps - 1, 1)
    pairs = 6 + peers_t
    out, small, grads = pl.pallas_call(
        functools.partial(body, tiles, dps, factor),
        out_shape=(
            jax.ShapeDtypeStruct((ts, ts, ch), BF16),
            jax.ShapeDtypeStruct((2, SMALL_ROWS // 2, ch), F32),
            jax.ShapeDtypeStruct((2 * part_rows, hid), F32),
        ),
        in_specs=[hbm] * 8,
        out_specs=(vmem,) * 3,
        scratch_shapes=[
            pltpu.SMEM((tiles, 2, 8), jnp.int32),
            pltpu.VMEM((KS * KS, ch), F32),
            pltpu.VMEM((1, ch), F32),
            pltpu.VMEM((1, ch), F32),
            pltpu.VMEM((ts, ts, ch), BF16),
            pltpu.VMEM((ts, ts, ch), BF16),
            pltpu.VMEM(((ts + 2 * H) * wide, ch), F32),
            pltpu.VMEM((4 * strip, ch), BF16),
            pltpu.VMEM((peers_t * SLOT_ROWS, 4 * strip), BF16),
            pltpu.VMEM((2, 4 * strip, peers_t * strip), BF16),
            pltpu.VMEM((peers_t * SLOT_ROWS, ch), BF16),
            pltpu.VMEM((tiles, SLOT_ROWS, ch), BF16),
            pltpu.VMEM((2, SIDE_ROWS, ch), F32),
            pltpu.VMEM((2, CORNER_ROWS, ch), F32),
            pltpu.VMEM((2, ch, hid), BF16),
            pltpu.VMEM((2, hid, ch), BF16),
            pltpu.VMEM((ts // 2 * ts, ch), F32),
            pltpu.VMEM((2, ch, hid), F32),
            pltpu.VMEM((2, ch, hid), BF16),
            pltpu.VMEM((2, ch, hid), BF16),
            pltpu.VMEM((ts, ts, ch), BF16),
            pltpu.VMEM(((ts + 2 * KS) * wide, ch), F32),
            pltpu.VMEM((H * (ts + 8), ch), F32),
            pltpu.VMEM((3, strip, ch), BF16),
            pltpu.VMEM((peers_t * strip, ch), BF16),
            pltpu.VMEM((2, peers_t * strip, ch), BF16),
            pltpu.VMEM((tiles, dps, 2 * part_rows // tiles, hid), BF16),
            pltpu.VMEM((tiles, dps, 2 * part_rows // tiles, hid), BF16),
            pltpu.VMEM((tiles, 2 * part_rows // tiles, hid), BF16),
            pltpu.VMEM((SMALL_ROWS, 8, ch), F32),
            pltpu.VMEM((2, SMALL_ROWS // 2, ch), F32),
            pltpu.VMEM((SMALL_ROWS // 2, ch), F32),
            pltpu.VMEM((dps, SMALL_ROWS // 2, ch), BF16),
            pltpu.VMEM((tiles, SMALL_ROWS // 2, ch), BF16),
            pltpu.VMEM((2, SMALL_ROWS // 2, ch), F32),
            pltpu.VMEM((ts * ts, ch), F32),
            dma((8,)),
            dma((peers_t,)), dma((peers_t,)), dma((pairs,)), dma((pairs,)), dma((peers_t,)), dma((peers_t,)),
            dma((tiles * dps,)), dma((tiles * dps,)), dma((peers_t,)), dma((tiles,)),
            dma((peers_d,)), dma((peers_d,)), dma((peers_t,)), dma((peers_t,)),
        ],
        compiler_params=pltpu.CompilerParams(
            collective_id=0, has_side_effects=True, vmem_limit_bytes=48 * 1024 * 1024
        ),
    )(
        in_hbm(jnp.transpose(adjacency, (0, 2, 1))), in_hbm(inputs[0, 0]), in_hbm(cotangent[0, 0]), in_hbm(kernel),
        in_hbm(norm_gain[None]), in_hbm(w_in), in_hbm(w_out), in_hbm(layer_scale[None]),
    )
    results = pl.pallas_call(
        write_out,
        out_shape=(
            jax.ShapeDtypeStruct((ts, ts, ch), BF16),
            jax.ShapeDtypeStruct((KS * KS, ch), F32),
            jax.ShapeDtypeStruct((1, ch), F32),
            jax.ShapeDtypeStruct((part_rows, hid), F32),
            jax.ShapeDtypeStruct((part_rows, hid), F32),
            jax.ShapeDtypeStruct((1, ch), F32),
        ),
        in_specs=[pl.BlockSpec(memory_space=pl.ANY)] * 3,
        out_specs=(hbm,) * 6,
        scratch_shapes=[dma((6,))],
        compiler_params=pltpu.CompilerParams(vmem_limit_bytes=1024 * 1024),
    )(out, small.reshape(SMALL_ROWS, ch), grads)
    return (
        results[0][None, None],
        results[1],
        results[2].reshape(ch),
        results[3],
        results[4].T,
        results[5].reshape(ch),
    )


def solution(mesh):
    placed = (
        P(("group", "dp"), "tile", None, None, None),
        P(),
        P(),
        P(None, "chan"),
        P("chan", None),
        P(),
        P(("group", "dp"), "tile", None, None, None),
        P(),
    )
    return jax.shard_map(
        on_device,
        mesh=mesh,
        in_specs=placed,
        out_specs=(
            P(("group", "dp"), "tile", None, None, None),
            P("group", None),
            P("group"),
            P(("group", "dp"), "chan"),
            P(("group", "chan"), "dp"),
            P("group"),
        ),
        check_vma=False,
    )
```

```python
import functools
import math

import jax
import jax.numpy as jnp
from jax import lax
from jax.experimental import pallas as pl
from jax.experimental.pallas import tpu as pltpu
from jax.sharding import PartitionSpec as P

KS = 7
H = KS // 2
COL = 8
ROWS_AT_ONCE = 4
SMALL_ROWS = 64
SIDE_ROWS = 64
SLOT_ROWS = 2 * SIDE_ROWS
CORNER_ROWS = 16

eps = 1e-06
root_two_pi = 0.7978845608028654
cubic_coef = 0.044715
MESH = pl.DeviceIdType.MESH
F32 = jnp.float32
BF16 = jnp.bfloat16


def gelu_pair(values):
    square = values * values
    tanh_part = jnp.tanh(values * (root_two_pi + (root_two_pi * cubic_coef) * square))
    half_up = 0.5 + 0.5 * tanh_part
    active = values * half_up
    gelu_slope = half_up + active * (1.0 - tanh_part) * (
        root_two_pi + (3.0 * root_two_pi * cubic_coef) * square
    )
    return active, gelu_slope


def mm(left, right, left_dim, right_dim):
    return lax.dot_general(
        left, right, (((left_dim,), (right_dim,)), ((), ())), preferred_element_type=F32
    )


def slot_source(adj, owner, reader, core, slot, ts, span, side_rows):
    strip = H * ts
    lower = core == 1
    edge_k, first_k, second_k = 2 * core, 4 + core, 7 - core
    near_turn = 2 - 2 * core

    def edge(face, flipped, depth, along):
        return face * strip + depth * ts + jnp.where(flipped, ts - 1 - along, along)

    def corner(face, depth, along):
        return face * strip + depth * ts + jnp.where(face < 2, along, ts - 1 - along)

    face = (adj[reader, 1, edge_k] + near_turn) % 4
    row_edge = edge(face, (core == 0) == (face < 2), slot // ts, slot % ts)
    is_row = adj[reader, 0, edge_k] == owner

    within = slot % side_rows
    depth = jnp.where(within >= span, 1, 0) + jnp.where(within >= 2 * span, 1, 0)
    along = within - depth * span + core * (ts - span)
    east = (adj[reader, 1, 1] + 3) % 4
    west = (adj[reader, 1, 3] + 1) % 4
    on_east = slot < side_rows
    side = jnp.where(on_east, edge(east, east < 2, depth, along), edge(west, west >= 2, depth, along))
    east_here, west_here = adj[reader, 0, 1] == owner, adj[reader, 0, 3] == owner
    side_ok = (within < H * span) & ((on_east & east_here) | ((slot >= side_rows) & west_here))

    spot = slot % CORNER_ROWS
    i = jnp.where(spot >= H, 1, 0) + jnp.where(spot >= 2 * H, 1, 0)
    j = spot - H * i
    into = jnp.where(lower, i, H - 1 - i)
    face_a = (adj[reader, 1, first_k] + near_turn) % 4
    face_b = (adj[reader, 1, second_k] + near_turn) % 4
    on_a = slot < CORNER_ROWS
    piece = jnp.where(
        on_a,
        corner(face_a, into, jnp.where(lower, j, ts - 1 - j)),
        corner(face_b, into, jnp.where(lower, ts - H + j, H - 1 - j)),
    )
    a_here, b_here = adj[reader, 0, first_k] == owner, adj[reader, 0, second_k] == owner
    piece_ok = (spot < H * H) & ((on_a & a_here) | ((slot >= CORNER_ROWS) & (slot < 2 * CORNER_ROWS) & b_here))

    found = jnp.where(side_ok, side, jnp.where(piece_ok & ~(east_here | west_here), piece, -1))
    return jnp.where(is_row, jnp.where(slot < strip, row_edge, -1), found)


def body(
    tiles, dps, factor,
    adj_hbm, x_hbm, ct_hbm, kern_hbm, gain_hbm, w_in_ref, w_out_ref, scale_hbm,
    out_ref, small_out, w_out_all,
    adj, kern, gain_ref, scale_ref, x_ref, ct_ref, pad, faces, sel, sel_t, face_slots, halo, side_tmp, corner_tmp,
    win, wout, conv_ref, part, chan_send, chan_recv, cg, cpad, vert, stage, rim_slots, rims,
    piece_send, piece_recv, piece_all, kacc, small_mine, small_sib, small_dp, small_tile, small_done, base,
    local_sem, face_send, face_recv, pair_send, pair_recv, rim_send, rim_recv,
    rs_send, rs_recv, tg_send, tg_recv, sd_send, sd_recv, st_send, st_recv,
):
    ts = x_ref.shape[0]
    channels = x_ref.shape[2]
    wide = ts + 2 * COL
    half = ts // 2
    span = half + H
    strip = H * ts
    me_t = lax.axis_index("tile")
    me_d = lax.axis_index("dp")
    me_c = lax.axis_index("chan")
    sib = 1 - me_c
    first = me_c * half
    side_first = me_c * (half - H)

    barrier = pltpu.get_barrier_semaphore()
    for o in range(1, tiles):
        pl.semaphore_signal(barrier, inc=1, device_id={"tile": lax.rem(me_t + o, tiles)}, device_id_type=MESH)
    for o in range(1, dps):
        pl.semaphore_signal(barrier, inc=1, device_id={"dp": lax.rem(me_d + o, dps)}, device_id_type=MESH)
    pl.semaphore_signal(barrier, inc=1, device_id={"chan": sib}, device_id_type=MESH)

    local = []
    for source, target in (
        (adj_hbm, adj), (x_hbm, x_ref), (kern_hbm, kern), (w_in_ref, win.at[me_c]), (w_out_ref, wout.at[me_c]),
        (ct_hbm, ct_ref), (gain_hbm, gain_ref), (scale_hbm, scale_ref),
    ):
        copy = pltpu.make_async_copy(source, target, local_sem.at[len(local)])
        copy.start()
        local.append(copy)

    dp_peers = [lax.rem(me_d + o, dps) for o in range(1, dps)]
    if tiles == 4:
        tile_peers = [lax.rem(me_t + 2, 4), 3 - me_t, me_t + 1 - 2 * lax.rem(me_t, 2)]
        tile_sources = tile_peers
    else:
        tile_peers = [lax.rem(me_t + o, tiles) for o in range(1, tiles)]
        tile_sources = [lax.rem(me_t - o + tiles, tiles) for o in range(1, tiles)]

    all_peers = [(t, d) for t in tile_peers for d in dp_peers + [me_d]] + [(me_t, d) for d in dp_peers]

    def to_peers(axis, peers, source, target, send_sems, recv_sems):
        copies = []
        for o, peer in enumerate(peers):
            copy = pltpu.make_async_remote_copy(
                src_ref=source(o, peer), dst_ref=target, send_sem=send_sems.at[o],
                recv_sem=recv_sems.at[o], device_id=axis(peer), device_id_type=MESH,
            )
            copy.start()
            copies.append(copy)
        return copies

    def to_sibling(source, target, index):
        copy = pltpu.make_async_remote_copy(
            src_ref=source, dst_ref=target, send_sem=pair_send.at[index],
            recv_sem=pair_recv.at[index], device_id={"chan": sib}, device_id_type=MESH,
        )
        copy.start()
        return copy

    def rows_loop(count, step, unroll=1):
        def wrapped(index, carry):
            step(index)
            return carry
        lax.fori_loop(0, count, wrapped, 0, unroll=unroll)

    def on_tile(peer):
        return {"tile": peer}

    def on_dp(peer):
        return {"dp": peer}

    def on_both(peer):
        return {"tile": peer[0], "dp": peer[1]}

    def zero_pad(i):
        pad[pl.ds(pl.multiple_of(i * wide, 8), wide), :] = jnp.zeros((wide, channels), F32)
    rows_loop(ts + 2 * H, zero_pad)

    local[0].wait()
    slot_down = lax.broadcasted_iota(jnp.int32, (SLOT_ROWS, 1), 0)
    face_across = lax.broadcasted_iota(jnp.int32, (SLOT_ROWS, 4 * strip), 1)
    for o, peer in enumerate(tile_peers):
        chosen = slot_source(adj, me_t, peer, me_c, slot_down, ts, span, SIDE_ROWS)
        sel[o * SLOT_ROWS:(o + 1) * SLOT_ROWS] = jnp.where(face_across == chosen, 1.0, 0.0).astype(BF16)

    local[1].wait()

    def fill(i):
        pad[pl.ds(pl.multiple_of((H + i) * wide + COL, 8), ts), :] = x_ref[i].astype(F32)
    rows_loop(ts, fill, 8)
    for d in range(H):
        faces[d * ts:(d + 1) * ts, :] = x_ref[d]
        faces[2 * strip + d * ts:2 * strip + (d + 1) * ts, :] = x_ref[ts - 1 - d]
        for f, col in ((1, COL + ts - 1 - d), (3, COL + d)):
            column = pad[pl.ds(H * wide + col, ts, stride=wide), :]
            faces[f * strip + d * ts:f * strip + (d + 1) * ts, :] = column.astype(BF16)
    face_slots[...] = mm(sel[...], faces[...], 1, 0).astype(BF16)

    pl.semaphore_wait(barrier, tiles - 1 + dps - 1 + 1)
    face_copies = to_peers(on_tile, tile_peers, lambda o, peer: face_slots.at[pl.ds(o * SLOT_ROWS, SLOT_ROWS)], halo.at[me_t], face_send, face_recv)
    win_copy = to_sibling(w_in_ref, win.at[me_c], 0)
    wout_copy = to_sibling(w_out_ref, wout.at[me_c], 1)

    halo[me_t] = jnp.zeros((SLOT_ROWS, channels), BF16)
    local[2].wait()

    def conv_rows(block):
        i = block * ROWS_AT_ONCE
        acc = [jnp.zeros((ts, channels), F32) for _ in range(ROWS_AT_ONCE)]
        for a in range(ROWS_AT_ONCE + KS - 1):
            for b in range(KS):
                window = pad[pl.ds((first + i + a) * wide + COL - H + b, ts), :]
                for r in range(ROWS_AT_ONCE):
                    if 0 <= a - r < KS:
                        at = (a - r) * KS + b
                        acc[r] = acc[r] + window * kern[at:at + 1, :]
        for r in range(ROWS_AT_ONCE):
            conv_ref[pl.ds(pl.multiple_of((i + r) * ts, 8), ts), :] = acc[r]
    rows_loop(half // ROWS_AT_ONCE, conv_rows)

    def zero_rows(i):
        cpad[pl.ds(pl.multiple_of(i * wide, 8), wide), :] = jnp.zeros((wide, channels), F32)
    rows_loop(cpad.shape[0] // wide, zero_rows)
    kacc[...] = jnp.zeros_like(kacc)
    lane = lax.broadcasted_iota(jnp.int32, (1, (tiles - 1) * strip), 1)
    face_down = lax.broadcasted_iota(jnp.int32, (4 * strip, (tiles - 1) * strip), 0)
    for core in range(2):
        chosen = jnp.full(lane.shape, -1, jnp.int32)
        for o, peer in enumerate(tile_sources):
            at = lane - o * strip
            here = slot_source(adj, me_t, peer, core, jnp.clip(at, 0, strip - 1), ts, half, strip // 2)
            chosen = jnp.where((at >= 0) & (at < strip), here, chosen)
        sel_t[core] = jnp.where(face_down == chosen, 1.0, 0.0).astype(BF16)

    for copy in face_copies:
        copy.wait_recv()
    side_tmp[0] = halo[adj[me_t, 0, 1], :SIDE_ROWS].astype(F32)
    side_tmp[1] = halo[adj[me_t, 0, 3], SIDE_ROWS:].astype(F32)
    corner_tmp[0] = halo[adj[me_t, 0, 4 + me_c], :CORNER_ROWS].astype(F32)
    corner_tmp[1] = halo[adj[me_t, 0, 7 - me_c], CORNER_ROWS:2 * CORNER_ROWS].astype(F32)
    row_strip = halo[adj[me_t, 0, 2 * me_c], :strip].astype(F32)
    side_row = (H + side_first) * wide
    for d in range(H):
        pad[pl.ds(side_row + COL + ts + d, span, stride=wide), :] = side_tmp[0, d * span:(d + 1) * span, :]
        pad[pl.ds(side_row + COL - 1 - d, span, stride=wide), :] = side_tmp[1, d * span:(d + 1) * span, :]

    west_fix = [jnp.zeros((half, channels), F32) for _ in range(H)]
    east_fix = [jnp.zeros((half, channels), F32) for _ in range(H)]
    for a in range(KS):
        for e in range(H):
            west = pad[pl.ds((first + a) * wide + COL - H + e, half, stride=wide), :]
            east = pad[pl.ds((first + a) * wide + COL + ts + e, half, stride=wide), :]
            for m in range(H):
                if m <= e:
                    at = a * KS + e - m
                    west_fix[m] = west_fix[m] + west * kern[at:at + 1, :]
                if e + m < H:
                    at = a * KS + H + 1 + e + m
                    east_fix[m] = east_fix[m] + east * kern[at:at + 1, :]
    for m in range(H):
        conv_ref[pl.ds(m, half, stride=ts), :] += west_fix[m]
        conv_ref[pl.ds(ts - 1 - m, half, stride=ts), :] += east_fix[m]

    for d in range(H):
        row = H - 1 - d + me_c * (ts + 1 + 2 * d)
        pad[pl.ds(pl.multiple_of(row * wide + COL, 8), ts), :] = row_strip[d * ts:(d + 1) * ts]
    for i in range(H):
        row = i + me_c * (ts + H)
        pad[pl.ds(row * wide + COL + ts, H), :] = corner_tmp[0, H * i:H * (i + 1), :]
        pad[pl.ds(row * wide + COL - H, H), :] = corner_tmp[1, H * i:H * (i + 1), :]
    row_fix = [jnp.zeros((ts, channels), F32) for _ in range(H)]
    for h in range(H):
        for b in range(KS):
            window = pad[pl.ds((h + me_c * (ts + 2 * H - 1 - 2 * h)) * wide + COL - H + b, ts), :]
            for i in range(h + 1):
                a = h - i + me_c * (KS - 1 - 2 * (h - i))
                row_fix[i] = row_fix[i] + window * kern[pl.ds(a * KS + b, 1), :]
    for i in range(H):
        conv_ref[pl.ds(pl.multiple_of((i + me_c * (half - 1 - 2 * i)) * ts, 8), ts), :] += row_fix[i]

    win_copy.wait_recv()
    wout_copy.wait_recv()
    for copy in local[3:]:
        copy.wait()

    gain = gain_ref[...]
    layer_scale = scale_ref[...]
    block_rows = 16
    pixels = block_rows * ts
    gain_total = jnp.zeros((1, channels), F32)
    scale_total = jnp.zeros((1, channels), F32)
    blocks = []
    for block in range(half // block_rows):
        at = block * block_rows
        conv = conv_ref[at * ts:(at + block_rows) * ts, :]
        mean = jnp.mean(conv, axis=1, keepdims=True)
        centred = conv - mean
        inv_std = lax.rsqrt(jnp.mean(centred * centred, axis=1, keepdims=True) + eps)
        normed = centred * inv_std
        normed_b = (normed * gain).astype(BF16)
        upstream = ct_ref[pl.ds(first + at, block_rows)].reshape(pixels, channels).astype(F32)
        scaled_b = (upstream * layer_scale).astype(BF16)
        blocks.append([inv_std, normed, normed_b, upstream, scaled_b, 0.0, 0.0])
    part_rows = channels // dps
    part_copy = None
    for c in (sib, me_c):
        grads = [0.0, 0.0]
        for state in blocks:
            inv_std, normed, normed_b, upstream, scaled_b, branch, normed_grad = state
            active, slope = gelu_pair(mm(normed_b, win[c], 1, 0))
            active_b = active.astype(BF16)
            state[5] = branch + mm(active_b, wout[c], 1, 0)
            hidden_grad = (mm(scaled_b, wout[c], 1, 1) * slope).astype(BF16)
            state[6] = normed_grad + mm(hidden_grad, win[c], 1, 1)
            grads[0] = grads[0] + mm(normed_b, hidden_grad, 0, 0)
            grads[1] = grads[1] + mm(scaled_b, active_b, 0, 0)
        for w in range(2):
            if part_copy is None:
                chan_send[w] = grads[w].astype(BF16)
            else:
                part[w] = grads[w]
        if part_copy is None:
            part_copy = to_sibling(chan_send, chan_recv, 2)
    for block, (inv_std, normed, normed_b, upstream, scaled_b, branch, normed_grad) in enumerate(blocks):
        at = block * block_rows
        scaled = normed_grad * gain
        first_mean = jnp.mean(scaled, axis=1, keepdims=True)
        second_mean = jnp.mean(scaled * normed, axis=1, keepdims=True)
        grad_b = (inv_std * (scaled - first_mean - normed * second_mean)).astype(BF16)
        cg[pl.ds(first + at, block_rows)] = grad_b.reshape(block_rows, ts, channels)
        scale_total = scale_total + jnp.sum(upstream * branch, axis=0, keepdims=True)
        gain_total = gain_total + jnp.sum(normed_grad * normed, axis=0, keepdims=True)
    cg_copy = to_sibling(cg.at[pl.ds(first, half)], cg.at[pl.ds(first, half)], 3)

    def widen(row):
        cpad[pl.ds(pl.multiple_of((KS - 1 + row) * wide + COL, 8), ts), :] = cg[row].astype(F32)
    rows_loop(half, lambda i: widen(first + i), 4)

    def kernel_taps(start, stop):
        for a in range(start, stop):
            def kernel_row(i, acc):
                grad = cpad[pl.ds(pl.multiple_of((KS - 1 + first + i) * wide + COL, 8), ts), :]
                new = []
                for b in range(KS):
                    window = pad[pl.ds((first + i + a) * wide + COL - H + b, ts), :]
                    new.append(acc[b] + jnp.sum((window * grad).reshape(ts // 8, 8, channels), axis=0))
                return tuple(new)
            sums = lax.fori_loop(0, half, kernel_row, tuple(jnp.zeros((8, channels), F32) for _ in range(KS)), unroll=4)
            for b in range(KS):
                kacc[a * KS + b] = sums[b]

    kernel_taps(0, KS)
    taps = KS * KS
    kacc[taps, 0:1, :] = gain_total
    kacc[taps + 1, 0:1, :] = scale_total
    half_small = SMALL_ROWS // 2
    for c in range(2):
        small_mine[c] = jnp.sum(kacc[c * half_small:(c + 1) * half_small], axis=1)
    small_copy = to_sibling(small_mine.at[sib], small_sib, 4)

    part_copy.wait_recv()
    at_once = part_rows // tiles
    for w in range(2):
        whole = (part[w] + chan_recv[w].astype(F32)).astype(BF16)
        for d in range(dps):
            for t in range(tiles):
                at = d * part_rows + t * at_once
                piece_send[t, d, w * at_once:(w + 1) * at_once] = whole[at:at + at_once]
    piece_recv[me_t, me_d] = piece_send[me_t, me_d]
    rs_copies = to_peers(
        on_both, all_peers, lambda o, peer: piece_send.at[peer[0], peer[1]], piece_recv.at[me_t, me_d], rs_send, rs_recv
    )

    cg_copy.wait_recv()
    rows_loop(half, lambda i: widen(sib * half + i), 4)

    small_copy.wait_recv()
    small_dp[me_d] = (small_mine[me_c] + small_sib[...]).astype(BF16)
    sd_copies = to_peers(on_dp, dp_peers, lambda o, peer: small_dp.at[me_d], small_dp.at[me_d], sd_send, sd_recv)

    across = ts + 8
    for h in range(H):
        acc = jnp.zeros((across, channels), F32)
        for i in range(h + 1):
            row = KS - 1 + i + me_c * (ts - 1 - 2 * i)
            a = h - i + me_c * (KS - 1 - 2 * (h - i))
            for b in range(KS):
                acc = acc + cpad[pl.ds(row * wide + COL - b, across), :] * kern[pl.ds(a * KS + b, 1), :]
        vert[h * across:(h + 1) * across, :] = acc
    west_rim = [jnp.zeros((half, channels), F32) for _ in range(H)]
    east_rim = [jnp.zeros((half, channels), F32) for _ in range(H)]
    for a in range(KS):
        row = (KS - 1 + H + first - a) * wide
        for j in range(H):
            west = cpad[pl.ds(row + COL + j, half, stride=wide), :]
            east = cpad[pl.ds(row + COL + ts - 1 - j, half, stride=wide), :]
            for d in range(H):
                if j <= H - 1 - d:
                    at = a * KS + H - 1 - d - j
                    west_rim[d] = west_rim[d] + west * kern[at:at + 1, :]
                    at = a * KS + H + 1 + d + j
                    east_rim[d] = east_rim[d] + east * kern[at:at + 1, :]
    for s in range(2):
        corner_tmp[s] = jnp.zeros((CORNER_ROWS, channels), F32)
    for d in range(H):
        stage[1, d * half:(d + 1) * half, :] = east_rim[d].astype(BF16)
        stage[1, (H + d) * half:(H + d + 1) * half, :] = west_rim[d].astype(BF16)
    for i in range(H):
        row = (i + me_c * (H - 1 - 2 * i)) * across
        corner_tmp[0, H * i:H * (i + 1), :] = vert[pl.ds(row + H + ts, H), :]
        corner_tmp[1, H * i:H * (i + 1), :] = vert[pl.ds(row, H), :]
    for h in range(H):
        d = H - 1 - h
        stage[0, d * ts:(d + 1) * ts, :] = vert[h * across + H:h * across + H + ts, :].astype(BF16)
    stage[2, 2 * CORNER_ROWS:, :] = jnp.zeros((strip - 2 * CORNER_ROWS, channels), BF16)
    for s in range(2):
        stage[2, s * CORNER_ROWS:(s + 1) * CORNER_ROWS, :] = corner_tmp[s].astype(BF16)
    for o, peer in enumerate(tile_peers):
        beside = (adj[me_t, 0, 1] == peer) | (adj[me_t, 0, 3] == peer)
        kind = jnp.where(adj[me_t, 0, 2 * me_c] == peer, 0, jnp.where(beside, 1, 2))
        rim_slots[o * strip:(o + 1) * strip] = stage[kind]
    rim_copies = []
    for o, peer in enumerate(tile_peers):
        slots = pl.ds(o * strip, strip)
        copy = pltpu.make_async_remote_copy(
            src_ref=rim_slots.at[slots], dst_ref=rims.at[me_c, slots], send_sem=rim_send.at[o],
            recv_sem=rim_recv.at[o], device_id={"tile": peer}, device_id_type=MESH,
        )
        copy.start()
        rim_copies.append(copy)

    def spread_rows(block):
        i = block * ROWS_AT_ONCE
        acc = [ct_ref[i + r].astype(F32) for r in range(ROWS_AT_ONCE)]
        for up in range(ROWS_AT_ONCE + KS - 1):
            for b in range(KS):
                window = cpad[pl.ds((i + H + up) * wide + COL + H - b, ts), :]
                for r in range(ROWS_AT_ONCE):
                    a = KS - 1 + r - up
                    if 0 <= a < KS:
                        acc[r] = acc[r] + window * kern[a * KS + b:a * KS + b + 1, :]
        for r in range(ROWS_AT_ONCE):
            base[pl.ds(pl.multiple_of((i + r) * ts, 8), ts), :] = acc[r]
    spread_blocks = ts // ROWS_AT_ONCE

    def spread_part(start, stop):
        rows_loop((stop - start) * spread_blocks // 8, lambda block: spread_rows(block + start * spread_blocks // 8))

    spread_part(0, 6)
    for copy in sd_copies:
        copy.wait_recv()
    total = small_dp[0].astype(F32)
    for d in range(1, dps):
        total = total + small_dp[d].astype(F32)
    small_tile[me_t] = total.astype(BF16)
    st_copies, st_waits = [], []
    for o in range(tiles - 1):
        peer = o + jnp.where(o >= me_t, 1, 0)
        for source, target, copies in ((me_t, peer, st_copies), (peer, peer, st_waits)):
            copies.append(pltpu.make_async_remote_copy(
                src_ref=small_tile.at[source], dst_ref=small_tile.at[source], send_sem=st_send.at[o],
                recv_sem=st_recv.at[source], device_id={"tile": target}, device_id_type=MESH,
            ))
        st_copies[o].start()
    spread_part(6, 8)

    for copy in rs_copies:
        copy.wait_recv()
    total = jnp.zeros((2 * at_once, win.shape[2]), F32)
    for t in range(tiles):
        for d in range(dps):
            total = total + piece_recv[t, d].astype(F32)
    piece_all[me_t] = (total * factor).astype(BF16)
    tg_copies, tg_waits = [], []
    for o in range(tiles - 1):
        peer = o + jnp.where(o >= me_t, 1, 0)
        for source, target, copies in ((me_t, peer, tg_copies), (peer, peer, tg_waits)):
            copies.append(pltpu.make_async_remote_copy(
                src_ref=piece_all.at[source], dst_ref=piece_all.at[source], send_sem=tg_send.at[o],
                recv_sem=tg_recv.at[source], device_id={"tile": target}, device_id_type=MESH,
            ))
        tg_copies[o].start()

    rim_passes = []
    for o, copy in enumerate(rim_copies):
        slots = pl.ds(o * strip, strip)
        copy.wait_recv()
        rim_passes.append(to_sibling(rims.at[me_c, slots], rims.at[me_c, slots], 5 + o))
    from_mine = mm(sel_t[me_c], rims[me_c], 1, 0)

    for copy in st_waits:
        copy.wait_recv()
    total = small_tile[0].astype(F32)
    for t in range(1, tiles):
        total = total + small_tile[t].astype(F32)
    small_done[me_c] = total * factor
    done_copy = to_sibling(small_done.at[me_c], small_done.at[me_c], 4 + tiles)

    for copy in rim_passes:
        copy.wait_recv()
    incoming = from_mine + mm(sel_t[sib], rims[sib], 1, 0)
    for d in range(H):
        part_of = [incoming[f * strip + d * ts:f * strip + (d + 1) * ts] for f in range(4)]
        base[d * ts:(d + 1) * ts, :] += part_of[0]
        base[(ts - 1 - d) * ts:(ts - d) * ts, :] += part_of[2]
        base[pl.ds(ts - 1 - d, ts, stride=ts), :] += part_of[1]
        base[pl.ds(d, ts, stride=ts), :] += part_of[3]

    def out_row(i):
        out_ref[i] = base[pl.ds(pl.multiple_of(i * ts, 8), ts), :].astype(BF16)
    rows_loop(ts, out_row, 4)

    done_copy.wait_recv()
    small_out[...] = small_done[...]
    for copy in tg_waits:
        copy.wait_recv()
    for w in range(2):
        for t in range(tiles):
            at = w * part_rows + t * at_once
            w_out_all[at:at + at_once, :] = piece_all[t, w * at_once:(w + 1) * at_once].astype(F32)

    for copy in face_copies + rim_copies + rim_passes + rs_copies + sd_copies + tg_copies + st_copies + [
        win_copy, wout_copy, cg_copy, part_copy, small_copy, done_copy
    ]:
        copy.wait_send()


def write_out(out, small, grads, out_hbm, kernel_hbm, gain_hbm, w_in_hbm, w_out_hbm, scale_hbm, sems):
    taps = KS * KS
    rows = w_in_hbm.shape[0]
    pairs = (
        (out, out_hbm),
        (grads.at[:rows], w_in_hbm),
        (grads.at[rows:], w_out_hbm),
        (small.at[:taps], kernel_hbm),
        (small.at[taps:taps + 1], gain_hbm),
        (small.at[taps + 1:taps + 2], scale_hbm),
    )
    copies = [pltpu.make_async_copy(source, target, sems.at[i]) for i, (source, target) in enumerate(pairs)]
    for copy in copies:
        copy.start()
    for copy in copies:
        copy.wait()


def in_hbm(array):
    return pltpu.with_memory_space_constraint(array, pltpu.MemorySpace.HBM)


def on_device(inputs, kernel, norm_gain, w_in, w_out, layer_scale, cotangent, adjacency):
    ts, ch = inputs.shape[2], inputs.shape[4]
    hid = w_in.shape[1]
    tiles, dps = lax.axis_size("tile"), lax.axis_size("dp")
    factor = 1.0 / math.sqrt(dps * tiles * ts * ts)
    strip = H * ts
    wide = ts + 2 * COL
    part_rows = ch // dps
    vmem = pl.BlockSpec(memory_space=pltpu.VMEM)
    hbm = pl.BlockSpec(memory_space=pltpu.MemorySpace.HBM)
    dma = pltpu.SemaphoreType.DMA
    peers_t, peers_d = max(tiles - 1, 1), max(dps - 1, 1)
    pairs = 6 + peers_t
    out, small, grads = pl.pallas_call(
        functools.partial(body, tiles, dps, factor),
        out_shape=(
            jax.ShapeDtypeStruct((ts, ts, ch), BF16),
            jax.ShapeDtypeStruct((2, SMALL_ROWS // 2, ch), F32),
            jax.ShapeDtypeStruct((2 * part_rows, hid), F32),
        ),
        in_specs=[hbm] * 8,
        out_specs=(vmem,) * 3,
        scratch_shapes=[
            pltpu.SMEM((tiles, 2, 8), jnp.int32),
            pltpu.VMEM((KS * KS, ch), F32),
            pltpu.VMEM((1, ch), F32),
            pltpu.VMEM((1, ch), F32),
            pltpu.VMEM((ts, ts, ch), BF16),
            pltpu.VMEM((ts, ts, ch), BF16),
            pltpu.VMEM(((ts + 2 * H) * wide, ch), F32),
            pltpu.VMEM((4 * strip, ch), BF16),
            pltpu.VMEM((peers_t * SLOT_ROWS, 4 * strip), BF16),
            pltpu.VMEM((2, 4 * strip, peers_t * strip), BF16),
            pltpu.VMEM((peers_t * SLOT_ROWS, ch), BF16),
            pltpu.VMEM((tiles, SLOT_ROWS, ch), BF16),
            pltpu.VMEM((2, SIDE_ROWS, ch), F32),
            pltpu.VMEM((2, CORNER_ROWS, ch), F32),
            pltpu.VMEM((2, ch, hid), BF16),
            pltpu.VMEM((2, hid, ch), BF16),
            pltpu.VMEM((ts // 2 * ts, ch), F32),
            pltpu.VMEM((2, ch, hid), F32),
            pltpu.VMEM((2, ch, hid), BF16),
            pltpu.VMEM((2, ch, hid), BF16),
            pltpu.VMEM((ts, ts, ch), BF16),
            pltpu.VMEM(((ts + 2 * KS) * wide, ch), F32),
            pltpu.VMEM((H * (ts + 8), ch), F32),
            pltpu.VMEM((3, strip, ch), BF16),
            pltpu.VMEM((peers_t * strip, ch), BF16),
            pltpu.VMEM((2, peers_t * strip, ch), BF16),
            pltpu.VMEM((tiles, dps, 2 * part_rows // tiles, hid), BF16),
            pltpu.VMEM((tiles, dps, 2 * part_rows // tiles, hid), BF16),
            pltpu.VMEM((tiles, 2 * part_rows // tiles, hid), BF16),
            pltpu.VMEM((SMALL_ROWS, 8, ch), F32),
            pltpu.VMEM((2, SMALL_ROWS // 2, ch), F32),
            pltpu.VMEM((SMALL_ROWS // 2, ch), F32),
            pltpu.VMEM((dps, SMALL_ROWS // 2, ch), BF16),
            pltpu.VMEM((tiles, SMALL_ROWS // 2, ch), BF16),
            pltpu.VMEM((2, SMALL_ROWS // 2, ch), F32),
            pltpu.VMEM((ts * ts, ch), F32),
            dma((8,)),
            dma((peers_t,)), dma((peers_t,)), dma((pairs,)), dma((pairs,)), dma((peers_t,)), dma((peers_t,)),
            dma((tiles * dps,)), dma((tiles * dps,)), dma((peers_t,)), dma((tiles,)),
            dma((peers_d,)), dma((peers_d,)), dma((peers_t,)), dma((tiles,)),
        ],
        compiler_params=pltpu.CompilerParams(
            collective_id=0, has_side_effects=True, vmem_limit_bytes=48 * 1024 * 1024
        ),
    )(
        in_hbm(jnp.transpose(adjacency, (0, 2, 1))), in_hbm(inputs[0, 0]), in_hbm(cotangent[0, 0]), in_hbm(kernel),
        in_hbm(norm_gain[None]), in_hbm(w_in), in_hbm(w_out), in_hbm(layer_scale[None]),
    )
    results = pl.pallas_call(
        write_out,
        out_shape=(
            jax.ShapeDtypeStruct((ts, ts, ch), BF16),
            jax.ShapeDtypeStruct((KS * KS, ch), F32),
            jax.ShapeDtypeStruct((1, ch), F32),
            jax.ShapeDtypeStruct((part_rows, hid), F32),
            jax.ShapeDtypeStruct((part_rows, hid), F32),
            jax.ShapeDtypeStruct((1, ch), F32),
        ),
        in_specs=[pl.BlockSpec(memory_space=pl.ANY)] * 3,
        out_specs=(hbm,) * 6,
        scratch_shapes=[dma((6,))],
        compiler_params=pltpu.CompilerParams(vmem_limit_bytes=1024 * 1024),
    )(out, small.reshape(SMALL_ROWS, ch), grads)
    return (
        results[0][None, None],
        results[1],
        results[2].reshape(ch),
        results[3],
        results[4].T,
        results[5].reshape(ch),
    )


def solution(mesh):
    placed = (
        P(("group", "dp"), "tile", None, None, None),
        P(),
        P(),
        P(None, "chan"),
        P("chan", None),
        P(),
        P(("group", "dp"), "tile", None, None, None),
        P(),
    )
    return jax.shard_map(
        on_device,
        mesh=mesh,
        in_specs=placed,
        out_specs=(
            P(("group", "dp"), "tile", None, None, None),
            P("group", None),
            P("group"),
            P(("group", "dp"), "chan"),
            P(("group", "chan"), "dp"),
            P("group"),
        ),
        check_vma=False,
    )
```

```python
import functools
import math

import jax
import jax.numpy as jnp
from jax import lax
from jax.experimental import pallas as pl
from jax.experimental.pallas import tpu as pltpu
from jax.sharding import PartitionSpec as P

KS = 7
H = KS // 2
COL = 8
ROWS_AT_ONCE = 4
SMALL_ROWS = 64
SIDE_ROWS = 64
SLOT_ROWS = 2 * SIDE_ROWS
CORNER_ROWS = 16

eps = 1e-06
root_two_pi = 0.7978845608028654
cubic_coef = 0.044715
MESH = pl.DeviceIdType.MESH
F32 = jnp.float32
BF16 = jnp.bfloat16


def gelu_pair(values):
    square = values * values
    tanh_part = jnp.tanh(values * (root_two_pi + (root_two_pi * cubic_coef) * square))
    half_up = 0.5 + 0.5 * tanh_part
    active = values * half_up
    gelu_slope = half_up + active * (1.0 - tanh_part) * (
        root_two_pi + (3.0 * root_two_pi * cubic_coef) * square
    )
    return active, gelu_slope


def mm(left, right, left_dim, right_dim):
    return lax.dot_general(
        left, right, (((left_dim,), (right_dim,)), ((), ())), preferred_element_type=F32
    )


def slot_source(adj, owner, reader, core, slot, ts, span, side_rows):
    strip = H * ts
    lower = core == 1
    edge_k, first_k, second_k = 2 * core, 4 + core, 7 - core
    near_turn = 2 - 2 * core

    def edge(face, flipped, depth, along):
        return face * strip + depth * ts + jnp.where(flipped, ts - 1 - along, along)

    def corner(face, depth, along):
        return face * strip + depth * ts + jnp.where(face < 2, along, ts - 1 - along)

    face = (adj[reader, 1, edge_k] + near_turn) % 4
    row_edge = edge(face, (core == 0) == (face < 2), slot // ts, slot % ts)
    is_row = adj[reader, 0, edge_k] == owner

    within = slot % side_rows
    depth = jnp.where(within >= span, 1, 0) + jnp.where(within >= 2 * span, 1, 0)
    along = within - depth * span + core * (ts - span)
    east = (adj[reader, 1, 1] + 3) % 4
    west = (adj[reader, 1, 3] + 1) % 4
    on_east = slot < side_rows
    side = jnp.where(on_east, edge(east, east < 2, depth, along), edge(west, west >= 2, depth, along))
    east_here, west_here = adj[reader, 0, 1] == owner, adj[reader, 0, 3] == owner
    side_ok = (within < H * span) & ((on_east & east_here) | ((slot >= side_rows) & west_here))

    spot = slot % CORNER_ROWS
    i = jnp.where(spot >= H, 1, 0) + jnp.where(spot >= 2 * H, 1, 0)
    j = spot - H * i
    into = jnp.where(lower, i, H - 1 - i)
    face_a = (adj[reader, 1, first_k] + near_turn) % 4
    face_b = (adj[reader, 1, second_k] + near_turn) % 4
    on_a = slot < CORNER_ROWS
    piece = jnp.where(
        on_a,
        corner(face_a, into, jnp.where(lower, j, ts - 1 - j)),
        corner(face_b, into, jnp.where(lower, ts - H + j, H - 1 - j)),
    )
    a_here, b_here = adj[reader, 0, first_k] == owner, adj[reader, 0, second_k] == owner
    piece_ok = (spot < H * H) & ((on_a & a_here) | ((slot >= CORNER_ROWS) & (slot < 2 * CORNER_ROWS) & b_here))

    found = jnp.where(side_ok, side, jnp.where(piece_ok & ~(east_here | west_here), piece, -1))
    return jnp.where(is_row, jnp.where(slot < strip, row_edge, -1), found)


def body(
    tiles, dps, factor,
    adj_hbm, x_hbm, ct_hbm, kern_hbm, gain_hbm, w_in_ref, w_out_ref, scale_hbm,
    out_ref, small_out, w_out_all,
    adj, kern, gain_ref, scale_ref, x_ref, ct_ref, pad, faces, sel, sel_t, face_slots, halo, side_tmp, corner_tmp,
    win, wout, conv_ref, part, chan_send, chan_recv, cg, cpad, vert, stage, rim_slots, rims,
    piece_send, piece_recv, piece_all, kacc, small_mine, small_sib, small_dp, small_tile, small_done, base,
    local_sem, face_send, face_recv, pair_send, pair_recv, rim_send, rim_recv,
    rs_send, rs_recv, tg_send, tg_recv, sd_send, sd_recv, st_send, st_recv,
):
    ts = x_ref.shape[0]
    channels = x_ref.shape[2]
    wide = ts + 2 * COL
    half = ts // 2
    span = half + H
    strip = H * ts
    me_t = lax.axis_index("tile")
    me_d = lax.axis_index("dp")
    me_c = lax.axis_index("chan")
    sib = 1 - me_c
    first = me_c * half
    side_first = me_c * (half - H)

    barrier = pltpu.get_barrier_semaphore()
    for o in range(1, tiles):
        pl.semaphore_signal(barrier, inc=1, device_id={"tile": lax.rem(me_t + o, tiles)}, device_id_type=MESH)
    for o in range(1, dps):
        pl.semaphore_signal(barrier, inc=1, device_id={"dp": lax.rem(me_d + o, dps)}, device_id_type=MESH)
    pl.semaphore_signal(barrier, inc=1, device_id={"chan": sib}, device_id_type=MESH)

    local = []
    for source, target in (
        (adj_hbm, adj), (x_hbm, x_ref), (kern_hbm, kern), (w_in_ref, win.at[me_c]), (w_out_ref, wout.at[me_c]),
        (ct_hbm, ct_ref), (gain_hbm, gain_ref), (scale_hbm, scale_ref),
    ):
        copy = pltpu.make_async_copy(source, target, local_sem.at[len(local)])
        copy.start()
        local.append(copy)

    dp_peers = [lax.rem(me_d + o, dps) for o in range(1, dps)]
    if tiles == 4:
        tile_peers = [lax.rem(me_t + 2, 4), 3 - me_t, me_t + 1 - 2 * lax.rem(me_t, 2)]
        tile_sources = tile_peers
    else:
        tile_peers = [lax.rem(me_t + o, tiles) for o in range(1, tiles)]
        tile_sources = [lax.rem(me_t - o + tiles, tiles) for o in range(1, tiles)]

    all_peers = [(t, d) for t in tile_peers for d in dp_peers + [me_d]] + [(me_t, d) for d in dp_peers]

    def to_peers(axis, peers, source, target, send_sems, recv_sems):
        copies = []
        for o, peer in enumerate(peers):
            copy = pltpu.make_async_remote_copy(
                src_ref=source(o, peer), dst_ref=target, send_sem=send_sems.at[o],
                recv_sem=recv_sems.at[o], device_id=axis(peer), device_id_type=MESH,
            )
            copy.start()
            copies.append(copy)
        return copies

    def to_sibling(source, target, index):
        copy = pltpu.make_async_remote_copy(
            src_ref=source, dst_ref=target, send_sem=pair_send.at[index],
            recv_sem=pair_recv.at[index], device_id={"chan": sib}, device_id_type=MESH,
        )
        copy.start()
        return copy

    def rows_loop(count, step, unroll=1):
        def wrapped(index, carry):
            step(index)
            return carry
        lax.fori_loop(0, count, wrapped, 0, unroll=unroll)

    def on_tile(peer):
        return {"tile": peer}

    def on_dp(peer):
        return {"dp": peer}

    def on_both(peer):
        return {"tile": peer[0], "dp": peer[1]}

    def zero_pad(i):
        pad[pl.ds(pl.multiple_of(i * wide, 8), wide), :] = jnp.zeros((wide, channels), F32)
    rows_loop(ts + 2 * H, zero_pad)

    local[0].wait()
    slot_down = lax.broadcasted_iota(jnp.int32, (SLOT_ROWS, 1), 0)
    face_across = lax.broadcasted_iota(jnp.int32, (SLOT_ROWS, 4 * strip), 1)
    for o, peer in enumerate(tile_peers):
        chosen = slot_source(adj, me_t, peer, me_c, slot_down, ts, span, SIDE_ROWS)
        sel[o * SLOT_ROWS:(o + 1) * SLOT_ROWS] = jnp.where(face_across == chosen, 1.0, 0.0).astype(BF16)

    local[1].wait()

    def fill(i):
        pad[pl.ds(pl.multiple_of((H + i) * wide + COL, 8), ts), :] = x_ref[i].astype(F32)
    rows_loop(ts, fill, 8)
    for d in range(H):
        faces[d * ts:(d + 1) * ts, :] = x_ref[d]
        faces[2 * strip + d * ts:2 * strip + (d + 1) * ts, :] = x_ref[ts - 1 - d]
        for f, col in ((1, COL + ts - 1 - d), (3, COL + d)):
            column = pad[pl.ds(H * wide + col, ts, stride=wide), :]
            faces[f * strip + d * ts:f * strip + (d + 1) * ts, :] = column.astype(BF16)
    face_slots[...] = mm(sel[...], faces[...], 1, 0).astype(BF16)

    pl.semaphore_wait(barrier, tiles - 1 + dps - 1 + 1)
    face_copies = to_peers(on_tile, tile_peers, lambda o, peer: face_slots.at[pl.ds(o * SLOT_ROWS, SLOT_ROWS)], halo.at[me_t], face_send, face_recv)
    win_copy = to_sibling(w_in_ref, win.at[me_c], 0)
    wout_copy = to_sibling(w_out_ref, wout.at[me_c], 1)

    halo[me_t] = jnp.zeros((SLOT_ROWS, channels), BF16)
    local[2].wait()

    def conv_rows(block):
        i = block * ROWS_AT_ONCE
        acc = [jnp.zeros((ts, channels), F32) for _ in range(ROWS_AT_ONCE)]
        for a in range(ROWS_AT_ONCE + KS - 1):
            for b in range(KS):
                window = pad[pl.ds((first + i + a) * wide + COL - H + b, ts), :]
                for r in range(ROWS_AT_ONCE):
                    if 0 <= a - r < KS:
                        at = (a - r) * KS + b
                        acc[r] = acc[r] + window * kern[at:at + 1, :]
        for r in range(ROWS_AT_ONCE):
            conv_ref[pl.ds(pl.multiple_of((i + r) * ts, 8), ts), :] = acc[r]
    rows_loop(half // ROWS_AT_ONCE, conv_rows)

    def zero_rows(i):
        cpad[pl.ds(pl.multiple_of(i * wide, 8), wide), :] = jnp.zeros((wide, channels), F32)
    rows_loop(cpad.shape[0] // wide, zero_rows)
    kacc[...] = jnp.zeros_like(kacc)
    lane = lax.broadcasted_iota(jnp.int32, (1, (tiles - 1) * strip), 1)
    face_down = lax.broadcasted_iota(jnp.int32, (4 * strip, (tiles - 1) * strip), 0)
    for core in range(2):
        chosen = jnp.full(lane.shape, -1, jnp.int32)
        for o, peer in enumerate(tile_sources):
            at = lane - o * strip
            here = slot_source(adj, me_t, peer, core, jnp.clip(at, 0, strip - 1), ts, half, strip // 2)
            chosen = jnp.where((at >= 0) & (at < strip), here, chosen)
        sel_t[core] = jnp.where(face_down == chosen, 1.0, 0.0).astype(BF16)

    for copy in face_copies:
        copy.wait_recv()
    side_tmp[0] = halo[adj[me_t, 0, 1], :SIDE_ROWS].astype(F32)
    side_tmp[1] = halo[adj[me_t, 0, 3], SIDE_ROWS:].astype(F32)
    corner_tmp[0] = halo[adj[me_t, 0, 4 + me_c], :CORNER_ROWS].astype(F32)
    corner_tmp[1] = halo[adj[me_t, 0, 7 - me_c], CORNER_ROWS:2 * CORNER_ROWS].astype(F32)
    row_strip = halo[adj[me_t, 0, 2 * me_c], :strip].astype(F32)
    side_row = (H + side_first) * wide
    for d in range(H):
        pad[pl.ds(side_row + COL + ts + d, span, stride=wide), :] = side_tmp[0, d * span:(d + 1) * span, :]
        pad[pl.ds(side_row + COL - 1 - d, span, stride=wide), :] = side_tmp[1, d * span:(d + 1) * span, :]

    west_fix = [jnp.zeros((half, channels), F32) for _ in range(H)]
    east_fix = [jnp.zeros((half, channels), F32) for _ in range(H)]
    for a in range(KS):
        for e in range(H):
            west = pad[pl.ds((first + a) * wide + COL - H + e, half, stride=wide), :]
            east = pad[pl.ds((first + a) * wide + COL + ts + e, half, stride=wide), :]
            for m in range(H):
                if m <= e:
                    at = a * KS + e - m
                    west_fix[m] = west_fix[m] + west * kern[at:at + 1, :]
                if e + m < H:
                    at = a * KS + H + 1 + e + m
                    east_fix[m] = east_fix[m] + east * kern[at:at + 1, :]
    for m in range(H):
        conv_ref[pl.ds(m, half, stride=ts), :] += west_fix[m]
        conv_ref[pl.ds(ts - 1 - m, half, stride=ts), :] += east_fix[m]

    for d in range(H):
        row = H - 1 - d + me_c * (ts + 1 + 2 * d)
        pad[pl.ds(pl.multiple_of(row * wide + COL, 8), ts), :] = row_strip[d * ts:(d + 1) * ts]
    for i in range(H):
        row = i + me_c * (ts + H)
        pad[pl.ds(row * wide + COL + ts, H), :] = corner_tmp[0, H * i:H * (i + 1), :]
        pad[pl.ds(row * wide + COL - H, H), :] = corner_tmp[1, H * i:H * (i + 1), :]
    row_fix = [jnp.zeros((ts, channels), F32) for _ in range(H)]
    for h in range(H):
        for b in range(KS):
            window = pad[pl.ds((h + me_c * (ts + 2 * H - 1 - 2 * h)) * wide + COL - H + b, ts), :]
            for i in range(h + 1):
                a = h - i + me_c * (KS - 1 - 2 * (h - i))
                row_fix[i] = row_fix[i] + window * kern[pl.ds(a * KS + b, 1), :]
    for i in range(H):
        conv_ref[pl.ds(pl.multiple_of((i + me_c * (half - 1 - 2 * i)) * ts, 8), ts), :] += row_fix[i]

    win_copy.wait_recv()
    wout_copy.wait_recv()
    for copy in local[3:]:
        copy.wait()

    gain = gain_ref[...]
    layer_scale = scale_ref[...]
    block_rows = 16
    pixels = block_rows * ts
    gain_total = jnp.zeros((1, channels), F32)
    scale_total = jnp.zeros((1, channels), F32)
    blocks = []
    for block in range(half // block_rows):
        at = block * block_rows
        conv = conv_ref[at * ts:(at + block_rows) * ts, :]
        mean = jnp.mean(conv, axis=1, keepdims=True)
        centred = conv - mean
        inv_std = lax.rsqrt(jnp.mean(centred * centred, axis=1, keepdims=True) + eps)
        normed = centred * inv_std
        normed_b = (normed * gain).astype(BF16)
        upstream = ct_ref[pl.ds(first + at, block_rows)].reshape(pixels, channels).astype(F32)
        scaled_b = (upstream * layer_scale).astype(BF16)
        blocks.append([inv_std, normed, normed_b, upstream, scaled_b, 0.0, 0.0])
    part_rows = channels // dps
    part_copy = None
    for c in (sib, me_c):
        grads = [0.0, 0.0]
        for state in blocks:
            inv_std, normed, normed_b, upstream, scaled_b, branch, normed_grad = state
            active, slope = gelu_pair(mm(normed_b, win[c], 1, 0))
            active_b = active.astype(BF16)
            state[5] = branch + mm(active_b, wout[c], 1, 0)
            hidden_grad = (mm(scaled_b, wout[c], 1, 1) * slope).astype(BF16)
            state[6] = normed_grad + mm(hidden_grad, win[c], 1, 1)
            grads[0] = grads[0] + mm(normed_b, hidden_grad, 0, 0)
            grads[1] = grads[1] + mm(scaled_b, active_b, 0, 0)
        for w in range(2):
            if part_copy is None:
                chan_send[w] = grads[w].astype(BF16)
            else:
                part[w] = grads[w]
        if part_copy is None:
            part_copy = to_sibling(chan_send, chan_recv, 2)
    for block, (inv_std, normed, normed_b, upstream, scaled_b, branch, normed_grad) in enumerate(blocks):
        at = block * block_rows
        scaled = normed_grad * gain
        first_mean = jnp.mean(scaled, axis=1, keepdims=True)
        second_mean = jnp.mean(scaled * normed, axis=1, keepdims=True)
        grad_b = (inv_std * (scaled - first_mean - normed * second_mean)).astype(BF16)
        cg[pl.ds(first + at, block_rows)] = grad_b.reshape(block_rows, ts, channels)
        scale_total = scale_total + jnp.sum(upstream * branch, axis=0, keepdims=True)
        gain_total = gain_total + jnp.sum(normed_grad * normed, axis=0, keepdims=True)
    cg_copy = to_sibling(cg.at[pl.ds(first, half)], cg.at[pl.ds(first, half)], 3)

    def widen(row):
        cpad[pl.ds(pl.multiple_of((KS - 1 + row) * wide + COL, 8), ts), :] = cg[row].astype(F32)
    rows_loop(half, lambda i: widen(first + i), 4)

    def kernel_taps(start, stop):
        for a in range(start, stop):
            def kernel_row(i, acc):
                grad = cpad[pl.ds(pl.multiple_of((KS - 1 + first + i) * wide + COL, 8), ts), :]
                new = []
                for b in range(KS):
                    window = pad[pl.ds((first + i + a) * wide + COL - H + b, ts), :]
                    new.append(acc[b] + jnp.sum((window * grad).reshape(ts // 8, 8, channels), axis=0))
                return tuple(new)
            sums = lax.fori_loop(0, half, kernel_row, tuple(jnp.zeros((8, channels), F32) for _ in range(KS)), unroll=4)
            for b in range(KS):
                kacc[a * KS + b] = sums[b]

    kernel_taps(0, KS)
    taps = KS * KS
    kacc[taps, 0:1, :] = gain_total
    kacc[taps + 1, 0:1, :] = scale_total
    half_small = SMALL_ROWS // 2
    for c in range(2):
        small_mine[c] = jnp.sum(kacc[c * half_small:(c + 1) * half_small], axis=1)
    small_copy = to_sibling(small_mine.at[sib], small_sib, 4)

    part_copy.wait_recv()
    at_once = part_rows // tiles
    for w in range(2):
        whole = (part[w] + chan_recv[w].astype(F32)).astype(BF16)
        for d in range(dps):
            for t in range(tiles):
                at = d * part_rows + t * at_once
                piece_send[t, d, w * at_once:(w + 1) * at_once] = whole[at:at + at_once]
    piece_recv[me_t, me_d] = piece_send[me_t, me_d]
    rs_copies = to_peers(
        on_both, all_peers, lambda o, peer: piece_send.at[peer[0], peer[1]], piece_recv.at[me_t, me_d], rs_send, rs_recv
    )

    cg_copy.wait_recv()
    rows_loop(half, lambda i: widen(sib * half + i), 4)

    small_copy.wait_recv()
    small_dp[me_d] = (small_mine[me_c] + small_sib[...]).astype(BF16)
    sd_copies = to_peers(on_dp, dp_peers, lambda o, peer: small_dp.at[me_d], small_dp.at[me_d], sd_send, sd_recv)

    across = ts + 8
    for h in range(H):
        acc = jnp.zeros((across, channels), F32)
        for i in range(h + 1):
            row = KS - 1 + i + me_c * (ts - 1 - 2 * i)
            a = h - i + me_c * (KS - 1 - 2 * (h - i))
            for b in range(KS):
                acc = acc + cpad[pl.ds(row * wide + COL - b, across), :] * kern[pl.ds(a * KS + b, 1), :]
        vert[h * across:(h + 1) * across, :] = acc
    west_rim = [jnp.zeros((half, channels), F32) for _ in range(H)]
    east_rim = [jnp.zeros((half, channels), F32) for _ in range(H)]
    for a in range(KS):
        row = (KS - 1 + H + first - a) * wide
        for j in range(H):
            west = cpad[pl.ds(row + COL + j, half, stride=wide), :]
            east = cpad[pl.ds(row + COL + ts - 1 - j, half, stride=wide), :]
            for d in range(H):
                if j <= H - 1 - d:
                    at = a * KS + H - 1 - d - j
                    west_rim[d] = west_rim[d] + west * kern[at:at + 1, :]
                    at = a * KS + H + 1 + d + j
                    east_rim[d] = east_rim[d] + east * kern[at:at + 1, :]
    for s in range(2):
        corner_tmp[s] = jnp.zeros((CORNER_ROWS, channels), F32)
    for d in range(H):
        stage[1, d * half:(d + 1) * half, :] = east_rim[d].astype(BF16)
        stage[1, (H + d) * half:(H + d + 1) * half, :] = west_rim[d].astype(BF16)
    for i in range(H):
        row = (i + me_c * (H - 1 - 2 * i)) * across
        corner_tmp[0, H * i:H * (i + 1), :] = vert[pl.ds(row + H + ts, H), :]
        corner_tmp[1, H * i:H * (i + 1), :] = vert[pl.ds(row, H), :]
    for h in range(H):
        d = H - 1 - h
        stage[0, d * ts:(d + 1) * ts, :] = vert[h * across + H:h * across + H + ts, :].astype(BF16)
    stage[2, 2 * CORNER_ROWS:, :] = jnp.zeros((strip - 2 * CORNER_ROWS, channels), BF16)
    for s in range(2):
        stage[2, s * CORNER_ROWS:(s + 1) * CORNER_ROWS, :] = corner_tmp[s].astype(BF16)
    for o, peer in enumerate(tile_peers):
        beside = (adj[me_t, 0, 1] == peer) | (adj[me_t, 0, 3] == peer)
        kind = jnp.where(adj[me_t, 0, 2 * me_c] == peer, 0, jnp.where(beside, 1, 2))
        rim_slots[o * strip:(o + 1) * strip] = stage[kind]
    rim_copies = []
    for o, peer in enumerate(tile_peers):
        slots = pl.ds(o * strip, strip)
        copy = pltpu.make_async_remote_copy(
            src_ref=rim_slots.at[slots], dst_ref=rims.at[me_c, slots], send_sem=rim_send.at[o],
            recv_sem=rim_recv.at[o], device_id={"tile": peer}, device_id_type=MESH,
        )
        copy.start()
        rim_copies.append(copy)

    def spread_rows(block):
        i = block * ROWS_AT_ONCE
        acc = [ct_ref[i + r].astype(F32) for r in range(ROWS_AT_ONCE)]
        for up in range(ROWS_AT_ONCE + KS - 1):
            for b in range(KS):
                window = cpad[pl.ds((i + H + up) * wide + COL + H - b, ts), :]
                for r in range(ROWS_AT_ONCE):
                    a = KS - 1 + r - up
                    if 0 <= a < KS:
                        acc[r] = acc[r] + window * kern[a * KS + b:a * KS + b + 1, :]
        for r in range(ROWS_AT_ONCE):
            base[pl.ds(pl.multiple_of((i + r) * ts, 8), ts), :] = acc[r]
    spread_blocks = ts // ROWS_AT_ONCE

    def spread_part(start, stop):
        rows_loop((stop - start) * spread_blocks // 8, lambda block: spread_rows(block + start * spread_blocks // 8))

    spread_part(0, 6)
    for copy in sd_copies:
        copy.wait_recv()
    total = small_dp[0].astype(F32)
    for d in range(1, dps):
        total = total + small_dp[d].astype(F32)
    small_tile[me_t] = total.astype(BF16)
    st_copies, st_waits = [], []
    for o in range(tiles - 1):
        peer = o + jnp.where(o >= me_t, 1, 0)
        for source, target, copies in ((me_t, peer, st_copies), (peer, peer, st_waits)):
            copies.append(pltpu.make_async_remote_copy(
                src_ref=small_tile.at[source], dst_ref=small_tile.at[source], send_sem=st_send.at[o],
                recv_sem=st_recv.at[source], device_id={"tile": target}, device_id_type=MESH,
            ))
        st_copies[o].start()
    spread_part(6, 8)

    for copy in rs_copies:
        copy.wait_recv()
    total = jnp.zeros((2 * at_once, win.shape[2]), F32)
    for t in range(tiles):
        for d in range(dps):
            total = total + piece_recv[t, d].astype(F32)
    piece_all[me_t] = (total * factor).astype(BF16)
    tg_copies, tg_waits = [], []
    for o in range(tiles - 1):
        peer = o + jnp.where(o >= me_t, 1, 0)
        for source, target, copies in ((me_t, peer, tg_copies), (peer, peer, tg_waits)):
            copies.append(pltpu.make_async_remote_copy(
                src_ref=piece_all.at[source], dst_ref=piece_all.at[source], send_sem=tg_send.at[o],
                recv_sem=tg_recv.at[source], device_id={"tile": target}, device_id_type=MESH,
            ))
        tg_copies[o].start()

    rim_passes = []
    for o, copy in enumerate(rim_copies):
        slots = pl.ds(o * strip, strip)
        copy.wait_recv()
        rim_passes.append(to_sibling(rims.at[me_c, slots], rims.at[me_c, slots], 5 + o))
    from_mine = mm(sel_t[me_c], rims[me_c], 1, 0)

    for copy in st_waits:
        copy.wait_recv()
    total = small_tile[0].astype(F32)
    for t in range(1, tiles):
        total = total + small_tile[t].astype(F32)
    small_done[me_c] = total * factor
    done_copy = to_sibling(small_done.at[me_c], small_done.at[me_c], 4 + tiles)

    for copy in rim_passes:
        copy.wait_recv()
    incoming = from_mine + mm(sel_t[sib], rims[sib], 1, 0)
    for d in range(H):
        part_of = [incoming[f * strip + d * ts:f * strip + (d + 1) * ts] for f in range(4)]
        base[d * ts:(d + 1) * ts, :] += part_of[0]
        base[(ts - 1 - d) * ts:(ts - d) * ts, :] += part_of[2]
        base[pl.ds(ts - 1 - d, ts, stride=ts), :] += part_of[1]
        base[pl.ds(d, ts, stride=ts), :] += part_of[3]

    def out_row(i):
        out_ref[i] = base[pl.ds(pl.multiple_of(i * ts, 8), ts), :].astype(BF16)
    rows_loop(ts, out_row, 4)

    done_copy.wait_recv()
    small_out[...] = small_done[...]
    for copy in tg_waits:
        copy.wait_recv()
    for w in range(2):
        for t in range(tiles):
            at = w * part_rows + t * at_once
            w_out_all[at:at + at_once, :] = piece_all[t, w * at_once:(w + 1) * at_once].astype(F32)

    for copy in face_copies + rim_copies + rim_passes + rs_copies + sd_copies + tg_copies + st_copies + [
        win_copy, wout_copy, cg_copy, part_copy, small_copy, done_copy
    ]:
        copy.wait_send()


def write_out(out, small, grads, out_hbm, kernel_hbm, gain_hbm, w_in_hbm, w_out_hbm, scale_hbm, sems):
    taps = KS * KS
    rows = w_in_hbm.shape[0]
    pairs = (
        (out, out_hbm),
        (grads.at[:rows], w_in_hbm),
        (grads.at[rows:], w_out_hbm),
        (small.at[:taps], kernel_hbm),
        (small.at[taps:taps + 1], gain_hbm),
        (small.at[taps + 1:taps + 2], scale_hbm),
    )
    copies = [pltpu.make_async_copy(source, target, sems.at[i]) for i, (source, target) in enumerate(pairs)]
    for copy in copies:
        copy.start()
    for copy in copies:
        copy.wait()


def in_hbm(array):
    return pltpu.with_memory_space_constraint(array, pltpu.MemorySpace.HBM)


def on_device(inputs, kernel, norm_gain, w_in, w_out, layer_scale, cotangent, adjacency):
    ts, ch = inputs.shape[2], inputs.shape[4]
    hid = w_in.shape[1]
    tiles, dps = lax.axis_size("tile"), lax.axis_size("dp")
    factor = 1.0 / math.sqrt(dps * tiles * ts * ts)
    strip = H * ts
    wide = ts + 2 * COL
    part_rows = ch // dps
    vmem = pl.BlockSpec(memory_space=pltpu.VMEM)
    hbm = pl.BlockSpec(memory_space=pltpu.MemorySpace.HBM)
    dma = pltpu.SemaphoreType.DMA
    peers_t, peers_d = max(tiles - 1, 1), max(dps - 1, 1)
    pairs = 6 + peers_t
    out, small, grads = pl.pallas_call(
        functools.partial(body, tiles, dps, factor),
        out_shape=(
            jax.ShapeDtypeStruct((ts, ts, ch), BF16),
            jax.ShapeDtypeStruct((2, SMALL_ROWS // 2, ch), F32),
            jax.ShapeDtypeStruct((2 * part_rows, hid), F32),
        ),
        in_specs=[hbm] * 8,
        out_specs=(vmem,) * 3,
        scratch_shapes=[
            pltpu.SMEM((tiles, 2, 8), jnp.int32),
            pltpu.VMEM((KS * KS, ch), F32),
            pltpu.VMEM((1, ch), F32),
            pltpu.VMEM((1, ch), F32),
            pltpu.VMEM((ts, ts, ch), BF16),
            pltpu.VMEM((ts, ts, ch), BF16),
            pltpu.VMEM(((ts + 2 * H + 8) * wide, ch), F32),
            pltpu.VMEM((4 * strip, ch), BF16),
            pltpu.VMEM((peers_t * SLOT_ROWS, 4 * strip), BF16),
            pltpu.VMEM((2, 4 * strip, peers_t * strip), BF16),
            pltpu.VMEM((peers_t * SLOT_ROWS, ch), BF16),
            pltpu.VMEM((tiles, SLOT_ROWS, ch), BF16),
            pltpu.VMEM((2, SIDE_ROWS, ch), F32),
            pltpu.VMEM((2, CORNER_ROWS, ch), F32),
            pltpu.VMEM((2, ch, hid), BF16),
            pltpu.VMEM((2, hid, ch), BF16),
            pltpu.VMEM((ts // 2 * ts + ts, ch), F32),
            pltpu.VMEM((2, ch, hid), F32),
            pltpu.VMEM((2, ch, hid), BF16),
            pltpu.VMEM((2, ch, hid), BF16),
            pltpu.VMEM((ts, ts, ch), BF16),
            pltpu.VMEM(((ts + 2 * KS) * wide, ch), F32),
            pltpu.VMEM((H * (ts + 8) + 8, ch), F32),
            pltpu.VMEM((3, strip, ch), BF16),
            pltpu.VMEM((peers_t * strip, ch), BF16),
            pltpu.VMEM((2, peers_t * strip, ch), BF16),
            pltpu.VMEM((tiles, dps, 2 * part_rows // tiles, hid), BF16),
            pltpu.VMEM((tiles, dps, 2 * part_rows // tiles, hid), BF16),
            pltpu.VMEM((tiles, 2 * part_rows // tiles, hid), BF16),
            pltpu.VMEM((SMALL_ROWS, 8, ch), F32),
            pltpu.VMEM((2, SMALL_ROWS // 2, ch), F32),
            pltpu.VMEM((SMALL_ROWS // 2, ch), F32),
            pltpu.VMEM((dps, SMALL_ROWS // 2, ch), BF16),
            pltpu.VMEM((tiles, SMALL_ROWS // 2, ch), BF16),
            pltpu.VMEM((2, SMALL_ROWS // 2, ch), F32),
            pltpu.VMEM((ts * ts + ts, ch), F32),
            dma((8,)),
            dma((peers_t,)), dma((peers_t,)), dma((pairs,)), dma((pairs,)), dma((peers_t,)), dma((peers_t,)),
            dma((tiles * dps,)), dma((tiles * dps,)), dma((peers_t,)), dma((tiles,)),
            dma((peers_d,)), dma((peers_d,)), dma((peers_t,)), dma((tiles,)),
        ],
        compiler_params=pltpu.CompilerParams(
            collective_id=0, has_side_effects=True, vmem_limit_bytes=48 * 1024 * 1024
        ),
    )(
        in_hbm(jnp.transpose(adjacency, (0, 2, 1))), in_hbm(inputs[0, 0]), in_hbm(cotangent[0, 0]), in_hbm(kernel),
        in_hbm(norm_gain[None]), in_hbm(w_in), in_hbm(w_out), in_hbm(layer_scale[None]),
    )
    results = pl.pallas_call(
        write_out,
        out_shape=(
            jax.ShapeDtypeStruct((ts, ts, ch), BF16),
            jax.ShapeDtypeStruct((KS * KS, ch), F32),
            jax.ShapeDtypeStruct((1, ch), F32),
            jax.ShapeDtypeStruct((part_rows, hid), F32),
            jax.ShapeDtypeStruct((part_rows, hid), F32),
            jax.ShapeDtypeStruct((1, ch), F32),
        ),
        in_specs=[pl.BlockSpec(memory_space=pl.ANY)] * 3,
        out_specs=(hbm,) * 6,
        scratch_shapes=[dma((6,))],
        compiler_params=pltpu.CompilerParams(vmem_limit_bytes=1024 * 1024),
    )(out, small.reshape(SMALL_ROWS, ch), grads)
    return (
        results[0][None, None],
        results[1],
        results[2].reshape(ch),
        results[3],
        results[4].T,
        results[5].reshape(ch),
    )


def solution(mesh):
    placed = (
        P(("group", "dp"), "tile", None, None, None),
        P(),
        P(),
        P(None, "chan"),
        P("chan", None),
        P(),
        P(("group", "dp"), "tile", None, None, None),
        P(),
    )
    return jax.shard_map(
        on_device,
        mesh=mesh,
        in_specs=placed,
        out_specs=(
            P(("group", "dp"), "tile", None, None, None),
            P("group", None),
            P("group"),
            P(("group", "dp"), "chan"),
            P(("group", "chan"), "dp"),
            P("group"),
        ),
        check_vma=False,
    )
```
